32 devices in a mesh: orb: 8 (over z, x), box: 4 (over y, core).
Axes of the slice: x: 2, y: 2, z: 4, core: 2. Of those that a mesh axis runs over, the one named last changes fastest.
Arguments:
- psi: float32 [64, 64, 4096], P('orb', 'box'), may hold values from -6 to 6
- potential: float32 [64, 4096], P('box'), may hold values from -3 to 3
- orbital_slot: int32 [32], replicated, may hold values from 0 to 63, as said below
Outputs:
- residual: float32 [32, 64, 4096], P('orb', 'box')
- direction: float32 [32, 64, 4096], P('orb', 'box')
- multipliers: float32 [32, 32], replicated
The draws below stay inside these ranges and needn't reach their ends.
Inputs may be any that keep to these rules, and one draw needn't show every extreme that they name: The values are distinct slots: orbital j sits in slot orbital_slot[j]. The 8 slots of one index of orb hold up to 8 orbitals, and in every draw all slots of one index are filled.
All inputs are finite; a program needn't handle non-finite values.
Results may differ from the reference program's by a relative error of at most 0.0002.
Values sent between devices are 32-bit elements; how exact they have to be, the bound alone decides.
No kernel may reach another device: no remote copies, remote signals or barrier semaphores. Data moves between devices by JAX's collectives and lax.ppermute only.
A program may use at most 64 MiB of HBM per device.

```python
import math
import jax
import jax.numpy as jnp
import numpy as np
from jax import lax

G = 64
MTAPS = 16
KREACH = 14
SWEEPS = 4
SLOTS = 8
ORBS = 32
SLOTS_ALL = 64


def draw_orbital_slot(key, part):
    base_key = jax.random.fold_in(key, 7)
    key_full, key_order, key_other = jax.random.split(base_key, 3)
    owners = SLOTS_ALL // SLOTS
    full_owner = jax.random.randint(key_full, (), 0, owners, dtype=jnp.int32)
    orbital_order = jax.random.permutation(key_order, ORBS)
    other_slots = jax.random.permutation(key_other, SLOTS_ALL - SLOTS)[:ORBS - SLOTS].astype(jnp.int32)
    other_slots = other_slots + SLOTS * (other_slots >= full_owner * SLOTS).astype(jnp.int32)
    placed = jnp.concatenate([full_owner * SLOTS + jnp.arange(SLOTS, dtype=jnp.int32), other_slots])
    return jnp.zeros((ORBS,), jnp.int32).at[orbital_order].set(placed)


def shard_levels(rng, shape, shards, smallest, high):
    def one(dim, blocks):
        heights = jax.random.uniform(jax.random.fold_in(jax.random.fold_in(rng, 6), dim), (blocks,), jnp.float32, smallest / len(shards), high / len(shards))
        return jnp.repeat(jnp.exp(heights), shape[dim] // blocks).reshape((-1,) + (1,) * (len(shape) - dim - 1))

    loudness = one(*shards[0])
    for cut in shards[1:]:
        loudness = loudness * one(*cut)
    return loudness


def bell_draw(rng, shape, scale, most, shards=(), kind=jnp.bfloat16):
    factor_of = shard_levels(rng, shape, shards, -0.22, 0.18) if shards else 1.0
    entries = jax.random.normal(rng, shape, jnp.float32) * scale * factor_of
    return jnp.minimum(jnp.maximum(entries, -most), most).astype(kind)


def setup_inputs(seed: int = 0) -> dict:
    key_list = jax.random.split(jax.random.key(seed), 4)
    return {
        "psi": bell_draw(key_list[0], (SLOTS_ALL, G, G * G), 1.0, 6.0, ((0, 8), (1, 4)), jnp.float32),
        "potential": jnp.clip(jax.random.uniform(key_list[1], (G, G * G), jnp.float32, -3.0, 3.0) * shard_levels(key_list[1], (G, G * G), ((0, 4),), -0.4, 0.0), -3.0, 3.0),
        "orbital_slot": draw_orbital_slot(jax.random.fold_in(key_list[3], 71), 0),
    }


highest = lax.Precision.HIGHEST
coupling_z = 4.0
coupling_xy = 1.0


def magic_weights(tap_count):
    half_len = tap_count // 2
    offsets = np.arange(1 - half_len, half_len + 1) * 1.0
    weights = np.ones(tap_count)
    for index_a in range(tap_count):
        for index_b in range(tap_count):
            if index_b != index_a:
                weights[index_a] *= (0.25 - offsets[index_b]) / (offsets[index_a] - offsets[index_b])
    return weights


def second_weights(reach_cells):
    factor = math.factorial(reach_cells) ** 2
    weights = np.zeros(2 * reach_cells + 1)
    for distance in range(1, reach_cells + 1):
        entry_value = 2.0 * (-1) ** (distance + 1) * factor / (distance * distance * math.factorial(reach_cells - distance) * math.factorial(reach_cells + distance))
        weights[reach_cells + distance] = entry_value
        weights[reach_cells - distance] = entry_value
    weights[reach_cells] = -weights.sum()
    return -0.5 * weights


def banded(row_count, col_count, row_start, col_start, weights, offset_low):
    row_index = np.arange(row_count)[:, None] + row_start
    col_index = np.arange(col_count)[None, :] + col_start
    position = row_index - col_index - offset_low
    inside = (position >= 0) & (position < len(weights))
    return np.where(inside, weights[np.clip(position, 0, len(weights) - 1)], 0.0)


def apply_orbital(coeffs, potential_cube, forward, kinetic):
    grid_values = jnp.einsum("zyx,zp->pyx", coeffs, forward, precision=highest)
    grid_values = jnp.einsum("zyx,yp->zpx", grid_values, forward, precision=highest)
    grid_values = jnp.einsum("zyx,xp->zyp", grid_values, forward, precision=highest)
    weighted = grid_values * potential_cube
    applied = jnp.einsum("pyx,zp->zyx", weighted, forward, precision=highest)
    applied = jnp.einsum("zpx,yp->zyx", applied, forward, precision=highest)
    applied = jnp.einsum("zyp,xp->zyx", applied, forward, precision=highest)
    applied = applied + jnp.einsum("zyx,zp->pyx", coeffs, kinetic, precision=highest)
    applied = applied + jnp.einsum("zyx,yp->zpx", coeffs, kinetic, precision=highest)
    applied = applied + jnp.einsum("zyx,xp->zyp", coeffs, kinetic, precision=highest)
    return applied


def relax_orbital(residual_cube, denominator):
    iterate = residual_cube / denominator
    for sweep_index in range(SWEEPS):
        padded = jnp.pad(iterate, 1)
        along_z = padded[2:, 1:-1, 1:-1] + padded[:-2, 1:-1, 1:-1]
        along_y = padded[1:-1, 2:, 1:-1] + padded[1:-1, :-2, 1:-1]
        along_x = padded[1:-1, 1:-1, 2:] + padded[1:-1, 1:-1, :-2]
        iterate = (residual_cube + coupling_xy * (along_y + along_x) + coupling_z * along_z) / denominator
    return iterate


def reference(psi, potential, orbital_slot):
    magic = magic_weights(MTAPS)
    kinetic_row = second_weights(KREACH)
    forward = jnp.asarray(banded(G, G, 0, 0, magic, 1 - MTAPS // 2), dtype=jnp.float32)
    kinetic = jnp.asarray(banded(G, G, 0, 0, kinetic_row, -KREACH), dtype=jnp.float32)
    potential_cube = potential.reshape(G, G, G)
    chosen = jnp.take(psi, orbital_slot, axis=0)
    applied = lax.map(lambda coeffs: apply_orbital(coeffs.reshape(G, G, G), potential_cube, forward, kinetic).reshape(G, G * G), chosen)
    chosen_flat = chosen.reshape(ORBS, G * G * G)
    applied_flat = applied.reshape(ORBS, G * G * G)
    multipliers = jnp.einsum("ia,ja->ij", chosen_flat, applied_flat, precision=highest) / float(G ** 3)
    residual = applied_flat - jnp.einsum("ji,ja->ia", multipliers, chosen_flat, precision=highest)
    residual = residual.reshape(ORBS, G, G * G)
    denominator = 2.0 * coupling_z + 4.0 * coupling_xy + 1.0 + jnp.abs(jnp.diagonal(multipliers))
    direction = lax.map(lambda pair: relax_orbital(pair[0].reshape(G, G, G), pair[1]).reshape(G, G * G), (residual, denominator))
    return (residual, direction, multipliers)
```

```python
import math

import jax
import jax.numpy as jnp
import numpy as np
from jax import lax
from jax.sharding import PartitionSpec as P

MTAPS = 16
KREACH = 14
SWEEPS = 4


highest = lax.Precision.HIGHEST
coupling_z = 4.0
coupling_xy = 1.0


def extended_2(block, sides, width):
    for axis, dim in sides:
        count = lax.axis_size(axis)
        forward = [(i, i + 1) for i in range(count - 1)]
        backward = [(target, source) for source, target in forward]
        low = lax.ppermute(
            lax.slice_in_dim(block, block.shape[dim] - width, None, axis=dim), axis, forward
        )
        high = lax.ppermute(lax.slice_in_dim(block, 0, width, axis=dim), axis, backward)
        block = jnp.concatenate([low, block, high], axis=dim)
    return block


def magic_weights(tap_count):
    half_len = tap_count // 2
    offsets = np.arange(1 - half_len, half_len + 1) * 1.0
    weights = np.ones(tap_count)
    for index_a in range(tap_count):
        for index_b in range(tap_count):
            if index_b != index_a:
                weights[index_a] *= (0.25 - offsets[index_b]) / (
                    offsets[index_a] - offsets[index_b]
                )
    return weights


def second_weights(reach_cells):
    factor = math.factorial(reach_cells) ** 2
    weights = np.zeros(2 * reach_cells + 1)
    for distance in range(1, reach_cells + 1):
        entry_value = (
            2.0
            * (-1) ** (distance + 1)
            * factor
            / (
                distance
                * distance
                * math.factorial(reach_cells - distance)
                * math.factorial(reach_cells + distance)
            )
        )
        weights[reach_cells + distance] = entry_value
        weights[reach_cells - distance] = entry_value
    weights[reach_cells] = -weights.sum()
    return -0.5 * weights


def banded(row_count, col_count, row_start, col_start, weights, offset_low):
    row_index = np.arange(row_count)[:, None] + row_start
    col_index = np.arange(col_count)[None, :] + col_start
    position = row_index - col_index - offset_low
    inside = (position >= 0) & (position < len(weights))
    return np.where(inside, weights[np.clip(position, 0, len(weights) - 1)], 0.0)


def along_cols(values, matrix, box_width):
    repeats = max(1, 128 // box_width)
    blocked = jnp.asarray(np.kron(np.eye(repeats), matrix), dtype=jnp.float32)
    shaped = values.shape
    result = jnp.dot(values.reshape(-1, box_width * repeats), blocked, precision=highest)
    return result.reshape(shaped)


def along_rows(values, matrix, box_width):
    shaped = values.shape
    split_rows = values.reshape(shaped[:-1] + (box_width, box_width))
    result = jnp.einsum(
        "nzyx,yq->nzqx", split_rows, jnp.asarray(matrix, dtype=jnp.float32), precision=highest
    )
    return result.reshape(shaped)


def apply_hamiltonian(coeffs, potential, box_width):
    count, slab_depth, plane_size = coeffs.shape
    margin = MTAPS
    half_len = MTAPS // 2
    stacked = jnp.concatenate([coeffs, potential[None]], 0)
    extended = extended_2(stacked, (("box", 1),), margin)
    coeff_ext = extended[:count]
    potential_ext = extended[count]
    magic = magic_weights(MTAPS)
    kinetic_row = second_weights(KREACH)
    into_grid = jnp.asarray(
        banded(
            slab_depth + 2 * margin,
            slab_depth + 2 * half_len,
            -margin,
            -half_len,
            magic,
            1 - half_len,
        ),
        dtype=jnp.float32,
    )
    from_grid = jnp.asarray(
        banded(slab_depth, slab_depth + 2 * half_len, 0, -half_len, magic, 1 - half_len).T,
        dtype=jnp.float32,
    )
    kinetic_z = jnp.asarray(
        banded(slab_depth + 2 * margin, slab_depth, -margin, 0, kinetic_row, -KREACH),
        dtype=jnp.float32,
    )
    forward = banded(box_width, box_width, 0, 0, magic, 1 - half_len)
    kinetic_xy = banded(box_width, box_width, 0, 0, kinetic_row, -KREACH)
    grid_values = jnp.einsum("nea,ep->npa", coeff_ext, into_grid, precision=highest)
    grid_values = along_cols(along_rows(grid_values, forward, box_width), forward, box_width)
    potential_slab = potential_ext[margin - half_len : margin + slab_depth + half_len]
    weighted = grid_values * potential_slab[None]
    weighted = along_cols(
        along_rows(weighted, forward.T.copy(), box_width), forward.T.copy(), box_width
    )
    applied = jnp.einsum("npa,pz->nza", weighted, from_grid, precision=highest)
    local_part = coeff_ext[:, margin : margin + slab_depth]
    applied = applied + along_rows(local_part, kinetic_xy, box_width)
    applied = applied + along_cols(local_part, kinetic_xy, box_width)
    applied = applied + jnp.einsum("nea,ez->nza", coeff_ext, kinetic_z, precision=highest)
    return applied


def relax(iterate, residual, denominator, box_width):
    count, slab_depth, plane_size = iterate.shape
    extended = extended_2(iterate, (("box", 1),), 1)
    along_z = extended[:, :-2] + extended[:, 2:]
    column = lax.broadcasted_iota(jnp.int32, (1, 1, plane_size), 2) % box_width
    zero_col = jnp.zeros((count, slab_depth, 1), jnp.float32)
    zero_row = jnp.zeros((count, slab_depth, box_width), jnp.float32)
    left_side = jnp.concatenate([zero_col, iterate[..., :-1]], 2) * (column != 0).astype(
        jnp.float32
    )
    right_side = jnp.concatenate([iterate[..., 1:], zero_col], 2) * (
        column != box_width - 1
    ).astype(jnp.float32)
    upper_row = jnp.concatenate([zero_row, iterate[..., :-box_width]], 2)
    lower_row = jnp.concatenate([iterate[..., box_width:], zero_row], 2)
    beside = left_side + right_side + upper_row + lower_row
    return (residual + coupling_xy * beside + coupling_z * along_z) / denominator


def whole_sum(value, axes):
    count = lax.axis_size(axes)
    rows, cols = value.shape
    fold = max(1, 128 // cols)
    if count * rows * cols > 1 << 20 or rows % fold:
        return lax.psum(value, axes)
    packed = value.reshape(rows // fold, fold * cols)
    spread = jnp.broadcast_to(packed[None], (count,) + packed.shape)
    received = lax.all_to_all(spread, axes, split_axis=0, concat_axis=0, tiled=True)
    return received.sum(0).reshape(rows, cols)


def local(psi, potential, orbital_slot):
    slot_count, slab_depth, plane_size = psi.shape
    box_width = math.isqrt(plane_size)
    flattened = psi.reshape(slot_count, slab_depth * plane_size)
    pieces = lax.all_to_all(flattened, "orb", split_axis=1, concat_axis=0, tiled=True)
    coeff_rows = jnp.take(pieces, orbital_slot, axis=0)
    owned_rows = lax.all_to_all(coeff_rows, "orb", split_axis=0, concat_axis=1, tiled=True)
    own_count = owned_rows.shape[0]
    applied = apply_hamiltonian(
        owned_rows.reshape(own_count, slab_depth, plane_size), potential, box_width
    )
    applied_rows = lax.all_to_all(
        applied.reshape(own_count, slab_depth * plane_size),
        "orb",
        split_axis=1,
        concat_axis=0,
        tiled=True,
    )
    partial_value = jnp.einsum("ia,ja->ij", coeff_rows, applied_rows, precision=highest) / float(
        box_width**3
    )
    multipliers = whole_sum(partial_value, ("orb", "box"))
    corrected = applied_rows - jnp.einsum("ji,ja->ia", multipliers, coeff_rows, precision=highest)
    returned = lax.all_to_all(corrected, "orb", split_axis=0, concat_axis=1, tiled=True)
    own_count = returned.shape[0]
    residual = returned.reshape(own_count, slab_depth, plane_size)
    first_row = lax.axis_index("orb") * own_count
    own_diagonal = lax.dynamic_slice_in_dim(jnp.diagonal(multipliers), first_row, own_count)
    denominator = (2.0 * coupling_z + 4.0 * coupling_xy + 1.0 + jnp.abs(own_diagonal))[
        :, None, None
    ]
    direction = residual / denominator
    for sweep_index in range(SWEEPS):
        direction = relax(direction, residual, denominator, box_width)
    return (residual, direction, multipliers)


def solution(mesh):
    in_specs = (P("orb", "box", None), P("box", None), P())
    out_specs = (P("orb", "box", None), P("orb", "box", None), P())
    return jax.shard_map(local, mesh=mesh, in_specs=in_specs, out_specs=out_specs, check_vma=False)
```

```python
import functools
import math

import jax
import jax.numpy as jnp
import numpy as np
from jax import lax
from jax.experimental import pallas as pl
from jax.experimental.pallas import tpu as pltpu
from jax.sharding import PartitionSpec as P

MTAPS = 16
KREACH = 14
SWEEPS = 4
LANES = 128

highest = lax.Precision.HIGHEST
coupling_z = 4.0
coupling_xy = 1.0


def magic_weights(tap_count):
    half_len = tap_count // 2
    offsets = np.arange(1 - half_len, half_len + 1) * 1.0
    weights = np.ones(tap_count)
    for index_a in range(tap_count):
        for index_b in range(tap_count):
            if index_b != index_a:
                weights[index_a] *= (0.25 - offsets[index_b]) / (
                    offsets[index_a] - offsets[index_b]
                )
    return weights


def second_weights(reach_cells):
    factor = math.factorial(reach_cells) ** 2
    weights = np.zeros(2 * reach_cells + 1)
    for distance in range(1, reach_cells + 1):
        entry_value = (
            2.0
            * (-1) ** (distance + 1)
            * factor
            / (
                distance
                * distance
                * math.factorial(reach_cells - distance)
                * math.factorial(reach_cells + distance)
            )
        )
        weights[reach_cells + distance] = entry_value
        weights[reach_cells - distance] = entry_value
    weights[reach_cells] = -weights.sum()
    return -0.5 * weights


def banded(row_count, col_count, row_start, col_start, weights, offset_low):
    row_index = np.arange(row_count)[:, None] + row_start
    col_index = np.arange(col_count)[None, :] + col_start
    position = row_index - col_index - offset_low
    inside = (position >= 0) & (position < len(weights))
    return np.where(inside, weights[np.clip(position, 0, len(weights) - 1)], 0.0)


def f32(value):
    return float(np.float32(value))


MAGIC = {k: f32(w) for k, w in zip(range(1 - MTAPS // 2, MTAPS // 2 + 1), magic_weights(MTAPS))}
MAGIC_T = {-k: w for k, w in MAGIC.items()}
KINETIC = {
    d: f32(w) for d, w in zip(range(-KREACH, KREACH + 1), second_weights(KREACH))
}
LOW = MTAPS // 2
HIGH = MTAPS // 2 - 1


def two_part(matrix):
    width = matrix.shape[0]
    block = np.kron(np.eye(LANES // width), matrix).astype(np.float32)
    high = block.astype(jnp.bfloat16)
    low = (block - high.astype(np.float32)).astype(jnp.bfloat16)
    return np.block([[high, low], [high, np.zeros_like(low)]])


def split(value):
    high = value.astype(jnp.bfloat16)
    low = (value - high.astype(jnp.float32)).astype(jnp.bfloat16)
    return high, low


def lane_product(parts, matrix):
    both = jnp.dot(parts, matrix, preferred_element_type=jnp.float32)
    return both[:, :LANES] + both[:, LANES:]


def params(**kw):
    return pltpu.CompilerParams(vmem_limit_bytes=56 << 20, **kw)


def cost(flops, bytes_accessed):
    return pl.CostEstimate(flops=flops, bytes_accessed=bytes_accessed, transcendentals=0)


class Shape:
    def __init__(self, slots, depth, plane, owners):
        self.slots, self.depth, self.plane, self.owners = slots, depth, plane, owners
        self.side = math.isqrt(plane)
        self.chunks = plane // LANES
        self.across = min(owners, self.chunks)
        self.layered = owners // self.across
        self.layers = depth // self.layered
        self.width = plane // self.across
        self.inner = self.width // LANES

    def at(self, layer, block, inner):
        piece = (layer // self.layers) * self.across + block
        lanes = slice(inner * LANES, (inner + 1) * LANES)
        return piece, layer % self.layers, slice(None), lanes


def reorder_kernel(sh, psi_ref, out_ref):
    for group in range(sh.layered):
        rows = psi_ref[:, group * sh.layers : (group + 1) * sh.layers, :]
        rows = jnp.transpose(rows, (1, 0, 2))
        for block in range(sh.across):
            out_ref[group * sh.across + block] = rows[
                :, :, block * sh.width : (block + 1) * sh.width
            ]


def reorder(sh, psi):
    return pl.pallas_call(
        functools.partial(reorder_kernel, sh),
        out_shape=jax.ShapeDtypeStruct((sh.owners, sh.layers, sh.slots, sh.width), jnp.float32),
        compiler_params=params(),
        name="reorder",
    )(psi)


def odd_pairs(even, lane):
    turned = [pltpu.roll(v, LANES // 2, 1) for v in even]
    zero = jnp.zeros_like(even[0])
    low = [zero] + turned
    high = turned + [zero]
    return [jnp.where(lane, a, b) for a, b in zip(low, high)]


def row_filter(even, odd, weights):
    count = len(even)
    out = []
    for b in range(count):
        total = None
        for d, w in weights.items():
            e = b + d // 2
            if d % 2 == 0:
                if not 0 <= e < count:
                    continue
                term = even[e]
            else:
                if not 0 <= e + 1 <= count:
                    continue
                term = odd[e + 1]
            total = term * w if total is None else total + term * w
        out.append(total)
    return out


def row_filter_even(even, odd, weights, reach):
    count = len(even)
    out = []
    for b in range(count):
        total = even[b] * weights[0]
        for d in range(1, reach + 1):
            if d % 2 == 0:
                places = [e for e in (b + d // 2, b - d // 2) if 0 <= e < count]
                terms = [even[e] for e in places]
            else:
                places = [e for e in (b + d // 2 + 1, b - d // 2) if 0 <= e <= count]
                terms = [odd[e] for e in places]
            if not terms:
                continue
            term = terms[0] if len(terms) == 1 else terms[0] + terms[1]
            total = total + term * weights[d]
        out.append(total)
    return out


def half_mask(slots):
    return lax.broadcasted_iota(jnp.int32, (slots, LANES), 1) < LANES // 2


def lane_pass(sh, source, matrices, targets, layers):
    def body(block, carry):
        parts = []
        for inner in range(sh.inner):
            rows = jnp.concatenate(
                [source[sh.at(layer, block, inner)] for layer in range(layers)], 0
            )
            high, low = split(rows)
            parts.append(jnp.concatenate([high, low], 1))
        parts = jnp.concatenate(parts, 0)
        for matrix, target in zip(matrices, targets):
            result = lane_product(parts, matrix[...])
            result = result.reshape(sh.inner, layers, sh.slots, LANES)
            for inner in range(sh.inner):
                for layer in range(layers):
                    target[layer, block * sh.inner + inner] = result[inner, layer]
        return carry

    lax.fori_loop(0, sh.across, body, 0)


def own_kernel(sh, c_ref, fwd_ref, kin_ref, w_out, kin_out, x_ref):
    lane_pass(sh, c_ref, [fwd_ref, kin_ref], [x_ref, kin_out], sh.depth)
    lane = half_mask(sh.slots)

    for group in range(sh.layered):

        def body(i, carry):
            layer = group * sh.layers + i
            even = [x_ref[layer, b] for b in range(sh.chunks)]
            for b, v in enumerate(row_filter(even, odd_pairs(even, lane), MAGIC)):
                w_out[layer, b] = v
            even = [
                c_ref[
                    group * sh.across + b // sh.inner,
                    i,
                    :,
                    (b % sh.inner) * LANES : (b % sh.inner + 1) * LANES,
                ]
                for b in range(sh.chunks)
            ]
            sums = row_filter_even(even, odd_pairs(even, lane), KINETIC, KREACH)
            for b, v in enumerate(sums):
                kin_out[layer, b] += v
            return carry

        lax.fori_loop(0, sh.layers, body, 0)


def own_part(sh, c, fwd, kin):
    full = jax.ShapeDtypeStruct((sh.depth, sh.chunks, sh.slots, LANES), jnp.float32)
    return pl.pallas_call(
        functools.partial(own_kernel, sh),
        out_shape=(full, full),
        scratch_shapes=[pltpu.VMEM(full.shape, jnp.float32)],
        compiler_params=params(),
        cost_estimate=cost(10**10, 10**7),
        name="own_part",
    )(c, fwd, kin)


def halo_kernel(
    sh, lo_ref, c_ref, hi_ref, w_ref, kin_ref, vlo_ref, v_ref, vhi_ref, fwd_ref, bwd_ref,
    out_ref, x_ref, wlo_ref, whi_ref,
):
    lane = half_mask(sh.slots)
    depth = sh.depth
    for side_ref, target in ((lo_ref, wlo_ref), (hi_ref, whi_ref)):
        lane_pass(sh, side_ref, [fwd_ref], [x_ref], depth)

        def filter_rows(layer, carry):
            even = [x_ref[layer, b] for b in range(sh.chunks)]
            for b, v in enumerate(row_filter(even, odd_pairs(even, lane), MAGIC)):
                target[layer, b] = v
            return carry

        lax.fori_loop(0, depth, filter_rows, 0)

    def along_z(block, carry):
        for inner in range(sh.inner):
            chunk = block * sh.inner + inner
            lanes = pl.ds(pl.multiple_of(chunk * LANES, LANES), LANES)

            def coeff(z):
                ref = lo_ref if z < 0 else (c_ref if z < depth else hi_ref)
                return ref[sh.at(z % depth, block, inner)]

            def mixed(z):
                ref = wlo_ref if z < 0 else (w_ref if z < depth else whi_ref)
                return ref[z % depth, chunk]

            def level(z):
                ref = vlo_ref if z < 0 else (v_ref if z < depth else vhi_ref)
                return jnp.broadcast_to(ref[pl.ds(z % depth, 1), lanes], (sh.slots, LANES))

            values = {z: mixed(z) for z in range(-LOW - HIGH, depth + LOW + HIGH)}
            grid = {}
            for p in range(-LOW, depth + HIGH):
                total = None
                for k, w in MAGIC.items():
                    term = values[p + k] * w
                    total = term if total is None else total + term
                grid[p] = total * level(p)
            for q in range(depth):
                total = None
                for k, w in MAGIC.items():
                    term = grid[q - k] * w
                    total = term if total is None else total + term
                x_ref[q, chunk] = total
            cs = {z: coeff(z) for z in range(-KREACH, depth + KREACH)}
            for q in range(depth):
                total = kin_ref[q, chunk] + cs[q] * KINETIC[0]
                for d in range(1, KREACH + 1):
                    total = total + (cs[q + d] + cs[q - d]) * KINETIC[d]
                whi_ref[q, chunk] = total
        return carry

    lax.fori_loop(0, sh.across, along_z, 0)

    def filter_back(layer, carry):
        even = [x_ref[layer, b] for b in range(sh.chunks)]
        for b, v in enumerate(row_filter(even, odd_pairs(even, lane), MAGIC_T)):
            wlo_ref[layer, b] = v
        return carry

    lax.fori_loop(0, depth, filter_back, 0)

    def finish(block, carry):
        parts = []
        for inner in range(sh.inner):
            chunk = block * sh.inner + inner
            rows = jnp.concatenate([wlo_ref[layer, chunk] for layer in range(depth)], 0)
            high, low = split(rows)
            parts.append(jnp.concatenate([high, low], 1))
        result = lane_product(jnp.concatenate(parts, 0), bwd_ref[...])
        result = result.reshape(sh.inner, depth, sh.slots, LANES)
        for inner in range(sh.inner):
            chunk = block * sh.inner + inner
            for layer in range(depth):
                out_ref[sh.at(layer, block, inner)] = result[inner, layer] + whi_ref[layer, chunk]
        return carry

    lax.fori_loop(0, sh.across, finish, 0)


def halo_part(sh, lo, c, hi, w, kin, v_lo, v, v_hi, fwd, bwd):
    full = pltpu.VMEM((sh.depth, sh.chunks, sh.slots, LANES), jnp.float32)
    return pl.pallas_call(
        functools.partial(halo_kernel, sh),
        out_shape=jax.ShapeDtypeStruct(c.shape, jnp.float32),
        scratch_shapes=[full] * 3,
        compiler_params=params(),
        cost_estimate=cost(3 * 10**10, 10**7),
        name="halo_part",
    )(lo, c, hi, w, kin, v_lo, v, v_hi, fwd, bwd)


def selection(slot_ref, count, slots_all):
    column = lax.broadcasted_iota(jnp.int32, (count, slots_all), 1)
    return (column == slot_ref[...]).astype(jnp.float32)


def packed_rows(matrix, fold):
    rows = matrix.shape[0] // fold
    return jnp.concatenate([matrix[i * rows : (i + 1) * rows] for i in range(fold)], 1)


def unpacked_rows(matrix, fold):
    cols = matrix.shape[1] // fold
    return jnp.concatenate([matrix[:, i * cols : (i + 1) * cols] for i in range(fold)], 0)


def gram_kernel(sh, fold, c_ref, a_ref, slot_ref, out_ref):
    total_slots = sh.owners * sh.slots
    count = slot_ref.shape[0]

    def parts(ref, layer):
        rows = ref[:, layer].reshape(total_slots, sh.width)
        return jnp.concatenate(split(rows), 0)

    def body(layer, total):
        return total + lax.dot_general(
            parts(c_ref, layer),
            parts(a_ref, layer),
            (((1,), (1,)), ((), ())),
            preferred_element_type=jnp.float32,
        )

    both = jnp.zeros((2 * total_slots, 2 * total_slots), jnp.float32)
    both = lax.fori_loop(0, sh.layers, body, both, unroll=sh.layers <= 16 and total_slots <= 64)
    wide = both[:total_slots] + both[total_slots:]
    full = wide[:, :total_slots] + wide[:, total_slots:]
    chosen = selection(slot_ref, count, total_slots)
    rows = jnp.dot(chosen, full, precision=highest, preferred_element_type=jnp.float32)
    picked = lax.dot_general(
        rows, chosen, (((1,), (1,)), ((), ())), precision=highest,
        preferred_element_type=jnp.float32,
    ) * (1.0 / sh.side**3)
    picked = packed_rows(picked, fold)
    if len(out_ref.shape) == 2:
        out_ref[...] = picked
    else:
        out_ref[...] = jnp.broadcast_to(picked[None], out_ref.shape)


def gram(sh, c, a, slot, fold, copies):
    count = slot.shape[0]
    shape = (count // fold, count * fold)
    if copies:
        shape = (copies,) + shape
    return pl.pallas_call(
        functools.partial(gram_kernel, sh, fold),
        out_shape=jax.ShapeDtypeStruct(shape, jnp.float32),
        compiler_params=params(),
        cost_estimate=cost(10**9, 10**7),
        name="gram",
    )(c, a, slot)


def correct_kernel(sh, fold, own, c_ref, a_ref, slot_ref, part_ref, out_ref, mult_ref, inv_ref):
    total_slots = sh.owners * sh.slots
    count = slot_ref.shape[0]
    packed = part_ref[...]
    if packed.ndim == 3:
        packed = packed.sum(0)
    multipliers = unpacked_rows(packed, fold)
    mult_ref[...] = multipliers
    row = lax.broadcasted_iota(jnp.int32, (count, count), 0)
    col = lax.broadcasted_iota(jnp.int32, (count, count), 1)
    diagonal = jnp.sum(jnp.where(row == col, multipliers, 0.0), axis=1, keepdims=True)
    denominator = 2.0 * coupling_z + 4.0 * coupling_xy + 1.0 + jnp.abs(diagonal)
    inv_ref[...] = jnp.broadcast_to(1.0 / denominator, (count, LANES))
    chosen = selection(slot_ref, count, total_slots)
    mixing = lax.dot_general(
        multipliers, chosen, (((0,), (0,)), ((), ())), precision=highest,
        preferred_element_type=jnp.float32,
    )
    weights = jnp.concatenate([chosen, -mixing], 1)
    high, low = split(weights)
    weights = jnp.concatenate(
        [
            jnp.concatenate([high, high], 1),
            jnp.concatenate([low, jnp.zeros_like(low)], 1),
        ],
        0,
    )

    def body(layer):
        a_rows = split(a_ref[:, layer].reshape(total_slots, sh.width))
        c_rows = split(c_ref[:, layer].reshape(total_slots, sh.width))
        data = jnp.concatenate([a_rows[0], c_rows[0], a_rows[1], c_rows[1]], 0)
        both = jnp.dot(weights, data, preferred_element_type=jnp.float32)
        result = both[:count] + both[count:]
        for owner in range(sh.owners):
            out_ref[owner, layer * own : (layer + 1) * own] = result[
                owner * own : (owner + 1) * own
            ]

    for layer in range(sh.layers):
        body(layer)


def correct(sh, c, a, slot, part, fold):
    count = slot.shape[0]
    own = count // sh.owners
    return pl.pallas_call(
        functools.partial(correct_kernel, sh, fold, own),
        out_shape=(
            jax.ShapeDtypeStruct((sh.owners, sh.layers * own, sh.width), jnp.float32),
            jax.ShapeDtypeStruct((count, count), jnp.float32),
            jax.ShapeDtypeStruct((count, LANES), jnp.float32),
        ),
        compiler_params=params(),
        cost_estimate=cost(10**9, 10**7),
        name="correct",
    )(c, a, slot, part)


def relax_kernel(
    sh, own, ends_ref, r_ref, lo_ref, hi_ref, inv_ref, res_out, dir_out, res_ref, one_ref, two_ref
):
    rows = sh.depth * own
    edge = SWEEPS * own
    first = pl.multiple_of(ends_ref[0] * own, own)
    inverse = inv_ref[pl.ds(first, own), :]
    inverse = jnp.concatenate([inverse] * (8 // own), 0)
    keep_lo = inverse * ends_ref[1].astype(jnp.float32)
    keep_hi = inverse * ends_ref[2].astype(jnp.float32)
    tiles = (rows + 2 * edge) // 8
    edge_tiles = edge // 8

    def scale(tile):
        if tile < edge_tiles:
            return keep_lo
        return keep_hi if tile >= tiles - edge_tiles else inverse

    def gather(block, carry):
        for inner in range(sh.inner):
            chunk = block * sh.inner + inner
            lanes = slice(inner * LANES, (inner + 1) * LANES)
            pieces = [lo_ref[block, :, lanes]]
            pieces += [r_ref[g * sh.across + block, :, lanes] for g in range(sh.layered)]
            pieces += [hi_ref[block, :, lanes]]
            column = jnp.concatenate(pieces, 0)
            for tile in range(tiles):
                value = column[tile * 8 : (tile + 1) * 8]
                res_ref[chunk, tile * 8 : (tile + 1) * 8] = value
                one_ref[chunk, tile * 8 : (tile + 1) * 8] = value * scale(tile)
            out_lanes = pl.ds(pl.multiple_of(chunk * LANES, LANES), LANES)
            for orbital in range(own):
                res_out[orbital, :, out_lanes] = res_ref[
                    chunk, pl.ds(edge + orbital, sh.depth, stride=own), :
                ]
        return carry

    lax.fori_loop(0, sh.across, gather, 0)

    sub = lax.broadcasted_iota(jnp.int32, (8, LANES), 0)
    lane = lax.broadcasted_iota(jnp.int32, (8, LANES), 1)
    upper = sub >= own
    right_half = lane >= LANES // 2
    not_last = (lane % sh.side) != sh.side - 1
    not_first = (lane % sh.side) != 0
    half = 8 // own
    assert half == 2

    def sweep(source, target, tile_list):
        def body(chunk, carry):
            before = jnp.maximum(chunk - 1, 0)
            after = jnp.minimum(chunk + 1, sh.chunks - 1)
            has_before = (chunk > 0).astype(jnp.float32)
            has_after = (chunk < sh.chunks - 1).astype(jnp.float32)
            for tile in tile_list:
                here = pl.ds(tile * 8, 8)
                value = source[chunk, here]
                zero = jnp.zeros_like(value)
                below = source[chunk, pl.ds(tile * 8 - 8, 8)] if tile > 0 else zero
                above = source[chunk, pl.ds(tile * 8 + 8, 8)] if tile < tiles - 1 else zero
                along_z = pltpu.roll(value + jnp.where(upper, below, above), own, 0)
                along_y = pltpu.roll(
                    value
                    + jnp.where(
                        right_half,
                        source[before, here] * has_before,
                        source[after, here] * has_after,
                    ),
                    LANES // 2,
                    1,
                )
                along_x = pltpu.roll(jnp.where(not_last, value, 0.0), 1, 1) + pltpu.roll(
                    jnp.where(not_first, value, 0.0), LANES - 1, 1
                )
                total = (
                    res_ref[chunk, here]
                    + coupling_xy * (along_y + along_x)
                    + coupling_z * along_z
                )
                target[chunk, here] = total * scale(tile)
            return carry

        lax.fori_loop(0, sh.chunks, body, 0)

    source, target = one_ref, two_ref
    for done in range(1, SWEEPS + 1):
        first_tile = done * own // 8
        sweep(source, target, range(first_tile, tiles - first_tile))
        source, target = target, source

    def spread(chunk, carry):
        out_lanes = pl.ds(pl.multiple_of(chunk * LANES, LANES), LANES)
        for orbital in range(own):
            dir_out[orbital, :, out_lanes] = source[
                chunk, pl.ds(edge + orbital, sh.depth, stride=own), :
            ]
        return carry

    lax.fori_loop(0, sh.chunks, spread, 0)


def relax(sh, own, ends, r, lo, hi, inverse):
    rows = (sh.depth + 2 * SWEEPS) * own
    scratch = pltpu.VMEM((sh.chunks, rows, LANES), jnp.float32)
    out = jax.ShapeDtypeStruct((own, sh.depth, sh.plane), jnp.float32)
    vmem = pl.BlockSpec(memory_space=pltpu.VMEM)
    return pl.pallas_call(
        functools.partial(relax_kernel, sh, own),
        out_shape=(out, out),
        in_specs=[pl.BlockSpec(memory_space=pltpu.SMEM)] + [vmem] * 4,
        scratch_shapes=[scratch] * 3,
        compiler_params=params(),
        cost_estimate=cost(10**9, 10**7),
        name="relax",
    )(ends, r, lo, hi, inverse)


def exchange(value, axis):
    count = lax.axis_size(axis)
    forward = [(i, i + 1) for i in range(count - 1)]
    backward = [(target, source) for source, target in forward]
    return lax.ppermute(value, axis, forward), lax.ppermute(value, axis, backward)


def to_all(value, axes):
    return lax.all_to_all(value, axes, split_axis=0, concat_axis=0, tiled=True)


def local(psi, potential, orbital_slot):
    slots, depth, plane = psi.shape
    owners = lax.axis_size("orb")
    boxes = lax.axis_size("box")
    sh = Shape(slots, depth, plane, owners)
    count = orbital_slot.shape[0]
    own = count // owners
    magic = banded(sh.side, sh.side, 0, 0, magic_weights(MTAPS), 1 - MTAPS // 2)
    kinetic = banded(sh.side, sh.side, 0, 0, second_weights(KREACH), -KREACH)
    fwd, bwd, kin = (jnp.asarray(two_part(m)) for m in (magic, magic.T, kinetic))

    c = reorder(sh, psi)
    pieces = to_all(c, "orb")
    lo, hi = exchange(c, "box")
    v_lo, v_hi = exchange(potential, "box")
    w, kin_own = own_part(sh, c, fwd, kin)
    applied = halo_part(sh, lo, c, hi, w, kin_own, v_lo, potential, v_hi, fwd, bwd)
    applied_pieces = to_all(applied, "orb")

    slot = orbital_slot.reshape(count, 1)
    fold = max(1, LANES // count)
    devices = owners * boxes
    copies = devices if devices * count * count <= 1 << 20 else 0
    part = gram(sh, pieces, applied_pieces, slot, fold, copies)
    part = to_all(part, ("orb", "box")) if copies else lax.psum(part, ("orb", "box"))
    corrected, multipliers, inverse = correct(sh, pieces, applied_pieces, slot, part, fold)
    returned = to_all(corrected, "orb")
    edge = SWEEPS * own
    box = lax.axis_index("box")
    from_low = lax.ppermute(
        returned[-sh.across :, -edge:], "box", [(i, i + 1) for i in range(boxes - 1)]
    )
    from_high = lax.ppermute(
        returned[: sh.across, :edge], "box", [(i + 1, i) for i in range(boxes - 1)]
    )
    ends = jnp.stack(
        [lax.axis_index("orb"), (box > 0).astype(jnp.int32), (box < boxes - 1).astype(jnp.int32)]
    ).astype(jnp.int32)
    residual, direction = relax(sh, own, ends, returned, from_low, from_high, inverse)
    return (residual, direction, multipliers)


def solution(mesh):
    in_specs = (P("orb", "box", None), P("box", None), P())
    out_specs = (P("orb", "box", None), P("orb", "box", None), P())
    return jax.shard_map(local, mesh=mesh, in_specs=in_specs, out_specs=out_specs, check_vma=False)
```

```python
import functools
import math

import jax
import jax.numpy as jnp
import numpy as np
from jax import lax
from jax.experimental import pallas as pl
from jax.experimental.pallas import tpu as pltpu
from jax.sharding import PartitionSpec as P

MTAPS = 16
KREACH = 14
SWEEPS = 4
LANES = 128

highest = lax.Precision.HIGHEST
coupling_z = 4.0
coupling_xy = 1.0


def magic_weights(tap_count):
    half_len = tap_count // 2
    offsets = np.arange(1 - half_len, half_len + 1) * 1.0
    weights = np.ones(tap_count)
    for index_a in range(tap_count):
        for index_b in range(tap_count):
            if index_b != index_a:
                weights[index_a] *= (0.25 - offsets[index_b]) / (
                    offsets[index_a] - offsets[index_b]
                )
    return weights


def second_weights(reach_cells):
    factor = math.factorial(reach_cells) ** 2
    weights = np.zeros(2 * reach_cells + 1)
    for distance in range(1, reach_cells + 1):
        entry_value = (
            2.0
            * (-1) ** (distance + 1)
            * factor
            / (
                distance
                * distance
                * math.factorial(reach_cells - distance)
                * math.factorial(reach_cells + distance)
            )
        )
        weights[reach_cells + distance] = entry_value
        weights[reach_cells - distance] = entry_value
    weights[reach_cells] = -weights.sum()
    return -0.5 * weights


def banded(row_count, col_count, row_start, col_start, weights, offset_low):
    row_index = np.arange(row_count)[:, None] + row_start
    col_index = np.arange(col_count)[None, :] + col_start
    position = row_index - col_index - offset_low
    inside = (position >= 0) & (position < len(weights))
    return np.where(inside, weights[np.clip(position, 0, len(weights) - 1)], 0.0)


def f32(value):
    return float(np.float32(value))


MAGIC = {k: f32(w) for k, w in zip(range(1 - MTAPS // 2, MTAPS // 2 + 1), magic_weights(MTAPS))}
MAGIC_T = {-k: w for k, w in MAGIC.items()}
KINETIC = {
    d: f32(w) for d, w in zip(range(-KREACH, KREACH + 1), second_weights(KREACH))
}
LOW = MTAPS // 2
HIGH = MTAPS // 2 - 1


def two_part(matrix):
    width = matrix.shape[0]
    block = np.kron(np.eye(LANES // width), matrix).astype(np.float32)
    high = block.astype(jnp.bfloat16)
    low = (block - high.astype(np.float32)).astype(jnp.bfloat16)
    return np.block([[high, low], [high, np.zeros_like(low)]])


def split(value):
    high = value.astype(jnp.bfloat16)
    low = (value - high.astype(jnp.float32)).astype(jnp.bfloat16)
    return high, low


def lane_product(parts, matrix):
    both = jnp.dot(parts, matrix, preferred_element_type=jnp.float32)
    return both[:, :LANES] + both[:, LANES:]


def params(mib):
    return pltpu.CompilerParams(vmem_limit_bytes=mib << 20)


def cost(flops, bytes_accessed):
    return pl.CostEstimate(flops=flops, bytes_accessed=bytes_accessed, transcendentals=0)


class Shape:
    def __init__(self, slots, depth, plane, owners):
        self.slots, self.depth, self.plane, self.owners = slots, depth, plane, owners
        self.box = math.isqrt(plane)
        self.chunks = plane // LANES
        self.across = min(owners, self.chunks)
        self.layered = owners // self.across
        self.layers = depth // self.layered
        self.width = plane // self.across
        self.inner = self.width // LANES

    def at(self, layer, block, inner):
        piece = (layer // self.layers) * self.across + block
        lanes = slice(inner * LANES, (inner + 1) * LANES)
        return piece, layer % self.layers, slice(None), lanes

    def side(self, layer, block, inner):
        return block, layer, slice(None), slice(inner * LANES, (inner + 1) * LANES)


def reorder_kernel(sh, psi_ref, v_ref, out_ref, up_ref, down_ref):
    for group in range(sh.layered):
        first = group * sh.layers
        rows = jnp.transpose(psi_ref[:, first : first + sh.layers, :], (1, 0, 2))
        for block in range(sh.across):
            lanes = slice(block * sh.width, (block + 1) * sh.width)
            out_ref[group * sh.across + block] = rows[:, :, lanes]
            skip = 1 if group == 0 else 0
            up_ref[block, first - 1 + skip : first - 1 + sh.layers] = rows[skip:, :, lanes]
            keep = sh.layers - (1 if group == sh.layered - 1 else 0)
            down_ref[block, first : first + keep] = rows[:keep, :, lanes]
    for block in range(sh.across):
        lanes = slice(block * sh.width, (block + 1) * sh.width)
        up_ref[block, sh.depth - 1] = v_ref[sh.depth - sh.slots :, lanes]
        down_ref[block, sh.depth - 1] = v_ref[: sh.slots, lanes]


def reorder(sh, psi, potential):
    send = jax.ShapeDtypeStruct((sh.across, sh.depth, sh.slots, sh.width), jnp.float32)
    return pl.pallas_call(
        functools.partial(reorder_kernel, sh),
        out_shape=(
            jax.ShapeDtypeStruct((sh.owners, sh.layers, sh.slots, sh.width), jnp.float32),
            send,
            send,
        ),
        compiler_params=params(14),
        name="reorder",
    )(psi, potential)


def odd_pairs(even, lane):
    turned = [pltpu.roll(v, LANES // 2, 1) for v in even]
    zero = jnp.zeros_like(even[0])
    low = [zero] + turned
    high = turned + [zero]
    return [jnp.where(lane, a, b) for a, b in zip(low, high)]


def row_filter(even, odd, weights):
    count = len(even)
    out = []
    for b in range(count):
        total = None
        for d, w in weights.items():
            e = b + d // 2
            if d % 2 == 0:
                if not 0 <= e < count:
                    continue
                term = even[e]
            else:
                if not 0 <= e + 1 <= count:
                    continue
                term = odd[e + 1]
            total = term * w if total is None else total + term * w
        out.append(total)
    return out


def row_filter_even(even, odd, weights, reach):
    count = len(even)
    out = []
    for b in range(count):
        total = even[b] * weights[0]
        for d in range(1, reach + 1):
            if d % 2 == 0:
                places = [e for e in (b + d // 2, b - d // 2) if 0 <= e < count]
                terms = [even[e] for e in places]
            else:
                places = [e for e in (b + d // 2 + 1, b - d // 2) if 0 <= e <= count]
                terms = [odd[e] for e in places]
            if not terms:
                continue
            term = terms[0] if len(terms) == 1 else terms[0] + terms[1]
            total = total + term * weights[d]
        out.append(total)
    return out


def half_mask(slots):
    return lax.broadcasted_iota(jnp.int32, (slots, LANES), 1) < LANES // 2


def lane_pass(sh, source, at, matrices, targets, layers):
    def body(block, carry):
        parts = []
        for inner in range(sh.inner):
            rows = jnp.concatenate(
                [source[at(layer, block, inner)] for layer in range(layers)], 0
            )
            high, low = split(rows)
            parts.append(jnp.concatenate([high, low], 1))
        parts = jnp.concatenate(parts, 0)
        for matrix, target in zip(matrices, targets):
            result = lane_product(parts, matrix[...])
            result = result.reshape(sh.inner, layers, sh.slots, LANES)
            for inner in range(sh.inner):
                for layer in range(layers):
                    target[layer, block * sh.inner + inner] = result[inner, layer]
        return carry

    lax.fori_loop(0, sh.across, body, 0)


def own_kernel(sh, c_ref, fwd_ref, kin_ref, w_out, kin_out, x_ref):
    lane_pass(sh, c_ref, sh.at, [fwd_ref, kin_ref], [x_ref, kin_out], sh.depth)
    lane = half_mask(sh.slots)

    for group in range(sh.layered):

        def body(i, carry):
            layer = group * sh.layers + i
            even = [x_ref[layer, b] for b in range(sh.chunks)]
            for b, v in enumerate(row_filter(even, odd_pairs(even, lane), MAGIC)):
                w_out[layer, b] = v
            even = [
                c_ref[
                    group * sh.across + b // sh.inner,
                    i,
                    :,
                    (b % sh.inner) * LANES : (b % sh.inner + 1) * LANES,
                ]
                for b in range(sh.chunks)
            ]
            sums = row_filter_even(even, odd_pairs(even, lane), KINETIC, KREACH)
            for b, v in enumerate(sums):
                kin_out[layer, b] += v
            return carry

        lax.fori_loop(0, sh.layers, body, 0)


def own_part(sh, c, fwd, kin):
    full = jax.ShapeDtypeStruct((sh.depth, sh.chunks, sh.slots, LANES), jnp.float32)
    return pl.pallas_call(
        functools.partial(own_kernel, sh),
        out_shape=(full, full),
        scratch_shapes=[pltpu.VMEM(full.shape, jnp.float32)],
        compiler_params=params(16),
        cost_estimate=cost(10**10, 10**7),
        name="own_part",
    )(c, fwd, kin)


def halo_kernel(
    sh, lo_ref, c_ref, hi_ref, w_ref, kin_ref, v_ref, fwd_ref, bwd_ref, out_ref,
    x_ref, wlo_ref, whi_ref,
):
    lane = half_mask(sh.slots)
    depth = sh.depth
    reach = depth - 1
    for side_ref, target in ((lo_ref, wlo_ref), (hi_ref, whi_ref)):
        lane_pass(sh, side_ref, sh.side, [fwd_ref], [x_ref], reach)

        def filter_rows(layer, carry):
            even = [x_ref[layer, b] for b in range(sh.chunks)]
            for b, v in enumerate(row_filter(even, odd_pairs(even, lane), MAGIC)):
                target[layer, b] = v
            return carry

        lax.fori_loop(0, reach, filter_rows, 0)

    def along_z(block, carry):
        for inner in range(sh.inner):
            chunk = block * sh.inner + inner
            lanes = pl.ds(pl.multiple_of(chunk * LANES, LANES), LANES)

            def coeff(z):
                if z < 0:
                    return lo_ref[sh.side(z + reach, block, inner)]
                if z < depth:
                    return c_ref[sh.at(z, block, inner)]
                return hi_ref[sh.side(z - depth, block, inner)]

            def mixed(z):
                if z < 0:
                    return wlo_ref[z + reach, chunk]
                return w_ref[z, chunk] if z < depth else whi_ref[z - depth, chunk]

            def level(z):
                part = slice(inner * LANES, (inner + 1) * LANES)
                if z < 0:
                    row = lo_ref[block, reach, z + sh.slots : z + sh.slots + 1, part]
                elif z < depth:
                    row = v_ref[z : z + 1, lanes]
                else:
                    row = hi_ref[block, reach, z - depth : z - depth + 1, part]
                return jnp.broadcast_to(row, (sh.slots, LANES))

            values = {z: mixed(z) for z in range(-LOW - HIGH, depth + LOW + HIGH)}
            grid = {}
            for p in range(-LOW, depth + HIGH):
                total = None
                for k, w in MAGIC.items():
                    term = values[p + k] * w
                    total = term if total is None else total + term
                grid[p] = total * level(p)
            for q in range(depth):
                total = None
                for k, w in MAGIC.items():
                    term = grid[q - k] * w
                    total = term if total is None else total + term
                x_ref[q, chunk] = total
            cs = {z: coeff(z) for z in range(-KREACH, depth + KREACH)}
            for q in range(depth):
                total = kin_ref[q, chunk] + cs[q] * KINETIC[0]
                for d in range(1, KREACH + 1):
                    total = total + (cs[q + d] + cs[q - d]) * KINETIC[d]
                whi_ref[q, chunk] = total
        return carry

    lax.fori_loop(0, sh.across, along_z, 0)

    def filter_back(layer, carry):
        even = [x_ref[layer, b] for b in range(sh.chunks)]
        for b, v in enumerate(row_filter(even, odd_pairs(even, lane), MAGIC_T)):
            wlo_ref[layer, b] = v
        return carry

    lax.fori_loop(0, depth, filter_back, 0)

    def finish(block, carry):
        parts = []
        for inner in range(sh.inner):
            chunk = block * sh.inner + inner
            rows = jnp.concatenate([wlo_ref[layer, chunk] for layer in range(depth)], 0)
            high, low = split(rows)
            parts.append(jnp.concatenate([high, low], 1))
        result = lane_product(jnp.concatenate(parts, 0), bwd_ref[...])
        result = result.reshape(sh.inner, depth, sh.slots, LANES)
        for inner in range(sh.inner):
            chunk = block * sh.inner + inner
            for layer in range(depth):
                out_ref[sh.at(layer, block, inner)] = result[inner, layer] + whi_ref[layer, chunk]
        return carry

    lax.fori_loop(0, sh.across, finish, 0)


def halo_part(sh, lo, c, hi, w, kin, v, fwd, bwd):
    full = pltpu.VMEM((sh.depth, sh.chunks, sh.slots, LANES), jnp.float32)
    return pl.pallas_call(
        functools.partial(halo_kernel, sh),
        out_shape=jax.ShapeDtypeStruct(c.shape, jnp.float32),
        scratch_shapes=[full] * 3,
        compiler_params=params(26),
        cost_estimate=cost(3 * 10**10, 10**7),
        name="halo_part",
    )(lo, c, hi, w, kin, v, fwd, bwd)


def selection(slot_ref, count, slots_all):
    column = lax.broadcasted_iota(jnp.int32, (count, slots_all), 1)
    return (column == slot_ref[...]).astype(jnp.float32)


def packed_rows(matrix, fold):
    rows = matrix.shape[0] // fold
    return jnp.concatenate([matrix[i * rows : (i + 1) * rows] for i in range(fold)], 1)


def unpacked_rows(matrix, fold):
    cols = matrix.shape[1] // fold
    return jnp.concatenate([matrix[:, i * cols : (i + 1) * cols] for i in range(fold)], 0)


def gram_kernel(sh, fold, c_ref, a_ref, slot_ref, out_ref):
    total_slots = sh.owners * sh.slots
    count = slot_ref.shape[0]

    def parts(ref, layer):
        rows = ref[:, layer].reshape(total_slots, sh.width)
        return jnp.concatenate(split(rows), 0)

    def body(layer, total):
        return total + lax.dot_general(
            parts(c_ref, layer),
            parts(a_ref, layer),
            (((1,), (1,)), ((), ())),
            preferred_element_type=jnp.float32,
        )

    both = jnp.zeros((2 * total_slots, 2 * total_slots), jnp.float32)
    both = lax.fori_loop(0, sh.layers, body, both, unroll=sh.layers <= 16 and total_slots <= 64)
    wide = both[:total_slots] + both[total_slots:]
    full = wide[:, :total_slots] + wide[:, total_slots:]
    chosen = selection(slot_ref, count, total_slots)
    rows = jnp.dot(chosen, full, precision=highest, preferred_element_type=jnp.float32)
    picked = lax.dot_general(
        rows, chosen, (((1,), (1,)), ((), ())), precision=highest,
        preferred_element_type=jnp.float32,
    ) * (1.0 / sh.box**3)
    picked = packed_rows(picked, fold)
    if len(out_ref.shape) == 2:
        out_ref[...] = picked
    else:
        out_ref[...] = jnp.broadcast_to(picked[None], out_ref.shape)


def gram(sh, c, a, slot, fold, copies):
    count = slot.shape[0]
    shape = (count // fold, count * fold)
    if copies:
        shape = (copies,) + shape
    return pl.pallas_call(
        functools.partial(gram_kernel, sh, fold),
        out_shape=jax.ShapeDtypeStruct(shape, jnp.float32),
        compiler_params=params(16),
        cost_estimate=cost(10**9, 10**7),
        name="gram",
    )(c, a, slot)


def correct_kernel(sh, fold, own, c_ref, a_ref, slot_ref, part_ref, out_ref, mult_ref, inv_ref):
    total_slots = sh.owners * sh.slots
    count = slot_ref.shape[0]
    packed = part_ref[...]
    if packed.ndim == 3:
        packed = packed.sum(0)
    multipliers = unpacked_rows(packed, fold)
    mult_ref[...] = multipliers
    row = lax.broadcasted_iota(jnp.int32, (count, count), 0)
    col = lax.broadcasted_iota(jnp.int32, (count, count), 1)
    diagonal = jnp.sum(jnp.where(row == col, multipliers, 0.0), axis=1, keepdims=True)
    denominator = 2.0 * coupling_z + 4.0 * coupling_xy + 1.0 + jnp.abs(diagonal)
    inv_ref[...] = jnp.broadcast_to(1.0 / denominator, (count, LANES))
    chosen = selection(slot_ref, count, total_slots)
    mixing = lax.dot_general(
        multipliers, chosen, (((0,), (0,)), ((), ())), precision=highest,
        preferred_element_type=jnp.float32,
    )
    weights = jnp.concatenate([chosen, -mixing], 1)
    high, low = split(weights)
    weights = jnp.concatenate(
        [
            jnp.concatenate([high, high], 1),
            jnp.concatenate([low, jnp.zeros_like(low)], 1),
        ],
        0,
    )

    def body(layer):
        a_rows = split(a_ref[:, layer].reshape(total_slots, sh.width))
        c_rows = split(c_ref[:, layer].reshape(total_slots, sh.width))
        data = jnp.concatenate([a_rows[0], c_rows[0], a_rows[1], c_rows[1]], 0)
        both = jnp.dot(weights, data, preferred_element_type=jnp.float32)
        result = both[:count] + both[count:]
        for owner in range(sh.owners):
            out_ref[owner, layer * own : (layer + 1) * own] = result[
                owner * own : (owner + 1) * own
            ]

    for layer in range(sh.layers):
        body(layer)


def correct(sh, c, a, slot, part, fold):
    count = slot.shape[0]
    own = count // sh.owners
    return pl.pallas_call(
        functools.partial(correct_kernel, sh, fold, own),
        out_shape=(
            jax.ShapeDtypeStruct((sh.owners, sh.layers * own, sh.width), jnp.float32),
            jax.ShapeDtypeStruct((count, count), jnp.float32),
            jax.ShapeDtypeStruct((count, LANES), jnp.float32),
        ),
        compiler_params=params(16),
        cost_estimate=cost(10**9, 10**7),
        name="correct",
    )(c, a, slot, part)


def relax_kernel(
    sh, own, ends_ref, r_ref, lo_ref, hi_ref, inv_ref, res_out, dir_out, res_ref, one_ref, two_ref
):
    rows = sh.depth * own
    edge = SWEEPS * own
    first = pl.multiple_of(ends_ref[0] * own, own)
    inverse = inv_ref[pl.ds(first, own), :]
    inverse = jnp.concatenate([inverse] * (8 // own), 0)
    keep_lo = inverse * ends_ref[1].astype(jnp.float32)
    keep_hi = inverse * ends_ref[2].astype(jnp.float32)
    tiles = (rows + 2 * edge) // 8
    edge_tiles = edge // 8

    def scale(tile):
        if tile < edge_tiles:
            return keep_lo
        return keep_hi if tile >= tiles - edge_tiles else inverse

    group = min(4, sh.chunks)
    blank = jnp.zeros((rows + 2 * edge, LANES), jnp.float32)
    for ref in (one_ref, two_ref):
        ref[0] = blank
        ref[sh.chunks + 1] = blank

    def gather(block, carry):
        for inner in range(sh.inner):
            chunk = block * sh.inner + inner
            lanes = slice(inner * LANES, (inner + 1) * LANES)
            pieces = [lo_ref[block, :, lanes]]
            pieces += [r_ref[g * sh.across + block, :, lanes] for g in range(sh.layered)]
            pieces += [hi_ref[block, :, lanes]]
            column = jnp.concatenate(pieces, 0)
            for tile in range(tiles):
                value = column[tile * 8 : (tile + 1) * 8]
                res_ref[chunk, tile * 8 : (tile + 1) * 8] = value
                one_ref[chunk + 1, tile * 8 : (tile + 1) * 8] = value * scale(tile)
        return carry

    lax.fori_loop(0, sh.across, gather, 0)

    sub = lax.broadcasted_iota(jnp.int32, (8, LANES), 0)
    lane = lax.broadcasted_iota(jnp.int32, (8, LANES), 1)
    upper = sub >= own
    right_half = lane >= LANES // 2
    not_last = (lane % sh.box) != sh.box - 1
    not_first = (lane % sh.box) != 0
    assert 8 // own == 2

    def sweep(source, target, tile_list):
        def body(step, carry):
            seen = {}

            def value_at(column, tile):
                if not 0 <= tile < tiles:
                    return jnp.zeros((8, LANES), jnp.float32)
                if (column, tile) not in seen:
                    seen[column, tile] = source[step * group + column + 1, pl.ds(tile * 8, 8)]
                return seen[column, tile]

            for column in range(group):
                for tile in tile_list:
                    here = pl.ds(tile * 8, 8)
                    value = value_at(column, tile)
                    beside = jnp.where(
                        upper, value_at(column, tile - 1), value_at(column, tile + 1)
                    )
                    along_z = pltpu.roll(value + beside, own, 0)
                    beside = jnp.where(
                        right_half, value_at(column - 1, tile), value_at(column + 1, tile)
                    )
                    along_y = pltpu.roll(value + beside, LANES // 2, 1)
                    along_x = pltpu.roll(jnp.where(not_last, value, 0.0), 1, 1) + pltpu.roll(
                        jnp.where(not_first, value, 0.0), LANES - 1, 1
                    )
                    total = (
                        res_ref[step * group + column, here]
                        + coupling_xy * (along_y + along_x)
                        + coupling_z * along_z
                    )
                    target[step * group + column + 1, here] = total * scale(tile)
            return carry

        lax.fori_loop(0, sh.chunks // group, body, 0)

    source, target = one_ref, two_ref
    for done in range(1, SWEEPS + 1):
        first_tile = done * own // 8
        sweep(source, target, range(first_tile, tiles - first_tile))
        source, target = target, source

    def spread(step, carry):
        for column in range(group):
            chunk = step * group + column
            out_lanes = pl.ds(pl.multiple_of(chunk * LANES, LANES), LANES)
            for orbital in range(own):
                here = pl.ds(edge + orbital, sh.depth, stride=own)
                res_out[orbital, :, out_lanes] = res_ref[chunk, here, :]
                dir_out[orbital, :, out_lanes] = source[chunk + 1, here, :]
        return carry

    lax.fori_loop(0, sh.chunks // group, spread, 0)


def relax(sh, own, ends, r, lo, hi, inverse):
    rows = (sh.depth + 2 * SWEEPS) * own
    scratch = pltpu.VMEM((sh.chunks, rows, LANES), jnp.float32)
    padded = pltpu.VMEM((sh.chunks + 2, rows, LANES), jnp.float32)
    out = jax.ShapeDtypeStruct((own, sh.depth, sh.plane), jnp.float32)
    vmem = pl.BlockSpec(memory_space=pltpu.VMEM)
    return pl.pallas_call(
        functools.partial(relax_kernel, sh, own),
        out_shape=(out, out),
        in_specs=[pl.BlockSpec(memory_space=pltpu.SMEM)] + [vmem] * 4,
        scratch_shapes=[scratch, padded, padded],
        compiler_params=params(14),
        cost_estimate=cost(10**9, 10**7),
        name="relax",
    )(ends, r, lo, hi, inverse)


def to_all(value, axes):
    return lax.all_to_all(value, axes, split_axis=0, concat_axis=0, tiled=True)


def local(psi, potential, orbital_slot):
    slots, depth, plane = psi.shape
    owners = lax.axis_size("orb")
    boxes = lax.axis_size("box")
    sh = Shape(slots, depth, plane, owners)
    count = orbital_slot.shape[0]
    own = count // owners
    magic = banded(sh.box, sh.box, 0, 0, magic_weights(MTAPS), 1 - MTAPS // 2)
    kinetic = banded(sh.box, sh.box, 0, 0, second_weights(KREACH), -KREACH)
    fwd, bwd, kin = (jnp.asarray(two_part(m)) for m in (magic, magic.T, kinetic))

    c, up, down = reorder(sh, psi, potential)
    lo = lax.ppermute(up, "box", [(i, i + 1) for i in range(boxes - 1)])
    hi = lax.ppermute(down, "box", [(i + 1, i) for i in range(boxes - 1)])
    pieces = to_all(c, "orb")
    w, kin_own = own_part(sh, c, fwd, kin)
    applied = halo_part(sh, lo, c, hi, w, kin_own, potential, fwd, bwd)
    applied_pieces = to_all(applied, "orb")

    slot = orbital_slot.reshape(count, 1)
    fold = max(1, LANES // count)
    devices = owners * boxes
    copies = devices if devices * count * count <= 1 << 20 else 0
    part = gram(sh, pieces, applied_pieces, slot, fold, copies)
    part = to_all(part, ("orb", "box")) if copies else lax.psum(part, ("orb", "box"))
    corrected, multipliers, inverse = correct(sh, pieces, applied_pieces, slot, part, fold)
    returned = to_all(corrected, "orb")
    edge = SWEEPS * own
    box = lax.axis_index("box")
    from_low = lax.ppermute(
        returned[-sh.across :, -edge:], "box", [(i, i + 1) for i in range(boxes - 1)]
    )
    from_high = lax.ppermute(
        returned[: sh.across, :edge], "box", [(i + 1, i) for i in range(boxes - 1)]
    )
    ends = jnp.stack(
        [lax.axis_index("orb"), (box > 0).astype(jnp.int32), (box < boxes - 1).astype(jnp.int32)]
    ).astype(jnp.int32)
    residual, direction = relax(sh, own, ends, returned, from_low, from_high, inverse)
    return (residual, direction, multipliers)


def solution(mesh):
    in_specs = (P("orb", "box", None), P("box", None), P())
    out_specs = (P("orb", "box", None), P("orb", "box", None), P())
    return jax.shard_map(local, mesh=mesh, in_specs=in_specs, out_specs=out_specs, check_vma=False)
```

```python
import functools
import math

import jax
import jax.numpy as jnp
import numpy as np
from jax import lax
from jax.experimental import pallas as pl
from jax.experimental.pallas import tpu as pltpu
from jax.sharding import PartitionSpec as P

MTAPS = 16
KREACH = 14
SWEEPS = 4
LANES = 128

highest = lax.Precision.HIGHEST
coupling_z = 4.0
coupling_xy = 1.0


def magic_weights(tap_count):
    half_len = tap_count // 2
    offsets = np.arange(1 - half_len, half_len + 1) * 1.0
    weights = np.ones(tap_count)
    for index_a in range(tap_count):
        for index_b in range(tap_count):
            if index_b != index_a:
                weights[index_a] *= (0.25 - offsets[index_b]) / (
                    offsets[index_a] - offsets[index_b]
                )
    return weights


def second_weights(reach_cells):
    factor = math.factorial(reach_cells) ** 2
    weights = np.zeros(2 * reach_cells + 1)
    for distance in range(1, reach_cells + 1):
        entry_value = (
            2.0
            * (-1) ** (distance + 1)
            * factor
            / (
                distance
                * distance
                * math.factorial(reach_cells - distance)
                * math.factorial(reach_cells + distance)
            )
        )
        weights[reach_cells + distance] = entry_value
        weights[reach_cells - distance] = entry_value
    weights[reach_cells] = -weights.sum()
    return -0.5 * weights


def banded(row_count, col_count, row_start, col_start, weights, offset_low):
    row_index = np.arange(row_count)[:, None] + row_start
    col_index = np.arange(col_count)[None, :] + col_start
    position = row_index - col_index - offset_low
    inside = (position >= 0) & (position < len(weights))
    return np.where(inside, weights[np.clip(position, 0, len(weights) - 1)], 0.0)


def f32(value):
    return float(np.float32(value))


MAGIC = {k: f32(w) for k, w in zip(range(1 - MTAPS // 2, MTAPS // 2 + 1), magic_weights(MTAPS))}
MAGIC_T = {-k: w for k, w in MAGIC.items()}
KINETIC = {
    d: f32(w) for d, w in zip(range(-KREACH, KREACH + 1), second_weights(KREACH))
}
LOW = MTAPS // 2
HIGH = MTAPS // 2 - 1


def two_part(matrix):
    width = matrix.shape[0]
    block = np.kron(np.eye(LANES // width), matrix).astype(np.float32)
    high = block.astype(jnp.bfloat16)
    low = (block - high.astype(np.float32)).astype(jnp.bfloat16)
    return np.block([[high, low], [high, np.zeros_like(low)]])


def split(value):
    high = value.astype(jnp.bfloat16)
    low = (value - high.astype(jnp.float32)).astype(jnp.bfloat16)
    return high, low


def lane_product(parts, matrix):
    both = jnp.dot(parts, matrix, preferred_element_type=jnp.float32)
    return both[:, :LANES] + both[:, LANES:]


def params(mib):
    return pltpu.CompilerParams(vmem_limit_bytes=mib << 20)


def cost(flops, bytes_accessed):
    return pl.CostEstimate(flops=flops, bytes_accessed=bytes_accessed, transcendentals=0)


class Shape:
    def __init__(self, slots, depth, plane, owners):
        self.slots, self.depth, self.plane, self.owners = slots, depth, plane, owners
        self.box = math.isqrt(plane)
        self.chunks = plane // LANES
        self.across = min(owners, self.chunks)
        self.layered = owners // self.across
        self.layers = depth // self.layered
        self.width = plane // self.across
        self.inner = self.width // LANES

    def at(self, layer, block, inner):
        piece = (layer // self.layers) * self.across + block
        lanes = slice(inner * LANES, (inner + 1) * LANES)
        return piece, layer % self.layers, slice(None), lanes


def pack_kernel(sh, psi_hbm, out_hbm, buffer, sems_in, sems_out):
    def pair(index):
        first = (index // sh.across) * sh.layers
        lane = (index % sh.across) * sh.width
        source = psi_hbm.at[:, pl.ds(first, sh.layers), pl.ds(lane, sh.width)]
        return (
            pltpu.make_async_copy(source, buffer.at[index], sems_in.at[index]),
            pltpu.make_async_copy(buffer.at[index], out_hbm.at[index], sems_out.at[index]),
        )

    copies = [pair(index) for index in range(sh.owners)]
    for arrive, leave in copies:
        arrive.start()
    for arrive, leave in copies:
        arrive.wait()
        leave.start()
    for arrive, leave in copies:
        leave.wait()


def pack(sh, psi):
    shape = (sh.owners, sh.slots, sh.layers, sh.width)
    return pl.pallas_call(
        functools.partial(pack_kernel, sh),
        out_shape=pltpu.HBM(shape, jnp.float32),
        in_specs=[pl.BlockSpec(memory_space=pltpu.HBM)],
        out_specs=pl.BlockSpec(memory_space=pltpu.HBM),
        scratch_shapes=[
            pltpu.VMEM(shape, jnp.float32),
            pltpu.SemaphoreType.DMA((sh.owners,)),
            pltpu.SemaphoreType.DMA((sh.owners,)),
        ],
        compiler_params=params(8),
        cost_estimate=cost(0, 2 * psi.size * 4),
        name="pack",
    )(pltpu.with_memory_space_constraint(psi, pltpu.HBM))


def turn_kernel(sh, in_ref, out_ref):
    for index in range(sh.owners):
        out_ref[index] = jnp.transpose(in_ref[index], (1, 0, 2))


def turn(sh, pieces):
    return pl.pallas_call(
        functools.partial(turn_kernel, sh),
        out_shape=pltpu.VMEM((sh.owners, sh.layers, sh.slots, sh.width), jnp.float32),
        compiler_params=params(10),
        cost_estimate=cost(10**8, 2 * pieces.size * 4),
        name="turn",
    )(pltpu.with_memory_space_constraint(pieces, pltpu.HBM))


def odd_pairs(even, lane):
    turned = [pltpu.roll(v, LANES // 2, 1) for v in even]
    zero = jnp.zeros_like(even[0])
    low = [zero] + turned
    high = turned + [zero]
    return [jnp.where(lane, a, b) for a, b in zip(low, high)]


def row_filter(even, odd, weights):
    count = len(even)
    out = []
    for b in range(count):
        total = None
        for d, w in weights.items():
            e = b + d // 2
            if d % 2 == 0:
                if not 0 <= e < count:
                    continue
                term = even[e]
            else:
                if not 0 <= e + 1 <= count:
                    continue
                term = odd[e + 1]
            total = term * w if total is None else total + term * w
        out.append(total)
    return out


def row_filter_even(even, odd, weights, reach):
    count = len(even)
    out = []
    for b in range(count):
        total = even[b] * weights[0]
        for d in range(1, reach + 1):
            if d % 2 == 0:
                places = [e for e in (b + d // 2, b - d // 2) if 0 <= e < count]
                terms = [even[e] for e in places]
            else:
                places = [e for e in (b + d // 2 + 1, b - d // 2) if 0 <= e <= count]
                terms = [odd[e] for e in places]
            if not terms:
                continue
            term = terms[0] if len(terms) == 1 else terms[0] + terms[1]
            total = total + term * weights[d]
        out.append(total)
    return out


def half_mask(slots):
    return lax.broadcasted_iota(jnp.int32, (slots, LANES), 1) < LANES // 2


def lane_pass(sh, slab, kept, matrices, targets):
    depth = sh.depth

    def body(block, carry):
        parts = []
        for inner in range(sh.inner):
            chunk = block * sh.inner + inner
            lanes = pl.ds(pl.multiple_of(chunk * LANES, LANES), LANES)
            rows = jnp.transpose(slab[:, :, lanes], (1, 0, 2))
            for layer in range(depth):
                kept[layer, chunk] = rows[layer]
            high, low = split(rows.reshape(depth * sh.slots, LANES))
            parts.append(jnp.concatenate([high, low], 1))
        parts = jnp.concatenate(parts, 0)
        for matrix, target in zip(matrices, targets):
            result = lane_product(parts, matrix[...])
            result = result.reshape(sh.inner, depth, sh.slots, LANES)
            for inner in range(sh.inner):
                for layer in range(depth):
                    target[layer, block * sh.inner + inner] = result[inner, layer]
        return carry

    lax.fori_loop(0, sh.across, body, 0)


def own_kernel(sh, psi_ref, fwd_ref, kin_ref, c_out, w_out, kin_out, x_ref):
    lane_pass(sh, psi_ref, c_out, [fwd_ref, kin_ref], [x_ref, kin_out])
    lane = half_mask(sh.slots)

    def body(layer, carry):
        even = [x_ref[layer, b] for b in range(sh.chunks)]
        for b, v in enumerate(row_filter(even, odd_pairs(even, lane), MAGIC)):
            w_out[layer, b] = v
        even = [c_out[layer, b] for b in range(sh.chunks)]
        sums = row_filter_even(even, odd_pairs(even, lane), KINETIC, KREACH)
        for b, v in enumerate(sums):
            kin_out[layer, b] += v
        return carry

    lax.fori_loop(0, sh.depth, body, 0)


def own_part(sh, psi, fwd, kin):
    full = jax.ShapeDtypeStruct((sh.depth, sh.chunks, sh.slots, LANES), jnp.float32)
    return pl.pallas_call(
        functools.partial(own_kernel, sh),
        out_shape=(full, full, full),
        scratch_shapes=[pltpu.VMEM(full.shape, jnp.float32)],
        compiler_params=params(14),
        cost_estimate=cost(10**10, 10**7),
        name="own_part",
    )(psi, fwd, kin)


def halo_kernel(
    sh, lo_hbm, hi_hbm, c_ref, w_ref, kin_ref, vlo_ref, v_ref, vhi_ref, fwd_ref, bwd_ref,
    out_hbm, lo_ref, hi_ref, clo_ref, chi_ref, x_ref, wlo_ref, whi_ref, out_ref, sems, in_sems,
):
    lane = half_mask(sh.slots)
    depth = sh.depth
    reach = depth - 1
    arrivals = [
        pltpu.make_async_copy(lo_hbm, lo_ref, in_sems.at[0]),
        pltpu.make_async_copy(hi_hbm, hi_ref, in_sems.at[1]),
    ]
    for copy in arrivals:
        copy.start()
    for copy, side_ref, kept, target, first in (
        (arrivals[0], lo_ref, clo_ref, wlo_ref, 1),
        (arrivals[1], hi_ref, chi_ref, whi_ref, 0),
    ):
        copy.wait()
        lane_pass(sh, side_ref, kept, [fwd_ref], [x_ref])

        def filter_rows(layer, carry):
            even = [x_ref[layer, b] for b in range(sh.chunks)]
            for b, v in enumerate(row_filter(even, odd_pairs(even, lane), MAGIC)):
                target[layer, b] = v
            return carry

        lax.fori_loop(first, first + reach, filter_rows, 0)

    def along_z(chunk, carry):
        lanes = pl.ds(pl.multiple_of(chunk * LANES, LANES), LANES)

        def pick(below, here, above, z):
            ref = below if z < 0 else (here if z < depth else above)
            return ref[z % depth, chunk]

        def level(z):
            ref = vlo_ref if z < 0 else (v_ref if z < depth else vhi_ref)
            return jnp.broadcast_to(ref[z % depth : z % depth + 1, lanes], (sh.slots, LANES))

        values = {
            z: pick(wlo_ref, w_ref, whi_ref, z) for z in range(-LOW - HIGH, depth + LOW + HIGH)
        }
        grid = {}
        for p in range(-LOW, depth + HIGH):
            total = None
            for k, w in MAGIC.items():
                term = values[p + k] * w
                total = term if total is None else total + term
            grid[p] = total * level(p)
        for q in range(depth):
            total = None
            for k, w in MAGIC.items():
                term = grid[q - k] * w
                total = term if total is None else total + term
            x_ref[q, chunk] = total
        cs = {z: pick(clo_ref, c_ref, chi_ref, z) for z in range(-KREACH, depth + KREACH)}
        for q in range(depth):
            total = kin_ref[q, chunk] + cs[q] * KINETIC[0]
            for d in range(1, KREACH + 1):
                total = total + (cs[q + d] + cs[q - d]) * KINETIC[d]
            whi_ref[q, chunk] = total
        return carry

    lax.fori_loop(0, sh.chunks, along_z, 0)

    def filter_back(layer, carry):
        even = [x_ref[layer, b] for b in range(sh.chunks)]
        for b, v in enumerate(row_filter(even, odd_pairs(even, lane), MAGIC_T)):
            wlo_ref[layer, b] = v
        return carry

    lax.fori_loop(0, depth, filter_back, 0)

    def piece(index):
        return pltpu.make_async_copy(out_ref.at[index], out_hbm.at[index], sems.at[index])

    def finish(block, carry):
        parts = []
        for inner in range(sh.inner):
            chunk = block * sh.inner + inner
            rows = jnp.concatenate([wlo_ref[layer, chunk] for layer in range(depth)], 0)
            high, low = split(rows)
            parts.append(jnp.concatenate([high, low], 1))
        result = lane_product(jnp.concatenate(parts, 0), bwd_ref[...])
        result = result.reshape(sh.inner, depth, sh.slots, LANES)
        for inner in range(sh.inner):
            chunk = block * sh.inner + inner
            for layer in range(depth):
                out_ref[sh.at(layer, block, inner)] = result[inner, layer] + whi_ref[layer, chunk]
        for group in range(sh.layered):
            piece(group * sh.across + block).start()
        return carry

    lax.fori_loop(0, sh.across, finish, 0)
    for index in range(sh.owners):
        piece(index).wait()


def halo_part(sh, lo, hi, c, w, kin, v_lo, v, v_hi, fwd, bwd):
    full = pltpu.VMEM((sh.depth, sh.chunks, sh.slots, LANES), jnp.float32)
    out = (sh.owners, sh.layers, sh.slots, sh.width)
    hbm = pl.BlockSpec(memory_space=pltpu.HBM)
    vmem = pl.BlockSpec(memory_space=pltpu.VMEM)
    lo, hi = (pltpu.with_memory_space_constraint(x, pltpu.HBM) for x in (lo, hi))
    return pl.pallas_call(
        functools.partial(halo_kernel, sh),
        out_shape=pltpu.HBM(out, jnp.float32),
        in_specs=[hbm] * 2 + [vmem] * 8,
        out_specs=hbm,
        scratch_shapes=[pltpu.VMEM(lo.shape, jnp.float32)] * 2
        + [full] * 5
        + [
            pltpu.VMEM(out, jnp.float32),
            pltpu.SemaphoreType.DMA((sh.owners,)),
            pltpu.SemaphoreType.DMA((2,)),
        ],
        compiler_params=params(26),
        cost_estimate=cost(3 * 10**10, 10**7),
        name="halo_part",
    )(lo, hi, c, w, kin, v_lo, v, v_hi, fwd, bwd)


def selection(slot_ref, count, slots_all):
    column = lax.broadcasted_iota(jnp.int32, (count, slots_all), 1)
    return (column == slot_ref[...]).astype(jnp.float32)


def packed_rows(matrix, fold):
    rows = matrix.shape[0] // fold
    return jnp.concatenate([matrix[i * rows : (i + 1) * rows] for i in range(fold)], 1)


def unpacked_rows(matrix, fold):
    cols = matrix.shape[1] // fold
    return jnp.concatenate([matrix[:, i * cols : (i + 1) * cols] for i in range(fold)], 0)


def gram_kernel(sh, fold, c_ref, a_ref, slot_ref, out_ref):
    total_slots = sh.owners * sh.slots
    count = slot_ref.shape[0]

    def parts(ref, layer):
        rows = ref[:, layer].reshape(total_slots, sh.width)
        return jnp.concatenate(split(rows), 0)

    def body(layer, total):
        return total + lax.dot_general(
            parts(c_ref, layer),
            parts(a_ref, layer),
            (((1,), (1,)), ((), ())),
            preferred_element_type=jnp.float32,
        )

    both = jnp.zeros((2 * total_slots, 2 * total_slots), jnp.float32)
    both = lax.fori_loop(0, sh.layers, body, both, unroll=sh.layers <= 16 and total_slots <= 64)
    wide = both[:total_slots] + both[total_slots:]
    full = wide[:, :total_slots] + wide[:, total_slots:]
    chosen = selection(slot_ref, count, total_slots)
    rows = jnp.dot(chosen, full, precision=highest, preferred_element_type=jnp.float32)
    picked = lax.dot_general(
        rows, chosen, (((1,), (1,)), ((), ())), precision=highest,
        preferred_element_type=jnp.float32,
    ) * (1.0 / sh.box**3)
    picked = packed_rows(picked, fold)
    if len(out_ref.shape) == 2:
        out_ref[...] = picked
    else:
        out_ref[...] = jnp.broadcast_to(picked[None], out_ref.shape)


def gram(sh, c, a, slot, fold, copies):
    count = slot.shape[0]
    shape = (count // fold, count * fold)
    if copies:
        shape = (copies,) + shape
    return pl.pallas_call(
        functools.partial(gram_kernel, sh, fold),
        out_shape=jax.ShapeDtypeStruct(shape, jnp.float32),
        compiler_params=params(16),
        cost_estimate=cost(10**9, 10**7),
        name="gram",
    )(c, a, slot)


def correct_kernel(sh, fold, own, parts, c_ref, a_ref, slot_ref, part_ref, *outs):
    *out_refs, mult_ref, inv_ref = outs
    total_slots = sh.owners * sh.slots
    count = slot_ref.shape[0]
    packed = part_ref[...]
    if packed.ndim == 3:
        packed = packed.sum(0)
    multipliers = unpacked_rows(packed, fold)
    mult_ref[...] = multipliers
    row = lax.broadcasted_iota(jnp.int32, (count, count), 0)
    col = lax.broadcasted_iota(jnp.int32, (count, count), 1)
    diagonal = jnp.sum(jnp.where(row == col, multipliers, 0.0), axis=1, keepdims=True)
    denominator = 2.0 * coupling_z + 4.0 * coupling_xy + 1.0 + jnp.abs(diagonal)
    inv_ref[...] = jnp.broadcast_to(1.0 / denominator, (count, LANES))
    chosen = selection(slot_ref, count, total_slots)
    mixing = lax.dot_general(
        multipliers, chosen, (((0,), (0,)), ((), ())), precision=highest,
        preferred_element_type=jnp.float32,
    )
    weights = jnp.concatenate([chosen, -mixing], 1)
    high, low = split(weights)
    weights = jnp.concatenate(
        [
            jnp.concatenate([high, high], 1),
            jnp.concatenate([low, jnp.zeros_like(low)], 1),
        ],
        0,
    )

    def body(layer, place, out_ref):
        a_rows = split(a_ref[:, layer].reshape(total_slots, sh.width))
        c_rows = split(c_ref[:, layer].reshape(total_slots, sh.width))
        data = jnp.concatenate([a_rows[0], c_rows[0], a_rows[1], c_rows[1]], 0)
        both = jnp.dot(weights, data, preferred_element_type=jnp.float32)
        result = both[:count] + both[count:]
        for owner in range(sh.owners):
            out_ref[owner, place * own : (place + 1) * own] = result[
                owner * own : (owner + 1) * own
            ]

    for part, out_ref in zip(parts, out_refs):
        for place, layer in enumerate(part):
            body(layer, place, out_ref)


def correct(sh, c, a, slot, part, fold, parts):
    count = slot.shape[0]
    own = count // sh.owners
    return pl.pallas_call(
        functools.partial(correct_kernel, sh, fold, own, parts),
        out_shape=tuple(
            jax.ShapeDtypeStruct((sh.owners, len(layers) * own, sh.width), jnp.float32)
            for layers in parts
        )
        + (
            jax.ShapeDtypeStruct((count, count), jnp.float32),
            jax.ShapeDtypeStruct((count, LANES), jnp.float32),
        ),
        compiler_params=params(16),
        cost_estimate=cost(10**9, 10**7),
        name="correct",
    )(c, a, slot, part)


def relax_kernel(sh, own, parts, ends_ref, *refs):
    r_refs = refs[: len(parts)]
    lo_ref, hi_ref, inv_ref, res_out, dir_out, res_ref, one_ref, two_ref = refs[len(parts) :]
    places = {layer: (ref, i) for part, ref in zip(parts, r_refs) for i, layer in enumerate(part)}
    rows = sh.depth * own
    edge = SWEEPS * own
    first = pl.multiple_of(ends_ref[0] * own, own)
    inverse = inv_ref[pl.ds(first, own), :]
    inverse = jnp.concatenate([inverse] * (8 // own), 0)
    keep_lo = inverse * ends_ref[1].astype(jnp.float32)
    keep_hi = inverse * ends_ref[2].astype(jnp.float32)
    tiles = (rows + 2 * edge) // 8
    edge_tiles = edge // 8

    def scale(tile):
        if tile < edge_tiles:
            return keep_lo
        return keep_hi if tile >= tiles - edge_tiles else inverse

    group = min(4, sh.chunks)
    blank = jnp.zeros((rows + 2 * edge, LANES), jnp.float32)
    for ref in (one_ref, two_ref):
        ref[0] = blank
        ref[sh.chunks + 1] = blank

    def gather(block, carry):
        for inner in range(sh.inner):
            chunk = block * sh.inner + inner
            lanes = slice(inner * LANES, (inner + 1) * LANES)
            pieces = [lo_ref[block, :, lanes]]
            for g in range(sh.layered):
                for layer in range(sh.layers):
                    ref, i = places[layer]
                    pieces.append(ref[g * sh.across + block, i * own : (i + 1) * own, lanes])
            pieces += [hi_ref[block, :, lanes]]
            column = jnp.concatenate(pieces, 0)
            for tile in range(tiles):
                value = column[tile * 8 : (tile + 1) * 8]
                res_ref[chunk, tile * 8 : (tile + 1) * 8] = value
                one_ref[chunk + 1, tile * 8 : (tile + 1) * 8] = value * scale(tile)
        return carry

    lax.fori_loop(0, sh.across, gather, 0)

    sub = lax.broadcasted_iota(jnp.int32, (8, LANES), 0)
    lane = lax.broadcasted_iota(jnp.int32, (8, LANES), 1)
    upper = sub >= own
    right_half = lane >= LANES // 2
    not_last = (lane % sh.box) != sh.box - 1
    not_first = (lane % sh.box) != 0
    assert 8 // own == 2

    def sweep(source, target, tile_list):
        def body(step, carry):
            seen = {}

            def value_at(column, tile):
                if not 0 <= tile < tiles:
                    return jnp.zeros((8, LANES), jnp.float32)
                if (column, tile) not in seen:
                    seen[column, tile] = source[step * group + column + 1, pl.ds(tile * 8, 8)]
                return seen[column, tile]

            for column in range(group):
                for tile in tile_list:
                    here = pl.ds(tile * 8, 8)
                    value = value_at(column, tile)
                    beside = jnp.where(
                        upper, value_at(column, tile - 1), value_at(column, tile + 1)
                    )
                    along_z = pltpu.roll(value + beside, own, 0)
                    beside = jnp.where(
                        right_half, value_at(column - 1, tile), value_at(column + 1, tile)
                    )
                    along_y = pltpu.roll(value + beside, LANES // 2, 1)
                    along_x = pltpu.roll(jnp.where(not_last, value, 0.0), 1, 1) + pltpu.roll(
                        jnp.where(not_first, value, 0.0), LANES - 1, 1
                    )
                    total = (
                        res_ref[step * group + column, here]
                        + coupling_xy * (along_y + along_x)
                        + coupling_z * along_z
                    )
                    target[step * group + column + 1, here] = total * scale(tile)
            return carry

        lax.fori_loop(0, sh.chunks // group, body, 0)

    source, target = one_ref, two_ref
    for done in range(1, SWEEPS + 1):
        first_tile = done * own // 8
        sweep(source, target, range(first_tile, tiles - first_tile))
        source, target = target, source

    def spread(step, carry):
        for column in range(group):
            chunk = step * group + column
            out_lanes = pl.ds(pl.multiple_of(chunk * LANES, LANES), LANES)
            for orbital in range(own):
                here = pl.ds(edge + orbital, sh.depth, stride=own)
                res_out[orbital, :, out_lanes] = res_ref[chunk, here, :]
                dir_out[orbital, :, out_lanes] = source[chunk + 1, here, :]
        return carry

    lax.fori_loop(0, sh.chunks // group, spread, 0)


def relax(sh, own, parts, ends, pieces, lo, hi, inverse):
    rows = (sh.depth + 2 * SWEEPS) * own
    scratch = pltpu.VMEM((sh.chunks, rows, LANES), jnp.float32)
    padded = pltpu.VMEM((sh.chunks + 2, rows, LANES), jnp.float32)
    out = jax.ShapeDtypeStruct((own, sh.depth, sh.plane), jnp.float32)
    vmem = pl.BlockSpec(memory_space=pltpu.VMEM)
    return pl.pallas_call(
        functools.partial(relax_kernel, sh, own, parts),
        out_shape=(out, out),
        in_specs=[pl.BlockSpec(memory_space=pltpu.SMEM)] + [vmem] * (3 + len(parts)),
        scratch_shapes=[scratch, padded, padded],
        compiler_params=params(14),
        cost_estimate=cost(10**9, 10**7),
        name="relax",
    )(ends, *pieces, lo, hi, inverse)


def to_all(value, axes):
    return lax.all_to_all(value, axes, split_axis=0, concat_axis=0, tiled=True)


def local(psi, potential, orbital_slot):
    slots, depth, plane = psi.shape
    owners = lax.axis_size("orb")
    boxes = lax.axis_size("box")
    sh = Shape(slots, depth, plane, owners)
    count = orbital_slot.shape[0]
    own = count // owners
    magic = banded(sh.box, sh.box, 0, 0, magic_weights(MTAPS), 1 - MTAPS // 2)
    kinetic = banded(sh.box, sh.box, 0, 0, second_weights(KREACH), -KREACH)
    fwd, bwd, kin = (jnp.asarray(two_part(m)) for m in (magic, magic.T, kinetic))

    upward = [(i, i + 1) for i in range(boxes - 1)]
    downward = [(i + 1, i) for i in range(boxes - 1)]
    lo = lax.ppermute(psi, "box", upward)
    hi = lax.ppermute(psi, "box", downward)
    pieces = turn(sh, to_all(pack(sh, psi), "orb"))
    c, w, kin_own = own_part(sh, psi, fwd, kin)
    w, sent = lax.optimization_barrier((w, potential))
    v_lo = lax.ppermute(sent, "box", upward)
    v_hi = lax.ppermute(sent, "box", downward)
    applied = halo_part(sh, lo, hi, c, w, kin_own, v_lo, potential, v_hi, fwd, bwd)
    applied_pieces = to_all(applied, "orb")

    slot = orbital_slot.reshape(count, 1)
    fold = max(1, LANES // count)
    devices = owners * boxes
    copies = devices if devices * count * count <= 1 << 20 else 0
    part = gram(sh, pieces, applied_pieces, slot, fold, copies)
    part = to_all(part, ("orb", "box")) if copies else lax.psum(part, ("orb", "box"))
    if sh.layered == 1 and depth > 2 * SWEEPS:
        parts = (
            tuple(range(SWEEPS)) + tuple(range(depth - SWEEPS, depth)),
            tuple(range(SWEEPS, depth - SWEEPS)),
        )
    else:
        parts = (tuple(range(sh.layers)),)
    *corrected, multipliers, inverse = correct(
        sh, pieces, applied_pieces, slot, part, fold, parts
    )
    returned = [to_all(value, "orb") for value in corrected]
    edge = SWEEPS * own
    box = lax.axis_index("box")
    from_low = lax.ppermute(
        returned[0][-sh.across :, -edge:], "box", [(i, i + 1) for i in range(boxes - 1)]
    )
    from_high = lax.ppermute(
        returned[0][: sh.across, :edge], "box", [(i + 1, i) for i in range(boxes - 1)]
    )
    ends = jnp.stack(
        [lax.axis_index("orb"), (box > 0).astype(jnp.int32), (box < boxes - 1).astype(jnp.int32)]
    ).astype(jnp.int32)
    residual, direction = relax(
        sh, own, parts, ends, returned, from_low, from_high, inverse
    )
    return (residual, direction, multipliers)


def solution(mesh):
    in_specs = (P("orb", "box", None), P("box", None), P())
    out_specs = (P("orb", "box", None), P("orb", "box", None), P())
    return jax.shard_map(local, mesh=mesh, in_specs=in_specs, out_specs=out_specs, check_vma=False)
```

```python
import functools
import math

import jax
import jax.numpy as jnp
import numpy as np
from jax import lax
from jax.experimental import pallas as pl
from jax.experimental.pallas import tpu as pltpu
from jax.sharding import PartitionSpec as P

MTAPS = 16
KREACH = 14
SWEEPS = 4
LANES = 128

highest = lax.Precision.HIGHEST
coupling_z = 4.0
coupling_xy = 1.0


def magic_weights(tap_count):
    half_len = tap_count // 2
    offsets = np.arange(1 - half_len, half_len + 1) * 1.0
    weights = np.ones(tap_count)
    for index_a in range(tap_count):
        for index_b in range(tap_count):
            if index_b != index_a:
                weights[index_a] *= (0.25 - offsets[index_b]) / (
                    offsets[index_a] - offsets[index_b]
                )
    return weights


def second_weights(reach_cells):
    factor = math.factorial(reach_cells) ** 2
    weights = np.zeros(2 * reach_cells + 1)
    for distance in range(1, reach_cells + 1):
        entry_value = (
            2.0
            * (-1) ** (distance + 1)
            * factor
            / (
                distance
                * distance
                * math.factorial(reach_cells - distance)
                * math.factorial(reach_cells + distance)
            )
        )
        weights[reach_cells + distance] = entry_value
        weights[reach_cells - distance] = entry_value
    weights[reach_cells] = -weights.sum()
    return -0.5 * weights


def banded(row_count, col_count, row_start, col_start, weights, offset_low):
    row_index = np.arange(row_count)[:, None] + row_start
    col_index = np.arange(col_count)[None, :] + col_start
    position = row_index - col_index - offset_low
    inside = (position >= 0) & (position < len(weights))
    return np.where(inside, weights[np.clip(position, 0, len(weights) - 1)], 0.0)


def f32(value):
    return float(np.float32(value))


MAGIC = {k: f32(w) for k, w in zip(range(1 - MTAPS // 2, MTAPS // 2 + 1), magic_weights(MTAPS))}
MAGIC_T = {-k: w for k, w in MAGIC.items()}
KINETIC = {
    d: f32(w) for d, w in zip(range(-KREACH, KREACH + 1), second_weights(KREACH))
}
LOW = MTAPS // 2
HIGH = MTAPS // 2 - 1


def two_part(matrix):
    width = matrix.shape[0]
    block = np.kron(np.eye(LANES // width), matrix).astype(np.float32)
    high = block.astype(jnp.bfloat16)
    low = (block - high.astype(np.float32)).astype(jnp.bfloat16)
    return np.block([[high, low], [high, np.zeros_like(low)]])


def split(value):
    high = value.astype(jnp.bfloat16)
    low = (value - high.astype(jnp.float32)).astype(jnp.bfloat16)
    return high, low


def lane_product(parts, matrix):
    both = jnp.dot(parts, matrix, preferred_element_type=jnp.float32)
    return both[:, :LANES] + both[:, LANES:]


def params(mib):
    return pltpu.CompilerParams(vmem_limit_bytes=mib << 20)


def cost(flops, bytes_accessed):
    return pl.CostEstimate(flops=flops, bytes_accessed=bytes_accessed, transcendentals=0)


class Shape:
    def __init__(self, slots, depth, plane, owners):
        self.slots, self.depth, self.plane, self.owners = slots, depth, plane, owners
        self.box = math.isqrt(plane)
        self.chunks = plane // LANES
        self.across = min(owners, self.chunks)
        self.layered = owners // self.across
        self.layers = depth // self.layered
        self.width = plane // self.across
        self.inner = self.width // LANES

    def at(self, layer, block, inner):
        piece = (layer // self.layers) * self.across + block
        lanes = slice(inner * LANES, (inner + 1) * LANES)
        return piece, layer % self.layers, slice(None), lanes


def pack_kernel(sh, psi_hbm, out_hbm, buffer, sems_in, sems_out):
    def pair(index):
        first = (index // sh.across) * sh.layers
        lane = (index % sh.across) * sh.width
        source = psi_hbm.at[:, pl.ds(first, sh.layers), pl.ds(lane, sh.width)]
        return (
            pltpu.make_async_copy(source, buffer.at[index], sems_in.at[index]),
            pltpu.make_async_copy(buffer.at[index], out_hbm.at[index], sems_out.at[index]),
        )

    copies = [pair(index) for index in range(sh.owners)]
    for arrive, leave in copies:
        arrive.start()
    for arrive, leave in copies:
        arrive.wait()
        leave.start()
    for arrive, leave in copies:
        leave.wait()


def pack(sh, psi):
    shape = (sh.owners, sh.slots, sh.layers, sh.width)
    return pl.pallas_call(
        functools.partial(pack_kernel, sh),
        out_shape=pltpu.HBM(shape, jnp.float32),
        in_specs=[pl.BlockSpec(memory_space=pltpu.HBM)],
        out_specs=pl.BlockSpec(memory_space=pltpu.HBM),
        scratch_shapes=[
            pltpu.VMEM(shape, jnp.float32),
            pltpu.SemaphoreType.DMA((sh.owners,)),
            pltpu.SemaphoreType.DMA((sh.owners,)),
        ],
        compiler_params=params(8),
        cost_estimate=cost(0, 2 * psi.size * 4),
        name="pack",
    )(pltpu.with_memory_space_constraint(psi, pltpu.HBM))


def choose_kernel(sh, slot_ref, in_ref, out_ref):
    count = slot_ref.shape[0]
    total_slots = sh.owners * sh.slots
    chosen = selection(slot_ref, count, total_slots).astype(jnp.bfloat16)
    turned = [
        jnp.transpose(in_ref[index], (1, 0, 2)) for index in range(sh.owners)
    ]
    for layer in range(sh.layers):
        high, low = split(jnp.concatenate([rows[layer] for rows in turned], 0))
        high = jnp.dot(chosen, high, preferred_element_type=jnp.float32)
        low = jnp.dot(chosen, low, preferred_element_type=jnp.float32)
        out_ref[layer, :count] = high.astype(jnp.bfloat16)
        out_ref[layer, count:] = low.astype(jnp.bfloat16)


def choose(sh, slot, pieces):
    count = slot.shape[0]
    return pl.pallas_call(
        functools.partial(choose_kernel, sh),
        out_shape=pltpu.HBM((sh.layers, 2 * count, sh.width), jnp.bfloat16),
        compiler_params=params(12),
        cost_estimate=cost(10**8, 2 * pieces.size * 4),
        name="choose",
    )(slot, pltpu.with_memory_space_constraint(pieces, pltpu.HBM))


def odd_pairs(even, lane):
    turned = [pltpu.roll(v, LANES // 2, 1) for v in even]
    zero = jnp.zeros_like(even[0])
    low = [zero] + turned
    high = turned + [zero]
    return [jnp.where(lane, a, b) for a, b in zip(low, high)]


def row_filter(even, odd, weights):
    count = len(even)
    out = []
    for b in range(count):
        total = None
        for d, w in weights.items():
            e = b + d // 2
            if d % 2 == 0:
                if not 0 <= e < count:
                    continue
                term = even[e]
            else:
                if not 0 <= e + 1 <= count:
                    continue
                term = odd[e + 1]
            total = term * w if total is None else total + term * w
        out.append(total)
    return out


def row_filter_even(even, odd, weights, reach):
    count = len(even)
    out = []
    for b in range(count):
        total = even[b] * weights[0]
        for d in range(1, reach + 1):
            if d % 2 == 0:
                places = [e for e in (b + d // 2, b - d // 2) if 0 <= e < count]
                terms = [even[e] for e in places]
            else:
                places = [e for e in (b + d // 2 + 1, b - d // 2) if 0 <= e <= count]
                terms = [odd[e] for e in places]
            if not terms:
                continue
            term = terms[0] if len(terms) == 1 else terms[0] + terms[1]
            total = total + term * weights[d]
        out.append(total)
    return out


def half_mask(slots):
    return lax.broadcasted_iota(jnp.int32, (slots, LANES), 1) < LANES // 2


def lane_pass(sh, slab, kept, matrices, targets):
    depth = sh.depth

    def body(block, carry):
        parts = []
        for inner in range(sh.inner):
            chunk = block * sh.inner + inner
            lanes = pl.ds(pl.multiple_of(chunk * LANES, LANES), LANES)
            rows = jnp.transpose(slab[:, :, lanes], (1, 0, 2))
            for layer in range(depth):
                kept[layer, chunk] = rows[layer]
            high, low = split(rows.reshape(depth * sh.slots, LANES))
            parts.append(jnp.concatenate([high, low], 1))
        parts = jnp.concatenate(parts, 0)
        for matrix, target in zip(matrices, targets):
            result = lane_product(parts, matrix[...])
            result = result.reshape(sh.inner, depth, sh.slots, LANES)
            for inner in range(sh.inner):
                for layer in range(depth):
                    target[layer, block * sh.inner + inner] = result[inner, layer]
        return carry

    lax.fori_loop(0, sh.across, body, 0)


def own_kernel(sh, psi_ref, fwd_ref, kin_ref, c_out, w_out, kin_out, x_ref):
    lane_pass(sh, psi_ref, c_out, [fwd_ref, kin_ref], [x_ref, kin_out])
    lane = half_mask(sh.slots)

    def body(layer, carry):
        even = [x_ref[layer, b] for b in range(sh.chunks)]
        for b, v in enumerate(row_filter(even, odd_pairs(even, lane), MAGIC)):
            w_out[layer, b] = v
        even = [c_out[layer, b] for b in range(sh.chunks)]
        sums = row_filter_even(even, odd_pairs(even, lane), KINETIC, KREACH)
        for b, v in enumerate(sums):
            kin_out[layer, b] += v
        return carry

    lax.fori_loop(0, sh.depth, body, 0)


def own_part(sh, psi, fwd, kin):
    full = jax.ShapeDtypeStruct((sh.depth, sh.chunks, sh.slots, LANES), jnp.float32)
    return pl.pallas_call(
        functools.partial(own_kernel, sh),
        out_shape=(full, full, full),
        scratch_shapes=[pltpu.VMEM(full.shape, jnp.float32)],
        compiler_params=params(14),
        cost_estimate=cost(10 * 10**9, 10**7),
        name="own_part",
    )(psi, fwd, kin)


def side_kernel(
    sh, lo_hbm, hi_hbm, fwd_ref, clo_ref, chi_ref, wlo_ref, whi_ref, lo_ref, hi_ref, x_ref, sems
):
    lane = half_mask(sh.slots)
    reach = sh.depth - 1
    arrivals = [
        pltpu.make_async_copy(lo_hbm, lo_ref, sems.at[0]),
        pltpu.make_async_copy(hi_hbm, hi_ref, sems.at[1]),
    ]
    for copy in arrivals:
        copy.start()
    for copy, side_ref, kept, target, first in (
        (arrivals[0], lo_ref, clo_ref, wlo_ref, 1),
        (arrivals[1], hi_ref, chi_ref, whi_ref, 0),
    ):
        copy.wait()
        lane_pass(sh, side_ref, kept, [fwd_ref], [x_ref])

        def filter_rows(layer, carry):
            even = [x_ref[layer, b] for b in range(sh.chunks)]
            for b, v in enumerate(row_filter(even, odd_pairs(even, lane), MAGIC)):
                target[layer, b] = v
            return carry

        lax.fori_loop(first, first + reach, filter_rows, 0)


def side_part(sh, lo, hi, fwd):
    full = (sh.depth, sh.chunks, sh.slots, LANES)
    hbm = pl.BlockSpec(memory_space=pltpu.HBM)
    lo, hi = (pltpu.with_memory_space_constraint(x, pltpu.HBM) for x in (lo, hi))
    return pl.pallas_call(
        functools.partial(side_kernel, sh),
        out_shape=(jax.ShapeDtypeStruct(full, jnp.float32),) * 4,
        in_specs=[hbm] * 2 + [pl.BlockSpec(memory_space=pltpu.VMEM)],
        scratch_shapes=[pltpu.VMEM(lo.shape, jnp.float32)] * 2
        + [pltpu.VMEM(full, jnp.float32), pltpu.SemaphoreType.DMA((2,))],
        compiler_params=params(12),
        cost_estimate=cost(10 * 10**9, 10**7),
        name="side_part",
    )(lo, hi, fwd)


def halo_kernel(
    sh, c_ref, w_ref, kin_ref, clo_ref, chi_ref, wlo_ref, whi_ref, vlo_ref, v_ref, vhi_ref,
    bwd_ref, out_hbm, x_ref, y_ref, kz_ref, out_ref, sems,
):
    lane = half_mask(sh.slots)
    depth = sh.depth

    def along_z(chunk, carry):
        lanes = pl.ds(pl.multiple_of(chunk * LANES, LANES), LANES)

        def pick(below, here, above, z):
            ref = below if z < 0 else (here if z < depth else above)
            return ref[z % depth, chunk]

        def level(z):
            ref = vlo_ref if z < 0 else (v_ref if z < depth else vhi_ref)
            return jnp.broadcast_to(ref[z % depth : z % depth + 1, lanes], (sh.slots, LANES))

        values = {
            z: pick(wlo_ref, w_ref, whi_ref, z) for z in range(-LOW - HIGH, depth + LOW + HIGH)
        }
        grid = {}
        for p in range(-LOW, depth + HIGH):
            total = None
            for k, w in MAGIC.items():
                term = values[p + k] * w
                total = term if total is None else total + term
            grid[p] = total * level(p)
        for q in range(depth):
            total = None
            for k, w in MAGIC.items():
                term = grid[q - k] * w
                total = term if total is None else total + term
            x_ref[q, chunk] = total
        cs = {z: pick(clo_ref, c_ref, chi_ref, z) for z in range(-KREACH, depth + KREACH)}
        for q in range(depth):
            total = kin_ref[q, chunk] + cs[q] * KINETIC[0]
            for d in range(1, KREACH + 1):
                total = total + (cs[q + d] + cs[q - d]) * KINETIC[d]
            kz_ref[q, chunk] = total
        return carry

    lax.fori_loop(0, sh.chunks, along_z, 0)

    def filter_back(layer, carry):
        even = [x_ref[layer, b] for b in range(sh.chunks)]
        for b, v in enumerate(row_filter(even, odd_pairs(even, lane), MAGIC_T)):
            y_ref[layer, b] = v
        return carry

    lax.fori_loop(0, depth, filter_back, 0)

    def piece(index):
        return pltpu.make_async_copy(out_ref.at[index], out_hbm.at[index], sems.at[index])

    def finish(block, carry):
        parts = []
        for inner in range(sh.inner):
            chunk = block * sh.inner + inner
            rows = jnp.concatenate([y_ref[layer, chunk] for layer in range(depth)], 0)
            high, low = split(rows)
            parts.append(jnp.concatenate([high, low], 1))
        result = lane_product(jnp.concatenate(parts, 0), bwd_ref[...])
        result = result.reshape(sh.inner, depth, sh.slots, LANES)
        for inner in range(sh.inner):
            chunk = block * sh.inner + inner
            for layer in range(depth):
                out_ref[sh.at(layer, block, inner)] = result[inner, layer] + kz_ref[layer, chunk]
        for group in range(sh.layered):
            piece(group * sh.across + block).start()
        return carry

    lax.fori_loop(0, sh.across, finish, 0)
    for index in range(sh.owners):
        piece(index).wait()


def halo_part(sh, own, sides, v_lo, v, v_hi, bwd):
    full = pltpu.VMEM((sh.depth, sh.chunks, sh.slots, LANES), jnp.float32)
    out = (sh.owners, sh.layers, sh.slots, sh.width)
    return pl.pallas_call(
        functools.partial(halo_kernel, sh),
        out_shape=pltpu.HBM(out, jnp.float32),
        in_specs=[pl.BlockSpec(memory_space=pltpu.VMEM)] * 11,
        out_specs=pl.BlockSpec(memory_space=pltpu.HBM),
        scratch_shapes=[full] * 3
        + [pltpu.VMEM(out, jnp.float32), pltpu.SemaphoreType.DMA((sh.owners,))],
        compiler_params=params(14),
        cost_estimate=cost(20 * 10**9, 10**7),
        name="halo_part",
    )(*own, *sides, v_lo, v, v_hi, bwd)


def selection(slot_ref, count, slots_all):
    column = lax.broadcasted_iota(jnp.int32, (count, slots_all), 1)
    return (column == slot_ref[...]).astype(jnp.float32)


def packed_rows(matrix, fold):
    rows = matrix.shape[0] // fold
    return jnp.concatenate([matrix[i * rows : (i + 1) * rows] for i in range(fold)], 1)


def unpacked_rows(matrix, fold):
    cols = matrix.shape[1] // fold
    return jnp.concatenate([matrix[:, i * cols : (i + 1) * cols] for i in range(fold)], 0)


def gram_kernel(sh, fold, c_hbm, a_ref, slot_ref, out_ref, c_ref, sem):
    copy = pltpu.make_async_copy(c_hbm, c_ref, sem)
    copy.start()
    total_slots = sh.owners * sh.slots
    count = slot_ref.shape[0]
    chosen = selection(slot_ref, count, total_slots)
    both = jnp.zeros((2 * count, 2 * total_slots), jnp.float32)
    copy.wait()
    for layer in range(sh.layers):
        rows = a_ref[:, layer].reshape(total_slots, sh.width)
        both = both + lax.dot_general(
            c_ref[layer],
            jnp.concatenate(split(rows), 0),
            (((1,), (1,)), ((), ())),
            preferred_element_type=jnp.float32,
        )
    wide = both[:count] + both[count:]
    rows = wide[:, :total_slots] + wide[:, total_slots:]
    picked = lax.dot_general(
        rows, chosen, (((1,), (1,)), ((), ())), precision=highest,
        preferred_element_type=jnp.float32,
    ) * (1.0 / sh.box**3)
    picked = packed_rows(picked, fold)
    if len(out_ref.shape) == 2:
        out_ref[...] = picked
    else:
        out_ref[...] = jnp.broadcast_to(picked[None], out_ref.shape)


def gram(sh, c, a, slot, fold, copies):
    count = slot.shape[0]
    shape = (count // fold, count * fold)
    if copies:
        shape = (copies,) + shape
    return pl.pallas_call(
        functools.partial(gram_kernel, sh, fold),
        out_shape=(jax.ShapeDtypeStruct(shape, jnp.float32), pltpu.VMEM(c.shape, c.dtype)),
        in_specs=[pl.BlockSpec(memory_space=pltpu.HBM)]
        + [pl.BlockSpec(memory_space=pltpu.VMEM)] * 2,
        scratch_shapes=[pltpu.SemaphoreType.DMA],
        compiler_params=params(16),
        cost_estimate=cost(10**9, 10**7),
        name="gram",
    )(pltpu.with_memory_space_constraint(c, pltpu.HBM), a, slot)


def correct_kernel(sh, fold, own, parts, c_ref, a_ref, slot_ref, part_ref, *outs):
    *out_refs, mult_ref, inv_ref = outs
    total_slots = sh.owners * sh.slots
    count = slot_ref.shape[0]
    packed = part_ref[...]
    if packed.ndim == 3:
        packed = packed.sum(0)
    multipliers = unpacked_rows(packed, fold)
    mult_ref[...] = multipliers
    row = lax.broadcasted_iota(jnp.int32, (count, count), 0)
    col = lax.broadcasted_iota(jnp.int32, (count, count), 1)
    diagonal = jnp.sum(jnp.where(row == col, multipliers, 0.0), axis=1, keepdims=True)
    denominator = 2.0 * coupling_z + 4.0 * coupling_xy + 1.0 + jnp.abs(diagonal)
    inv_ref[...] = jnp.broadcast_to(1.0 / denominator, (count, LANES))
    chosen = selection(slot_ref, count, total_slots)
    high, low = split(-multipliers.T)
    chosen = chosen.astype(jnp.bfloat16)
    weights = jnp.concatenate(
        [
            jnp.concatenate([chosen, chosen, high, high], 1),
            jnp.concatenate(
                [jnp.zeros((count, 2 * total_slots), jnp.bfloat16), low, jnp.zeros_like(low)], 1
            ),
        ],
        0,
    )

    def body(layer, place, out_ref):
        rows = split(a_ref[:, layer].reshape(total_slots, sh.width))
        data = jnp.concatenate([rows[0], rows[1], c_ref[layer]], 0)
        both = jnp.dot(weights, data, preferred_element_type=jnp.float32)
        result = both[:count] + both[count:]
        for owner in range(sh.owners):
            out_ref[owner, place * own : (place + 1) * own] = result[
                owner * own : (owner + 1) * own
            ]

    for part, out_ref in zip(parts, out_refs):
        for place, layer in enumerate(part):
            body(layer, place, out_ref)


def correct(sh, c, a, slot, part, fold, parts):
    count = slot.shape[0]
    own = count // sh.owners
    return pl.pallas_call(
        functools.partial(correct_kernel, sh, fold, own, parts),
        out_shape=tuple(
            jax.ShapeDtypeStruct((sh.owners, len(layers) * own, sh.width), jnp.float32)
            for layers in parts
        )
        + (
            jax.ShapeDtypeStruct((count, count), jnp.float32),
            jax.ShapeDtypeStruct((count, LANES), jnp.float32),
        ),
        compiler_params=params(16),
        cost_estimate=cost(10**9, 10**7),
        name="correct",
    )(c, a, slot, part)


def relax_kernel(sh, own, parts, ends_ref, *refs):
    r_refs = refs[: len(parts)]
    lo_ref, hi_ref, inv_ref, res_hbm, dir_hbm, *refs = refs[len(parts) :]
    res_ref, one_ref, two_ref, res_out, dir_out, sems = refs
    places = {layer: (ref, i) for part, ref in zip(parts, r_refs) for i, layer in enumerate(part)}
    rows = sh.depth * own
    edge = SWEEPS * own
    first = pl.multiple_of(ends_ref[0] * own, own)
    inverse = inv_ref[pl.ds(first, own), :]
    inverse = jnp.concatenate([inverse] * (8 // own), 0)
    keep_lo = inverse * ends_ref[1].astype(jnp.float32)
    keep_hi = inverse * ends_ref[2].astype(jnp.float32)
    tiles = (rows + 2 * edge) // 8
    edge_tiles = edge // 8

    def scale(tile):
        if tile < edge_tiles:
            return keep_lo
        return keep_hi if tile >= tiles - edge_tiles else inverse

    group = min(16, sh.chunks)
    blank = jnp.zeros((rows + 2 * edge, LANES), jnp.float32)
    for ref in (one_ref, two_ref):
        ref[0] = blank
        ref[sh.chunks + 1] = blank

    def leave(source, target, kind, step, width):
        lanes = pl.ds(pl.multiple_of(step * width, LANES), width)
        return pltpu.make_async_copy(
            source.at[:, :, lanes], target.at[:, :, lanes], sems.at[kind, step]
        )

    def gather(block, carry):
        for inner in range(sh.inner):
            chunk = block * sh.inner + inner
            lanes = slice(inner * LANES, (inner + 1) * LANES)
            pieces = [lo_ref[block, :, lanes]]
            for g in range(sh.layered):
                for layer in range(sh.layers):
                    ref, i = places[layer]
                    pieces.append(ref[g * sh.across + block, i * own : (i + 1) * own, lanes])
            pieces += [hi_ref[block, :, lanes]]
            column = jnp.concatenate(pieces, 0)
            for tile in range(tiles):
                value = column[tile * 8 : (tile + 1) * 8]
                res_ref[chunk, tile * 8 : (tile + 1) * 8] = value
                one_ref[chunk + 1, tile * 8 : (tile + 1) * 8] = value * scale(tile)
            out_lanes = pl.ds(pl.multiple_of(chunk * LANES, LANES), LANES)
            for orbital in range(own):
                here = pl.ds(edge + orbital, sh.depth, stride=own)
                res_out[orbital, :, out_lanes] = res_ref[chunk, here, :]
        leave(res_out, res_hbm, 0, block, sh.width).start()
        return carry

    lax.fori_loop(0, sh.across, gather, 0)

    sub = lax.broadcasted_iota(jnp.int32, (8, LANES), 0)
    lane = lax.broadcasted_iota(jnp.int32, (8, LANES), 1)
    upper = sub >= own
    right_half = lane >= LANES // 2
    not_last = (lane % sh.box) != sh.box - 1
    not_first = (lane % sh.box) != 0
    assert 8 // own == 2

    def sweep(source, target, tile_list):
        def body(step, carry):
            seen = {}

            def value_at(column, tile):
                if not 0 <= tile < tiles:
                    return jnp.zeros((8, LANES), jnp.float32)
                if (column, tile) not in seen:
                    seen[column, tile] = source[step * group + column + 1, pl.ds(tile * 8, 8)]
                return seen[column, tile]

            for column in range(group):
                for tile in tile_list:
                    here = pl.ds(tile * 8, 8)
                    value = value_at(column, tile)
                    beside = jnp.where(
                        upper, value_at(column, tile - 1), value_at(column, tile + 1)
                    )
                    along_z = pltpu.roll(value + beside, own, 0)
                    beside = jnp.where(
                        right_half, value_at(column - 1, tile), value_at(column + 1, tile)
                    )
                    along_y = pltpu.roll(value + beside, LANES // 2, 1)
                    along_x = pltpu.roll(jnp.where(not_last, value, 0.0), 1, 1) + pltpu.roll(
                        jnp.where(not_first, value, 0.0), LANES - 1, 1
                    )
                    total = (
                        res_ref[step * group + column, here]
                        + coupling_xy * (along_y + along_x)
                        + coupling_z * along_z
                    )
                    target[step * group + column + 1, here] = total * scale(tile)
            return carry

        lax.fori_loop(0, sh.chunks // group, body, 0)

    source, target = one_ref, two_ref
    for done in range(1, SWEEPS + 1):
        first_tile = done * own // 8
        sweep(source, target, range(first_tile, tiles - first_tile))
        source, target = target, source

    def spread(step, carry):
        for column in range(group):
            chunk = step * group + column
            out_lanes = pl.ds(pl.multiple_of(chunk * LANES, LANES), LANES)
            for orbital in range(own):
                here = pl.ds(edge + orbital, sh.depth, stride=own)
                dir_out[orbital, :, out_lanes] = source[chunk + 1, here, :]
        leave(dir_out, dir_hbm, 1, step, group * LANES).start()
        return carry

    lax.fori_loop(0, sh.chunks // group, spread, 0)
    for block in range(sh.across):
        leave(res_out, res_hbm, 0, block, sh.width).wait()
    for step in range(sh.chunks // group):
        leave(dir_out, dir_hbm, 1, step, group * LANES).wait()


def relax(sh, own, parts, ends, pieces, lo, hi, inverse):
    rows = (sh.depth + 2 * SWEEPS) * own
    scratch = pltpu.VMEM((sh.chunks, rows, LANES), jnp.float32)
    padded = pltpu.VMEM((sh.chunks + 2, rows, LANES), jnp.float32)
    out = (own, sh.depth, sh.plane)
    hbm = pl.BlockSpec(memory_space=pltpu.HBM)
    vmem = pl.BlockSpec(memory_space=pltpu.VMEM)
    return pl.pallas_call(
        functools.partial(relax_kernel, sh, own, parts),
        out_shape=(pltpu.HBM(out, jnp.float32),) * 2,
        out_specs=(hbm, hbm),
        in_specs=[pl.BlockSpec(memory_space=pltpu.SMEM)] + [vmem] * (3 + len(parts)),
        scratch_shapes=[scratch, padded, padded]
        + [pltpu.VMEM(out, jnp.float32)] * 2
        + [pltpu.SemaphoreType.DMA((2, max(sh.across, sh.chunks)))],
        compiler_params=params(14),
        cost_estimate=cost(10**9, 10**7),
        name="relax",
    )(ends, *pieces, lo, hi, inverse)


def to_all(value, axes):
    return lax.all_to_all(value, axes, split_axis=0, concat_axis=0, tiled=True)


def local(psi, potential, orbital_slot):
    slots, depth, plane = psi.shape
    owners = lax.axis_size("orb")
    boxes = lax.axis_size("box")
    sh = Shape(slots, depth, plane, owners)
    count = orbital_slot.shape[0]
    own = count // owners
    magic = banded(sh.box, sh.box, 0, 0, magic_weights(MTAPS), 1 - MTAPS // 2)
    kinetic = banded(sh.box, sh.box, 0, 0, second_weights(KREACH), -KREACH)
    fwd, bwd, kin = (jnp.asarray(two_part(m)) for m in (magic, magic.T, kinetic))

    upward = [(i, i + 1) for i in range(boxes - 1)]
    downward = [(i + 1, i) for i in range(boxes - 1)]
    lo = lax.ppermute(psi, "box", upward)
    hi = lax.ppermute(psi, "box", downward)
    slot = orbital_slot.reshape(count, 1)
    pieces = choose(sh, slot, to_all(pack(sh, psi), "orb"))
    c, w, kin_own = own_part(sh, psi, fwd, kin)
    w, sent = lax.optimization_barrier((w, potential))
    v_lo = lax.ppermute(sent, "box", upward)
    v_hi = lax.ppermute(sent, "box", downward)
    sides = side_part(sh, lo, hi, fwd)
    applied = halo_part(sh, (c, w, kin_own), sides, v_lo, potential, v_hi, bwd)
    applied_pieces = to_all(applied, "orb")

    fold = max(1, LANES // count)
    devices = owners * boxes
    copies = devices if devices * count * count <= 1 << 20 else 0
    part, pieces = gram(sh, pieces, applied_pieces, slot, fold, copies)
    part = to_all(part, ("orb", "box")) if copies else lax.psum(part, ("orb", "box"))
    if sh.layered == 1 and depth > 2 * SWEEPS:
        parts = (
            tuple(range(SWEEPS)) + tuple(range(depth - SWEEPS, depth)),
            tuple(range(SWEEPS, depth - SWEEPS)),
        )
    else:
        parts = (tuple(range(sh.layers)),)
    *corrected, multipliers, inverse = correct(
        sh, pieces, applied_pieces, slot, part, fold, parts
    )
    returned = [to_all(value, "orb") for value in corrected]
    edge = SWEEPS * own
    box = lax.axis_index("box")
    from_low = lax.ppermute(
        returned[0][-sh.across :, -edge:], "box", [(i, i + 1) for i in range(boxes - 1)]
    )
    from_high = lax.ppermute(
        returned[0][: sh.across, :edge], "box", [(i + 1, i) for i in range(boxes - 1)]
    )
    ends = jnp.stack(
        [lax.axis_index("orb"), (box > 0).astype(jnp.int32), (box < boxes - 1).astype(jnp.int32)]
    ).astype(jnp.int32)
    residual, direction = relax(
        sh, own, parts, ends, returned, from_low, from_high, inverse
    )
    return (residual, direction, multipliers)


def solution(mesh):
    in_specs = (P("orb", "box", None), P("box", None), P())
    out_specs = (P("orb", "box", None), P("orb", "box", None), P())
    return jax.shard_map(local, mesh=mesh, in_specs=in_specs, out_specs=out_specs, check_vma=False)
```

```python
import functools
import math

import jax
import jax.numpy as jnp
import numpy as np
from jax import lax
from jax.experimental import pallas as pl
from jax.experimental.pallas import tpu as pltpu
from jax.sharding import PartitionSpec as P


MTAPS = 16
KREACH = 14
SWEEPS = 4
LANES = 128

highest = lax.Precision.HIGHEST
coupling_z = 4.0
coupling_xy = 1.0


def magic_weights(tap_count):
    half_len = tap_count // 2
    offsets = np.arange(1 - half_len, half_len + 1) * 1.0
    weights = np.ones(tap_count)
    for index_a in range(tap_count):
        for index_b in range(tap_count):
            if index_b != index_a:
                weights[index_a] *= (0.25 - offsets[index_b]) / (
                    offsets[index_a] - offsets[index_b]
                )
    return weights


def second_weights(reach_cells):
    factor = math.factorial(reach_cells) ** 2
    weights = np.zeros(2 * reach_cells + 1)
    for distance in range(1, reach_cells + 1):
        entry_value = (
            2.0
            * (-1) ** (distance + 1)
            * factor
            / (
                distance
                * distance
                * math.factorial(reach_cells - distance)
                * math.factorial(reach_cells + distance)
            )
        )
        weights[reach_cells + distance] = entry_value
        weights[reach_cells - distance] = entry_value
    weights[reach_cells] = -weights.sum()
    return -0.5 * weights


def banded(row_count, col_count, row_start, col_start, weights, offset_low):
    row_index = np.arange(row_count)[:, None] + row_start
    col_index = np.arange(col_count)[None, :] + col_start
    position = row_index - col_index - offset_low
    inside = (position >= 0) & (position < len(weights))
    return np.where(inside, weights[np.clip(position, 0, len(weights) - 1)], 0.0)


def f32(value):
    return float(np.float32(value))


MAGIC = {k: f32(w) for k, w in zip(range(1 - MTAPS // 2, MTAPS // 2 + 1), magic_weights(MTAPS))}
MAGIC_T = {-k: w for k, w in MAGIC.items()}
KINETIC = {
    d: f32(w) for d, w in zip(range(-KREACH, KREACH + 1), second_weights(KREACH))
}
LOW = MTAPS // 2
HIGH = MTAPS // 2 - 1


def two_part(matrix):
    width = matrix.shape[0]
    block = np.kron(np.eye(LANES // width), matrix).astype(np.float32)
    high = block.astype(jnp.bfloat16)
    low = (block - high.astype(np.float32)).astype(jnp.bfloat16)
    return np.block([[high, low], [high, np.zeros_like(low)]])


def split(value):
    high = value.astype(jnp.bfloat16)
    low = (value - high.astype(jnp.float32)).astype(jnp.bfloat16)
    return high, low


def lane_product(parts, matrix):
    both = jnp.dot(parts, matrix, preferred_element_type=jnp.float32)
    return both[:, :LANES] + both[:, LANES:]


def params(mib):
    return pltpu.CompilerParams(vmem_limit_bytes=mib << 20)


def cost(flops, bytes_accessed):
    return pl.CostEstimate(flops=flops, bytes_accessed=bytes_accessed, transcendentals=0)


class Shape:
    def __init__(self, slots, depth, plane, owners):
        self.slots, self.depth, self.plane, self.owners = slots, depth, plane, owners
        self.box = math.isqrt(plane)
        self.chunks = plane // LANES
        self.across = min(owners, self.chunks)
        self.layered = owners // self.across
        self.layers = depth // self.layered
        self.width = plane // self.across
        self.inner = self.width // LANES

    def at(self, layer, block, inner):
        piece = (layer // self.layers) * self.across + block
        lanes = slice(inner * LANES, (inner + 1) * LANES)
        return piece, layer % self.layers, slice(None), lanes


def pack_kernel(sh, psi_hbm, out_hbm, buffer, sems_in, sems_out):
    def pair(index):
        first = (index // sh.across) * sh.layers
        lane = (index % sh.across) * sh.width
        source = psi_hbm.at[:, pl.ds(first, sh.layers), pl.ds(lane, sh.width)]
        return (
            pltpu.make_async_copy(source, buffer.at[index], sems_in.at[index]),
            pltpu.make_async_copy(buffer.at[index], out_hbm.at[index], sems_out.at[index]),
        )

    copies = [pair(index) for index in range(sh.owners)]
    for arrive, leave in copies:
        arrive.start()
    for arrive, leave in copies:
        arrive.wait()
        leave.start()
    for arrive, leave in copies:
        leave.wait()


def pack(sh, psi):
    shape = (sh.owners, sh.slots, sh.layers, sh.width)
    return pl.pallas_call(
        functools.partial(pack_kernel, sh),
        out_shape=pltpu.HBM(shape, jnp.float32),
        in_specs=[pl.BlockSpec(memory_space=pltpu.HBM)],
        out_specs=pl.BlockSpec(memory_space=pltpu.HBM),
        scratch_shapes=[
            pltpu.VMEM(shape, jnp.float32),
            pltpu.SemaphoreType.DMA((sh.owners,)),
            pltpu.SemaphoreType.DMA((sh.owners,)),
        ],
        compiler_params=params(8),
        cost_estimate=cost(0, 2 * psi.size * 4),
        name="pack",
    )(pltpu.with_memory_space_constraint(psi, pltpu.HBM))


def choose_kernel(sh, slot_ref, in_ref, out_ref):
    count = slot_ref.shape[0]
    total_slots = sh.owners * sh.slots
    chosen = selection(slot_ref, count, total_slots).astype(jnp.bfloat16)
    turned = [
        jnp.transpose(in_ref[index], (1, 0, 2)) for index in range(sh.owners)
    ]
    for layer in range(sh.layers):
        high, low = split(jnp.concatenate([rows[layer] for rows in turned], 0))
        high = jnp.dot(chosen, high, preferred_element_type=jnp.float32)
        low = jnp.dot(chosen, low, preferred_element_type=jnp.float32)
        out_ref[layer, :count] = high.astype(jnp.bfloat16)
        out_ref[layer, count:] = low.astype(jnp.bfloat16)


def choose(sh, slot, pieces):
    count = slot.shape[0]
    return pl.pallas_call(
        functools.partial(choose_kernel, sh),
        out_shape=pltpu.HBM((sh.layers, 2 * count, sh.width), jnp.bfloat16),
        compiler_params=params(12),
        cost_estimate=cost(10**8, 2 * pieces.size * 4),
        name="choose",
    )(slot, pltpu.with_memory_space_constraint(pieces, pltpu.HBM))


def odd_pairs(even, lane):
    turned = [pltpu.roll(v, LANES // 2, 1) for v in even]
    zero = jnp.zeros_like(even[0])
    low = [zero] + turned
    high = turned + [zero]
    return [jnp.where(lane, a, b) for a, b in zip(low, high)]


def row_filter(even, odd, weights):
    count = len(even)
    out = []
    for b in range(count):
        total = None
        for d, w in weights.items():
            e = b + d // 2
            if d % 2 == 0:
                if not 0 <= e < count:
                    continue
                term = even[e]
            else:
                if not 0 <= e + 1 <= count:
                    continue
                term = odd[e + 1]
            total = term * w if total is None else total + term * w
        out.append(total)
    return out


def row_filter_even(even, odd, weights, reach):
    count = len(even)
    out = []
    for b in range(count):
        total = even[b] * weights[0]
        for d in range(1, reach + 1):
            if d % 2 == 0:
                places = [e for e in (b + d // 2, b - d // 2) if 0 <= e < count]
                terms = [even[e] for e in places]
            else:
                places = [e for e in (b + d // 2 + 1, b - d // 2) if 0 <= e <= count]
                terms = [odd[e] for e in places]
            if not terms:
                continue
            term = terms[0] if len(terms) == 1 else terms[0] + terms[1]
            total = total + term * weights[d]
        out.append(total)
    return out


def half_mask(slots):
    return lax.broadcasted_iota(jnp.int32, (slots, LANES), 1) < LANES // 2


def lane_pass(sh, slab, kept, matrices, targets):
    depth = sh.depth

    def body(block, carry):
        parts = []
        for inner in range(sh.inner):
            chunk = block * sh.inner + inner
            lanes = pl.ds(pl.multiple_of(chunk * LANES, LANES), LANES)
            rows = jnp.transpose(slab[:, :, lanes], (1, 0, 2))
            for layer in range(depth):
                kept[layer, chunk] = rows[layer]
            high, low = split(rows.reshape(depth * sh.slots, LANES))
            parts.append(jnp.concatenate([high, low], 1))
        parts = jnp.concatenate(parts, 0)
        for matrix, target in zip(matrices, targets):
            result = lane_product(parts, matrix[...])
            result = result.reshape(sh.inner, depth, sh.slots, LANES)
            for inner in range(sh.inner):
                for layer in range(depth):
                    target[layer, block * sh.inner + inner] = result[inner, layer]
        return carry

    lax.fori_loop(0, sh.across, body, 0)


def own_kernel(sh, psi_ref, fwd_ref, kin_ref, c_out, w_out, kin_out, x_ref):
    lane_pass(sh, psi_ref, c_out, [fwd_ref, kin_ref], [x_ref, kin_out])
    lane = half_mask(sh.slots)

    def body(layer, carry):
        even = [x_ref[layer, b] for b in range(sh.chunks)]
        for b, v in enumerate(row_filter(even, odd_pairs(even, lane), MAGIC)):
            w_out[layer, b] = v
        even = [c_out[layer, b] for b in range(sh.chunks)]
        sums = row_filter_even(even, odd_pairs(even, lane), KINETIC, KREACH)
        for b, v in enumerate(sums):
            kin_out[layer, b] += v
        return carry

    lax.fori_loop(0, sh.depth, body, 0)


def own_part(sh, psi, fwd, kin):
    full = jax.ShapeDtypeStruct((sh.depth, sh.chunks, sh.slots, LANES), jnp.float32)
    return pl.pallas_call(
        functools.partial(own_kernel, sh),
        out_shape=(full, full, full),
        scratch_shapes=[pltpu.VMEM(full.shape, jnp.float32)],
        compiler_params=params(14),
        cost_estimate=cost(10 * 10**9, 10**7),
        name="own_part",
    )(psi, fwd, kin)


def side_kernel(
    sh, far_hbm, near_hbm, fwd_ref, clo_ref, chi_ref, wlo_ref, whi_ref, lo_ref, hi_ref,
    x_ref, sems,
):
    lane = half_mask(sh.slots)
    reach = sh.depth - 1

    def bring(source_lo, source_hi):
        pltpu.make_async_copy(source_lo, lo_ref, sems.at[0]).start()
        pltpu.make_async_copy(source_hi, hi_ref, sems.at[1]).start()

    @pl.when(lax.rem(lax.axis_index("box"), 2) == 0)
    def _():
        bring(far_hbm, near_hbm)

    @pl.when(lax.rem(lax.axis_index("box"), 2) != 0)
    def _():
        bring(near_hbm, far_hbm)

    arrivals = [
        pltpu.make_async_copy(far_hbm, lo_ref, sems.at[0]),
        pltpu.make_async_copy(near_hbm, hi_ref, sems.at[1]),
    ]
    for copy, side_ref, kept, target, first in (
        (arrivals[0], lo_ref, clo_ref, wlo_ref, 1),
        (arrivals[1], hi_ref, chi_ref, whi_ref, 0),
    ):
        copy.wait()
        lane_pass(sh, side_ref, kept, [fwd_ref], [x_ref])

        def filter_rows(layer, carry):
            even = [x_ref[layer, b] for b in range(sh.chunks)]
            for b, v in enumerate(row_filter(even, odd_pairs(even, lane), MAGIC)):
                target[layer, b] = v
            return carry

        lax.fori_loop(first, first + reach, filter_rows, 0)


def side_part(sh, far, near, fwd):
    full = (sh.depth, sh.chunks, sh.slots, LANES)
    return pl.pallas_call(
        functools.partial(side_kernel, sh),
        out_shape=(jax.ShapeDtypeStruct(full, jnp.float32),) * 4,
        in_specs=[pl.BlockSpec(memory_space=pl.ANY)] * 2
        + [pl.BlockSpec(memory_space=pltpu.VMEM)],
        scratch_shapes=[pltpu.VMEM(far.shape, jnp.float32)] * 2
        + [pltpu.VMEM(full, jnp.float32), pltpu.SemaphoreType.DMA((2,))],
        compiler_params=params(12),
        cost_estimate=cost(10 * 10**9, 10**7),
        name="side_part",
    )(far, near, fwd)


def halo_kernel(
    sh, c_ref, w_ref, kin_ref, clo_ref, chi_ref, wlo_ref, whi_ref, vfar_ref, v_ref,
    vnear_ref, bwd_ref, out_hbm, x_ref, y_ref, kz_ref, vlo_ref, vhi_ref, out_ref, sems,
):
    lane = half_mask(sh.slots)
    depth = sh.depth
    even = lax.rem(lax.axis_index("box"), 2) == 0
    vlo_ref[...] = jnp.where(even, vfar_ref[...], vnear_ref[...])
    vhi_ref[...] = jnp.where(even, vnear_ref[...], vfar_ref[...])

    def along_z(chunk, carry):
        lanes = pl.ds(pl.multiple_of(chunk * LANES, LANES), LANES)

        def pick(below, here, above, z):
            ref = below if z < 0 else (here if z < depth else above)
            return ref[z % depth, chunk]

        def level(z):
            ref = vlo_ref if z < 0 else (v_ref if z < depth else vhi_ref)
            return jnp.broadcast_to(ref[z % depth : z % depth + 1, lanes], (sh.slots, LANES))

        values = {
            z: pick(wlo_ref, w_ref, whi_ref, z) for z in range(-LOW - HIGH, depth + LOW + HIGH)
        }
        grid = {}
        for p in range(-LOW, depth + HIGH):
            total = None
            for k, w in MAGIC.items():
                term = values[p + k] * w
                total = term if total is None else total + term
            grid[p] = total * level(p)
        for q in range(depth):
            total = None
            for k, w in MAGIC.items():
                term = grid[q - k] * w
                total = term if total is None else total + term
            x_ref[q, chunk] = total
        cs = {z: pick(clo_ref, c_ref, chi_ref, z) for z in range(-KREACH, depth + KREACH)}
        for q in range(depth):
            total = kin_ref[q, chunk] + cs[q] * KINETIC[0]
            for d in range(1, KREACH + 1):
                total = total + (cs[q + d] + cs[q - d]) * KINETIC[d]
            kz_ref[q, chunk] = total
        return carry

    lax.fori_loop(0, sh.chunks, along_z, 0)

    def filter_back(layer, carry):
        even = [x_ref[layer, b] for b in range(sh.chunks)]
        for b, v in enumerate(row_filter(even, odd_pairs(even, lane), MAGIC_T)):
            y_ref[layer, b] = v
        return carry

    lax.fori_loop(0, depth, filter_back, 0)

    def piece(index):
        return pltpu.make_async_copy(out_ref.at[index], out_hbm.at[index], sems.at[index])

    def finish(block, carry):
        parts = []
        for inner in range(sh.inner):
            chunk = block * sh.inner + inner
            rows = jnp.concatenate([y_ref[layer, chunk] for layer in range(depth)], 0)
            high, low = split(rows)
            parts.append(jnp.concatenate([high, low], 1))
        result = lane_product(jnp.concatenate(parts, 0), bwd_ref[...])
        result = result.reshape(sh.inner, depth, sh.slots, LANES)
        for inner in range(sh.inner):
            chunk = block * sh.inner + inner
            for layer in range(depth):
                out_ref[sh.at(layer, block, inner)] = result[inner, layer] + kz_ref[layer, chunk]
        for group in range(sh.layered):
            piece(group * sh.across + block).start()
        return carry

    lax.fori_loop(0, sh.across, finish, 0)
    for index in range(sh.owners):
        piece(index).wait()


def halo_part(sh, own, sides, v_far, v, v_near, bwd):
    full = pltpu.VMEM((sh.depth, sh.chunks, sh.slots, LANES), jnp.float32)
    out = (sh.owners, sh.layers, sh.slots, sh.width)
    return pl.pallas_call(
        functools.partial(halo_kernel, sh),
        out_shape=pltpu.HBM(out, jnp.float32),
        in_specs=[pl.BlockSpec(memory_space=pltpu.VMEM)] * 11,
        out_specs=pl.BlockSpec(memory_space=pltpu.HBM),
        scratch_shapes=[full] * 3
        + [pltpu.VMEM(v.shape, jnp.float32)] * 2
        + [pltpu.VMEM(out, jnp.float32), pltpu.SemaphoreType.DMA((sh.owners,))],
        compiler_params=params(14),
        cost_estimate=cost(20 * 10**9, 10**7),
        name="halo_part",
    )(*own, *sides, v_far, v, v_near, bwd)


def selection(slot_ref, count, slots_all):
    column = lax.broadcasted_iota(jnp.int32, (count, slots_all), 1)
    return (column == slot_ref[...]).astype(jnp.float32)


def packed_rows(matrix, fold):
    rows = matrix.shape[0] // fold
    return jnp.concatenate([matrix[i * rows : (i + 1) * rows] for i in range(fold)], 1)


def unpacked_rows(matrix, fold):
    cols = matrix.shape[1] // fold
    return jnp.concatenate([matrix[:, i * cols : (i + 1) * cols] for i in range(fold)], 0)


def gram_kernel(sh, fold, c_hbm, a_ref, slot_ref, out_ref, c_ref, sem):
    copy = pltpu.make_async_copy(c_hbm, c_ref, sem)
    copy.start()
    total_slots = sh.owners * sh.slots
    count = slot_ref.shape[0]
    chosen = selection(slot_ref, count, total_slots)
    both = jnp.zeros((2 * count, 2 * total_slots), jnp.float32)
    copy.wait()
    for layer in range(sh.layers):
        rows = a_ref[:, layer].reshape(total_slots, sh.width)
        both = both + lax.dot_general(
            c_ref[layer],
            jnp.concatenate(split(rows), 0),
            (((1,), (1,)), ((), ())),
            preferred_element_type=jnp.float32,
        )
    wide = both[:count] + both[count:]
    rows = wide[:, :total_slots] + wide[:, total_slots:]
    picked = lax.dot_general(
        rows, chosen, (((1,), (1,)), ((), ())), precision=highest,
        preferred_element_type=jnp.float32,
    ) * (1.0 / sh.box**3)
    picked = packed_rows(picked, fold)
    if len(out_ref.shape) == 2:
        out_ref[...] = picked
    else:
        out_ref[...] = jnp.broadcast_to(picked[None], out_ref.shape)


def gram(sh, c, a, slot, fold, copies):
    count = slot.shape[0]
    shape = (count // fold, count * fold)
    if copies:
        shape = (copies,) + shape
    return pl.pallas_call(
        functools.partial(gram_kernel, sh, fold),
        out_shape=(jax.ShapeDtypeStruct(shape, jnp.float32), pltpu.VMEM(c.shape, c.dtype)),
        in_specs=[pl.BlockSpec(memory_space=pltpu.HBM)]
        + [pl.BlockSpec(memory_space=pltpu.VMEM)] * 2,
        scratch_shapes=[pltpu.SemaphoreType.DMA],
        compiler_params=params(16),
        cost_estimate=cost(10**9, 10**7),
        name="gram",
    )(pltpu.with_memory_space_constraint(c, pltpu.HBM), a, slot)


def correct_kernel(sh, fold, own, parts, c_ref, a_ref, slot_ref, part_ref, *outs):
    *out_refs, mult_ref, inv_ref = outs
    total_slots = sh.owners * sh.slots
    count = slot_ref.shape[0]
    packed = part_ref[...]
    if packed.ndim == 3:
        packed = packed.sum(0)
    multipliers = unpacked_rows(packed, fold)
    mult_ref[...] = multipliers
    row = lax.broadcasted_iota(jnp.int32, (count, count), 0)
    col = lax.broadcasted_iota(jnp.int32, (count, count), 1)
    diagonal = jnp.sum(jnp.where(row == col, multipliers, 0.0), axis=1, keepdims=True)
    denominator = 2.0 * coupling_z + 4.0 * coupling_xy + 1.0 + jnp.abs(diagonal)
    inv_ref[...] = jnp.broadcast_to(1.0 / denominator, (count, LANES))
    chosen = selection(slot_ref, count, total_slots)
    high, low = split(-multipliers.T)
    chosen = chosen.astype(jnp.bfloat16)
    weights = jnp.concatenate(
        [
            jnp.concatenate([chosen, chosen, high, high], 1),
            jnp.concatenate(
                [jnp.zeros((count, 2 * total_slots), jnp.bfloat16), low, jnp.zeros_like(low)], 1
            ),
        ],
        0,
    )

    def body(layer, place, out_ref):
        rows = split(a_ref[:, layer].reshape(total_slots, sh.width))
        data = jnp.concatenate([rows[0], rows[1], c_ref[layer]], 0)
        both = jnp.dot(weights, data, preferred_element_type=jnp.float32)
        result = both[:count] + both[count:]
        for owner in range(sh.owners):
            out_ref[owner, place * own : (place + 1) * own] = result[
                owner * own : (owner + 1) * own
            ]

    for part, out_ref in zip(parts, out_refs):
        for place, layer in enumerate(part):
            body(layer, place, out_ref)


def correct(sh, c, a, slot, part, fold, parts):
    count = slot.shape[0]
    own = count // sh.owners
    return pl.pallas_call(
        functools.partial(correct_kernel, sh, fold, own, parts),
        out_shape=tuple(
            jax.ShapeDtypeStruct((sh.owners, len(layers) * own, sh.width), jnp.float32)
            for layers in parts
        )
        + (
            jax.ShapeDtypeStruct((count, count), jnp.float32),
            jax.ShapeDtypeStruct((count, LANES), jnp.float32),
        ),
        compiler_params=params(16),
        cost_estimate=cost(10**9, 10**7),
        name="correct",
    )(c, a, slot, part)


def relax_kernel(sh, own, parts, boxes, *refs):
    r_refs = refs[: len(parts)]
    lo_ref, hi_ref, inv_ref, res_hbm, dir_hbm, *refs = refs[len(parts) :]
    res_ref, one_ref, two_ref, res_out, dir_out, sems = refs
    places = {layer: (ref, i) for part, ref in zip(parts, r_refs) for i, layer in enumerate(part)}
    rows = sh.depth * own
    edge = SWEEPS * own
    first = pl.multiple_of(lax.axis_index("orb") * own, own)
    inverse = inv_ref[pl.ds(first, own), :]
    inverse = jnp.concatenate([inverse] * (8 // own), 0)
    keep_lo = inverse * (lax.axis_index("box") > 0).astype(jnp.float32)
    keep_hi = inverse * (lax.axis_index("box") < boxes - 1).astype(jnp.float32)
    tiles = (rows + 2 * edge) // 8
    edge_tiles = edge // 8

    def scale(tile):
        if tile < edge_tiles:
            return keep_lo
        return keep_hi if tile >= tiles - edge_tiles else inverse

    group = min(16, sh.chunks)
    blank = jnp.zeros((rows + 2 * edge, LANES), jnp.float32)
    for ref in (one_ref, two_ref):
        ref[0] = blank
        ref[sh.chunks + 1] = blank

    def leave(source, target, kind, step, width):
        lanes = pl.ds(pl.multiple_of(step * width, LANES), width)
        return pltpu.make_async_copy(
            source.at[:, :, lanes], target.at[:, :, lanes], sems.at[kind, step]
        )

    def gather(block, carry):
        for inner in range(sh.inner):
            chunk = block * sh.inner + inner
            lanes = slice(inner * LANES, (inner + 1) * LANES)
            pieces = [lo_ref[block, :, lanes]]
            for g in range(sh.layered):
                for layer in range(sh.layers):
                    ref, i = places[layer]
                    pieces.append(ref[g * sh.across + block, i * own : (i + 1) * own, lanes])
            pieces += [hi_ref[block, :, lanes]]
            column = jnp.concatenate(pieces, 0)
            for tile in range(tiles):
                value = column[tile * 8 : (tile + 1) * 8]
                res_ref[chunk, tile * 8 : (tile + 1) * 8] = value
                one_ref[chunk + 1, tile * 8 : (tile + 1) * 8] = value * scale(tile)
            out_lanes = pl.ds(pl.multiple_of(chunk * LANES, LANES), LANES)
            for orbital in range(own):
                here = pl.ds(edge + orbital, sh.depth, stride=own)
                res_out[orbital, :, out_lanes] = res_ref[chunk, here, :]
        leave(res_out, res_hbm, 0, block, sh.width).start()
        return carry

    lax.fori_loop(0, sh.across, gather, 0)

    sub = lax.broadcasted_iota(jnp.int32, (8, LANES), 0)
    lane = lax.broadcasted_iota(jnp.int32, (8, LANES), 1)
    upper = sub >= own
    right_half = lane >= LANES // 2
    not_last = (lane % sh.box) != sh.box - 1
    not_first = (lane % sh.box) != 0
    assert 8 // own == 2

    def sweep(source, target, tile_list):
        def body(step, carry):
            seen = {}

            def value_at(column, tile):
                if not 0 <= tile < tiles:
                    return jnp.zeros((8, LANES), jnp.float32)
                if (column, tile) not in seen:
                    seen[column, tile] = source[step * group + column + 1, pl.ds(tile * 8, 8)]
                return seen[column, tile]

            for column in range(group):
                for tile in tile_list:
                    here = pl.ds(tile * 8, 8)
                    value = value_at(column, tile)
                    beside = jnp.where(
                        upper, value_at(column, tile - 1), value_at(column, tile + 1)
                    )
                    along_z = pltpu.roll(value + beside, own, 0)
                    beside = jnp.where(
                        right_half, value_at(column - 1, tile), value_at(column + 1, tile)
                    )
                    along_y = pltpu.roll(value + beside, LANES // 2, 1)
                    along_x = pltpu.roll(jnp.where(not_last, value, 0.0), 1, 1) + pltpu.roll(
                        jnp.where(not_first, value, 0.0), LANES - 1, 1
                    )
                    total = (
                        res_ref[step * group + column, here]
                        + coupling_xy * (along_y + along_x)
                        + coupling_z * along_z
                    )
                    target[step * group + column + 1, here] = total * scale(tile)
            return carry

        lax.fori_loop(0, sh.chunks // group, body, 0)

    source, target = one_ref, two_ref
    for done in range(1, SWEEPS + 1):
        first_tile = done * own // 8
        sweep(source, target, range(first_tile, tiles - first_tile))
        source, target = target, source

    def spread(step, carry):
        for column in range(group):
            chunk = step * group + column
            out_lanes = pl.ds(pl.multiple_of(chunk * LANES, LANES), LANES)
            for orbital in range(own):
                here = pl.ds(edge + orbital, sh.depth, stride=own)
                dir_out[orbital, :, out_lanes] = source[chunk + 1, here, :]
        leave(dir_out, dir_hbm, 1, step, group * LANES).start()
        return carry

    lax.fori_loop(0, sh.chunks // group, spread, 0)
    for block in range(sh.across):
        leave(res_out, res_hbm, 0, block, sh.width).wait()
    for step in range(sh.chunks // group):
        leave(dir_out, dir_hbm, 1, step, group * LANES).wait()


def relax(sh, own, parts, boxes, pieces, lo, hi, inverse):
    rows = (sh.depth + 2 * SWEEPS) * own
    scratch = pltpu.VMEM((sh.chunks, rows, LANES), jnp.float32)
    padded = pltpu.VMEM((sh.chunks + 2, rows, LANES), jnp.float32)
    out = (own, sh.depth, sh.plane)
    hbm = pl.BlockSpec(memory_space=pltpu.HBM)
    vmem = pl.BlockSpec(memory_space=pltpu.VMEM)
    return pl.pallas_call(
        functools.partial(relax_kernel, sh, own, parts, boxes),
        out_shape=(pltpu.HBM(out, jnp.float32),) * 2,
        out_specs=(hbm, hbm),
        in_specs=[vmem] * (3 + len(parts)),
        scratch_shapes=[scratch, padded, padded]
        + [pltpu.VMEM(out, jnp.float32)] * 2
        + [pltpu.SemaphoreType.DMA((2, max(sh.across, sh.chunks)))],
        compiler_params=params(14),
        cost_estimate=cost(10**9, 10**7),
        name="relax",
    )(*pieces, lo, hi, inverse)


def pairs(first, count):
    lower = range(first, count - 1, 2)
    return [(i, i + 1) for i in lower] + [(i + 1, i) for i in lower]


def to_all(value, axes):
    return lax.all_to_all(value, axes, split_axis=0, concat_axis=0, tiled=True)


def step(psi, potential, orbital_slot):
    slots, depth, plane = psi.shape
    owners = lax.axis_size("orb")
    boxes = lax.axis_size("box")
    sh = Shape(slots, depth, plane, owners)
    count = orbital_slot.shape[0]
    own = count // owners
    magic = banded(sh.box, sh.box, 0, 0, magic_weights(MTAPS), 1 - MTAPS // 2)
    kinetic = banded(sh.box, sh.box, 0, 0, second_weights(KREACH), -KREACH)
    fwd, bwd, kin = (jnp.asarray(two_part(m)) for m in (magic, magic.T, kinetic))

    swap_far = pairs(1, boxes)
    swap_near = pairs(0, boxes)
    slot = orbital_slot.reshape(count, 1)
    far = lax.ppermute(psi, "box", swap_far)
    packed = pack(sh, psi)
    received = to_all(packed, "orb")
    near = lax.ppermute(psi, "box", swap_near)
    c, w, kin_own = own_part(sh, psi, fwd, kin)
    pieces = choose(sh, slot, received)
    v_far = lax.ppermute(potential, "box", swap_far)
    v_near = lax.ppermute(potential, "box", swap_near)
    sides = side_part(sh, far, near, fwd)
    applied = halo_part(sh, (c, w, kin_own), sides, v_far, potential, v_near, bwd)
    applied_pieces = to_all(applied, "orb")

    fold = max(1, LANES // count)
    devices = owners * boxes
    copies = devices if devices * count * count <= 1 << 20 else 0
    part, pieces = gram(sh, pieces, applied_pieces, slot, fold, copies)
    part = to_all(part, ("orb", "box")) if copies else lax.psum(part, ("orb", "box"))
    if sh.layered == 1 and depth > 2 * SWEEPS:
        parts = (
            tuple(range(SWEEPS)) + tuple(range(depth - SWEEPS, depth)),
            tuple(range(SWEEPS, depth - SWEEPS)),
        )
    else:
        parts = (tuple(range(sh.layers)),)
    *corrected, multipliers, inverse = correct(
        sh, pieces, applied_pieces, slot, part, fold, parts
    )
    returned = [to_all(value, "orb") for value in corrected]
    edge = SWEEPS * own
    from_low = lax.ppermute(
        returned[0][-sh.across :, -edge:], "box", [(i, i + 1) for i in range(boxes - 1)]
    )
    from_high = lax.ppermute(
        returned[0][: sh.across, :edge], "box", [(i + 1, i) for i in range(boxes - 1)]
    )
    residual, direction = relax(
        sh, own, parts, boxes, returned, from_low, from_high, inverse
    )
    return (residual, direction, multipliers)


def solution(mesh):
    in_specs = (P("orb", "box", None), P("box", None), P())
    out_specs = (P("orb", "box", None), P("orb", "box", None), P())
    return jax.shard_map(step, mesh=mesh, in_specs=in_specs, out_specs=out_specs, check_vma=False)
```

```python
import functools
import math

import jax
import jax.numpy as jnp
import numpy as np
from jax import lax
from jax.experimental import pallas as pl
from jax.experimental.pallas import tpu as pltpu
from jax.sharding import PartitionSpec as P


MTAPS = 16
KREACH = 14
SWEEPS = 4
LANES = 128

highest = lax.Precision.HIGHEST
coupling_z = 4.0
coupling_xy = 1.0


def magic_weights(tap_count):
    half_len = tap_count // 2
    offsets = np.arange(1 - half_len, half_len + 1) * 1.0
    weights = np.ones(tap_count)
    for index_a in range(tap_count):
        for index_b in range(tap_count):
            if index_b != index_a:
                weights[index_a] *= (0.25 - offsets[index_b]) / (
                    offsets[index_a] - offsets[index_b]
                )
    return weights


def second_weights(reach_cells):
    factor = math.factorial(reach_cells) ** 2
    weights = np.zeros(2 * reach_cells + 1)
    for distance in range(1, reach_cells + 1):
        entry_value = (
            2.0
            * (-1) ** (distance + 1)
            * factor
            / (
                distance
                * distance
                * math.factorial(reach_cells - distance)
                * math.factorial(reach_cells + distance)
            )
        )
        weights[reach_cells + distance] = entry_value
        weights[reach_cells - distance] = entry_value
    weights[reach_cells] = -weights.sum()
    return -0.5 * weights


def banded(row_count, col_count, row_start, col_start, weights, offset_low):
    row_index = np.arange(row_count)[:, None] + row_start
    col_index = np.arange(col_count)[None, :] + col_start
    position = row_index - col_index - offset_low
    inside = (position >= 0) & (position < len(weights))
    return np.where(inside, weights[np.clip(position, 0, len(weights) - 1)], 0.0)


def f32(value):
    return float(np.float32(value))


MAGIC = {k: f32(w) for k, w in zip(range(1 - MTAPS // 2, MTAPS // 2 + 1), magic_weights(MTAPS))}
MAGIC_T = {-k: w for k, w in MAGIC.items()}
KINETIC = {
    d: f32(w) for d, w in zip(range(-KREACH, KREACH + 1), second_weights(KREACH))
}
LOW = MTAPS // 2
HIGH = MTAPS // 2 - 1


def two_part(matrix):
    width = matrix.shape[0]
    block = np.kron(np.eye(LANES // width), matrix).astype(np.float32)
    high = block.astype(jnp.bfloat16)
    low = (block - high.astype(np.float32)).astype(jnp.bfloat16)
    return np.block([[high, low], [high, np.zeros_like(low)]])


def split(value):
    high = value.astype(jnp.bfloat16)
    low = (value - high.astype(jnp.float32)).astype(jnp.bfloat16)
    return high, low


def lane_product(parts, matrix):
    both = jnp.dot(parts, matrix, preferred_element_type=jnp.float32)
    return both[:, :LANES] + both[:, LANES:]


def params(mib):
    return pltpu.CompilerParams(vmem_limit_bytes=mib << 20)


def cost(flops, bytes_accessed):
    return pl.CostEstimate(flops=flops, bytes_accessed=bytes_accessed, transcendentals=0)


class Shape:
    def __init__(self, slots, depth, plane, owners):
        self.slots, self.depth, self.plane, self.owners = slots, depth, plane, owners
        self.box = math.isqrt(plane)
        self.chunks = plane // LANES
        self.across = min(owners, self.chunks)
        self.layered = owners // self.across
        self.layers = depth // self.layered
        self.width = plane // self.across
        self.inner = self.width // LANES

    def at(self, layer, block, inner):
        piece = (layer // self.layers) * self.across + block
        lanes = slice(inner * LANES, (inner + 1) * LANES)
        return piece, layer % self.layers, slice(None), lanes


def pack_kernel(sh, psi_hbm, out_hbm, buffer, sems_in, sems_out):
    def pair(index):
        first = (index // sh.across) * sh.layers
        lane = (index % sh.across) * sh.width
        source = psi_hbm.at[:, pl.ds(first, sh.layers), pl.ds(lane, sh.width)]
        return (
            pltpu.make_async_copy(source, buffer.at[index], sems_in.at[index]),
            pltpu.make_async_copy(buffer.at[index], out_hbm.at[index], sems_out.at[index]),
        )

    copies = [pair(index) for index in range(sh.owners)]
    for arrive, leave in copies:
        arrive.start()
    for arrive, leave in copies:
        arrive.wait()
        leave.start()
    for arrive, leave in copies:
        leave.wait()


def pack(sh, psi):
    shape = (sh.owners, sh.slots, sh.layers, sh.width)
    return pl.pallas_call(
        functools.partial(pack_kernel, sh),
        out_shape=pltpu.HBM(shape, jnp.float32),
        in_specs=[pl.BlockSpec(memory_space=pltpu.HBM)],
        out_specs=pl.BlockSpec(memory_space=pltpu.HBM),
        scratch_shapes=[
            pltpu.VMEM(shape, jnp.float32),
            pltpu.SemaphoreType.DMA((sh.owners,)),
            pltpu.SemaphoreType.DMA((sh.owners,)),
        ],
        compiler_params=params(8),
        cost_estimate=cost(0, 2 * psi.size * 4),
        name="pack",
    )(pltpu.with_memory_space_constraint(psi, pltpu.HBM))


def choose_kernel(sh, slot_ref, in_ref, out_ref):
    count = slot_ref.shape[0]
    total_slots = sh.owners * sh.slots
    chosen = selection(slot_ref, count, total_slots).astype(jnp.bfloat16)
    turned = [
        jnp.transpose(in_ref[index], (1, 0, 2)) for index in range(sh.owners)
    ]
    for layer in range(sh.layers):
        high, low = split(jnp.concatenate([rows[layer] for rows in turned], 0))
        high = jnp.dot(chosen, high, preferred_element_type=jnp.float32)
        low = jnp.dot(chosen, low, preferred_element_type=jnp.float32)
        out_ref[layer, :count] = high.astype(jnp.bfloat16)
        out_ref[layer, count:] = low.astype(jnp.bfloat16)


def choose(sh, slot, pieces):
    count = slot.shape[0]
    return pl.pallas_call(
        functools.partial(choose_kernel, sh),
        out_shape=pltpu.HBM((sh.layers, 2 * count, sh.width), jnp.bfloat16),
        compiler_params=params(12),
        cost_estimate=cost(10**8, 2 * pieces.size * 4),
        name="choose",
    )(slot, pltpu.with_memory_space_constraint(pieces, pltpu.HBM))


def odd_pairs(even, lane):
    turned = [pltpu.roll(v, LANES // 2, 1) for v in even]
    zero = jnp.zeros_like(even[0])
    low = [zero] + turned
    high = turned + [zero]
    return [jnp.where(lane, a, b) for a, b in zip(low, high)]


def row_filter(even, odd, weights):
    count = len(even)
    out = []
    for b in range(count):
        total = None
        for d, w in weights.items():
            e = b + d // 2
            if d % 2 == 0:
                if not 0 <= e < count:
                    continue
                term = even[e]
            else:
                if not 0 <= e + 1 <= count:
                    continue
                term = odd[e + 1]
            total = term * w if total is None else total + term * w
        out.append(total)
    return out


def row_filter_even(even, odd, weights, reach):
    count = len(even)
    out = []
    for b in range(count):
        total = even[b] * weights[0]
        for d in range(1, reach + 1):
            if d % 2 == 0:
                places = [e for e in (b + d // 2, b - d // 2) if 0 <= e < count]
                terms = [even[e] for e in places]
            else:
                places = [e for e in (b + d // 2 + 1, b - d // 2) if 0 <= e <= count]
                terms = [odd[e] for e in places]
            if not terms:
                continue
            term = terms[0] if len(terms) == 1 else terms[0] + terms[1]
            total = total + term * weights[d]
        out.append(total)
    return out


def layer_sum(p, weights, layer, total=None):
    for k, w in weights.items():
        value = layer(p + k)
        if value is not None:
            total = value * w if total is None else total + value * w
    return total


def layer_sum_even(q, total, layer):
    for d in range(1, KREACH + 1):
        terms = [t for t in (layer(q - d), layer(q + d)) if t is not None]
        if terms:
            term = terms[0] if len(terms) == 1 else terms[0] + terms[1]
            total = total + term * KINETIC[d]
    return total


def half_mask(slots):
    return lax.broadcasted_iota(jnp.int32, (slots, LANES), 1) < LANES // 2


def lane_pass(sh, slab, kept, matrices, targets):
    depth = sh.depth

    def body(block, carry):
        parts = []
        for inner in range(sh.inner):
            chunk = block * sh.inner + inner
            lanes = pl.ds(pl.multiple_of(chunk * LANES, LANES), LANES)
            rows = jnp.transpose(slab[:, :, lanes], (1, 0, 2))
            for layer in range(depth):
                kept[layer, chunk] = rows[layer]
            high, low = split(rows.reshape(depth * sh.slots, LANES))
            parts.append(jnp.concatenate([high, low], 1))
        parts = jnp.concatenate(parts, 0)
        for matrix, target in zip(matrices, targets):
            result = lane_product(parts, matrix[...])
            result = result.reshape(sh.inner, depth, sh.slots, LANES)
            for inner in range(sh.inner):
                for layer in range(depth):
                    target[layer, block * sh.inner + inner] = result[inner, layer]
        return carry

    lax.fori_loop(0, sh.across, body, 0)


def own_kernel(sh, psi_ref, fwd_ref, kin_ref, c_out, grid_out, kin_out, x_ref, w_ref):
    lane_pass(sh, psi_ref, c_out, [fwd_ref, kin_ref], [x_ref, kin_out])
    lane = half_mask(sh.slots)

    def body(layer, carry):
        even = [x_ref[layer, b] for b in range(sh.chunks)]
        for b, v in enumerate(row_filter(even, odd_pairs(even, lane), MAGIC)):
            w_ref[layer, b] = v
        even = [c_out[layer, b] for b in range(sh.chunks)]
        sums = row_filter_even(even, odd_pairs(even, lane), KINETIC, KREACH)
        for b, v in enumerate(sums):
            kin_out[layer, b] += v
        return carry

    lax.fori_loop(0, sh.depth, body, 0)
    depth = sh.depth

    def along_z(chunk, carry):
        values = [w_ref[z, chunk] for z in range(depth)]
        for p in range(-LOW, depth + HIGH):
            grid_out[p + LOW, chunk] = layer_sum(
                p, MAGIC, lambda z: values[z] if 0 <= z < depth else None
            )
        cs = [c_out[z, chunk] for z in range(depth)]
        for q in range(depth):
            total = kin_out[q, chunk] + cs[q] * KINETIC[0]
            kin_out[q, chunk] = layer_sum_even(
                q, total, lambda z: cs[z] if 0 <= z < depth else None
            )
        return carry

    lax.fori_loop(0, sh.chunks, along_z, 0)


def own_part(sh, psi, fwd, kin):
    full = jax.ShapeDtypeStruct((sh.depth, sh.chunks, sh.slots, LANES), jnp.float32)
    grid = jax.ShapeDtypeStruct((sh.depth + LOW + HIGH,) + full.shape[1:], jnp.float32)
    return pl.pallas_call(
        functools.partial(own_kernel, sh),
        out_shape=(full, grid, full),
        scratch_shapes=[pltpu.VMEM(full.shape, jnp.float32)] * 2,
        compiler_params=params(18),
        cost_estimate=cost(10 * 10**9, 10**7),
        name="own_part",
    )(psi, fwd, kin)


def side_kernel(sh, slab_hbm, fwd_ref, c_out, w_out, slab_ref, x_ref, sem):
    copy = pltpu.make_async_copy(slab_hbm, slab_ref, sem)
    copy.start()
    lane = half_mask(sh.slots)
    copy.wait()
    lane_pass(sh, slab_ref, c_out, [fwd_ref], [x_ref])

    def filter_rows(layer, carry):
        even = [x_ref[layer, b] for b in range(sh.chunks)]
        for b, v in enumerate(row_filter(even, odd_pairs(even, lane), MAGIC)):
            w_out[layer, b] = v
        return carry

    lax.fori_loop(0, sh.depth, filter_rows, 0)


def side_part(sh, slab, fwd):
    full = (sh.depth, sh.chunks, sh.slots, LANES)
    return pl.pallas_call(
        functools.partial(side_kernel, sh),
        out_shape=(jax.ShapeDtypeStruct(full, jnp.float32),) * 2,
        in_specs=[pl.BlockSpec(memory_space=pl.ANY), pl.BlockSpec(memory_space=pltpu.VMEM)],
        scratch_shapes=[
            pltpu.VMEM(slab.shape, jnp.float32),
            pltpu.VMEM(full, jnp.float32),
            pltpu.SemaphoreType.DMA,
        ],
        compiler_params=params(8),
        cost_estimate=cost(5 * 10**9, 10**7),
        name="side_part",
    )(slab, fwd)


def halo_kernel(
    sh, grid_ref, kin_ref, cfar_ref, wfar_ref, cnear_ref, wnear_ref, vfar_ref, v_ref,
    vnear_ref, bwd_ref, out_hbm, x_ref, y_ref, kz_ref, vlo_ref, vhi_ref, out_ref, sems,
):
    lane = half_mask(sh.slots)
    depth = sh.depth
    even = lax.rem(lax.axis_index("box"), 2) == 0
    vlo_ref[...] = jnp.where(even, vfar_ref[...], vnear_ref[...])
    vhi_ref[...] = jnp.where(even, vnear_ref[...], vfar_ref[...])

    def along_z(clo_ref, wlo_ref, chi_ref, whi_ref, chunk, carry):
        lanes = pl.ds(pl.multiple_of(chunk * LANES, LANES), LANES)

        def outside(below, above):
            places = {}

            def layer(z):
                if 0 <= z < depth:
                    return None
                if z not in places:
                    places[z] = (below if z < 0 else above)[z % depth, chunk]
                return places[z]

            return layer

        def level(z):
            ref = vlo_ref if z < 0 else (v_ref if z < depth else vhi_ref)
            return jnp.broadcast_to(ref[z % depth : z % depth + 1, lanes], (sh.slots, LANES))

        mixed = outside(wlo_ref, whi_ref)
        grid = {}
        for p in range(-LOW, depth + HIGH):
            grid[p] = layer_sum(p, MAGIC, mixed, grid_ref[p + LOW, chunk]) * level(p)
        for q in range(depth):
            x_ref[q, chunk] = layer_sum(q, MAGIC_T, grid.get)
        coeffs = outside(clo_ref, chi_ref)
        for q in range(depth):
            kz_ref[q, chunk] = layer_sum_even(q, kin_ref[q, chunk], coeffs)
        return carry

    far_pair, near_pair = (cfar_ref, wfar_ref), (cnear_ref, wnear_ref)

    @pl.when(even)
    def _():
        lax.fori_loop(0, sh.chunks, functools.partial(along_z, *far_pair, *near_pair), 0)

    @pl.when(jnp.logical_not(even))
    def _():
        lax.fori_loop(0, sh.chunks, functools.partial(along_z, *near_pair, *far_pair), 0)

    def filter_back(layer, carry):
        even = [x_ref[layer, b] for b in range(sh.chunks)]
        for b, v in enumerate(row_filter(even, odd_pairs(even, lane), MAGIC_T)):
            y_ref[layer, b] = v
        return carry

    lax.fori_loop(0, depth, filter_back, 0)

    def piece(index):
        return pltpu.make_async_copy(out_ref.at[index], out_hbm.at[index], sems.at[index])

    def finish(block, carry):
        parts = []
        for inner in range(sh.inner):
            chunk = block * sh.inner + inner
            rows = jnp.concatenate([y_ref[layer, chunk] for layer in range(depth)], 0)
            high, low = split(rows)
            parts.append(jnp.concatenate([high, low], 1))
        result = lane_product(jnp.concatenate(parts, 0), bwd_ref[...])
        result = result.reshape(sh.inner, depth, sh.slots, LANES)
        for inner in range(sh.inner):
            chunk = block * sh.inner + inner
            for layer in range(depth):
                out_ref[sh.at(layer, block, inner)] = result[inner, layer] + kz_ref[layer, chunk]
        for group in range(sh.layered):
            piece(group * sh.across + block).start()
        return carry

    lax.fori_loop(0, sh.across, finish, 0)
    for index in range(sh.owners):
        piece(index).wait()


def halo_part(sh, own, sides, v_far, v, v_near, bwd):
    full = pltpu.VMEM((sh.depth, sh.chunks, sh.slots, LANES), jnp.float32)
    out = (sh.owners, sh.layers, sh.slots, sh.width)
    return pl.pallas_call(
        functools.partial(halo_kernel, sh),
        out_shape=pltpu.HBM(out, jnp.float32),
        in_specs=[pl.BlockSpec(memory_space=pltpu.VMEM)] * 10,
        out_specs=pl.BlockSpec(memory_space=pltpu.HBM),
        scratch_shapes=[full] * 3
        + [pltpu.VMEM(v.shape, jnp.float32)] * 2
        + [pltpu.VMEM(out, jnp.float32), pltpu.SemaphoreType.DMA((sh.owners,))],
        compiler_params=params(14),
        cost_estimate=cost(20 * 10**9, 10**7),
        name="halo_part",
    )(*own, *sides, v_far, v, v_near, bwd)


def selection(slot_ref, count, slots_all):
    column = lax.broadcasted_iota(jnp.int32, (count, slots_all), 1)
    return (column == slot_ref[...]).astype(jnp.float32)


def packed_rows(matrix, fold):
    rows = matrix.shape[0] // fold
    return jnp.concatenate([matrix[i * rows : (i + 1) * rows] for i in range(fold)], 1)


def unpacked_rows(matrix, fold):
    cols = matrix.shape[1] // fold
    return jnp.concatenate([matrix[:, i * cols : (i + 1) * cols] for i in range(fold)], 0)


def gram_kernel(sh, fold, c_hbm, a_ref, slot_ref, out_ref, c_ref, sem):
    copy = pltpu.make_async_copy(c_hbm, c_ref, sem)
    copy.start()
    total_slots = sh.owners * sh.slots
    count = slot_ref.shape[0]
    chosen = selection(slot_ref, count, total_slots)
    both = jnp.zeros((2 * count, 2 * total_slots), jnp.float32)
    copy.wait()
    for layer in range(sh.layers):
        rows = a_ref[:, layer].reshape(total_slots, sh.width)
        both = both + lax.dot_general(
            c_ref[layer],
            jnp.concatenate(split(rows), 0),
            (((1,), (1,)), ((), ())),
            preferred_element_type=jnp.float32,
        )
    wide = both[:count] + both[count:]
    rows = wide[:, :total_slots] + wide[:, total_slots:]
    picked = lax.dot_general(
        rows, chosen, (((1,), (1,)), ((), ())), precision=highest,
        preferred_element_type=jnp.float32,
    ) * (1.0 / sh.box**3)
    picked = packed_rows(picked, fold)
    if len(out_ref.shape) == 2:
        out_ref[...] = picked
    else:
        out_ref[...] = jnp.broadcast_to(picked[None], out_ref.shape)


def gram(sh, c, a, slot, fold, copies):
    count = slot.shape[0]
    shape = (count // fold, count * fold)
    if copies:
        shape = (copies,) + shape
    return pl.pallas_call(
        functools.partial(gram_kernel, sh, fold),
        out_shape=(jax.ShapeDtypeStruct(shape, jnp.float32), pltpu.VMEM(c.shape, c.dtype)),
        in_specs=[pl.BlockSpec(memory_space=pltpu.HBM)]
        + [pl.BlockSpec(memory_space=pltpu.VMEM)] * 2,
        scratch_shapes=[pltpu.SemaphoreType.DMA],
        compiler_params=params(16),
        cost_estimate=cost(10**9, 10**7),
        name="gram",
    )(pltpu.with_memory_space_constraint(c, pltpu.HBM), a, slot)


def correct_kernel(sh, fold, own, parts, c_ref, a_ref, slot_ref, part_ref, *outs):
    *out_refs, mult_ref, inv_ref = outs
    total_slots = sh.owners * sh.slots
    count = slot_ref.shape[0]
    packed = part_ref[...]
    if packed.ndim == 3:
        packed = packed.sum(0)
    multipliers = unpacked_rows(packed, fold)
    mult_ref[...] = multipliers
    row = lax.broadcasted_iota(jnp.int32, (count, count), 0)
    col = lax.broadcasted_iota(jnp.int32, (count, count), 1)
    diagonal = jnp.sum(jnp.where(row == col, multipliers, 0.0), axis=1, keepdims=True)
    denominator = 2.0 * coupling_z + 4.0 * coupling_xy + 1.0 + jnp.abs(diagonal)
    inv_ref[...] = jnp.broadcast_to(1.0 / denominator, (count, LANES))
    chosen = selection(slot_ref, count, total_slots)
    high, low = split(-multipliers.T)
    chosen = chosen.astype(jnp.bfloat16)
    weights = jnp.concatenate(
        [
            jnp.concatenate([chosen, chosen, high, high], 1),
            jnp.concatenate(
                [jnp.zeros((count, 2 * total_slots), jnp.bfloat16), low, jnp.zeros_like(low)], 1
            ),
        ],
        0,
    )

    def body(layer, place, out_ref):
        rows = split(a_ref[:, layer].reshape(total_slots, sh.width))
        data = jnp.concatenate([rows[0], rows[1], c_ref[layer]], 0)
        both = jnp.dot(weights, data, preferred_element_type=jnp.float32)
        result = both[:count] + both[count:]
        for owner in range(sh.owners):
            out_ref[owner, place * own : (place + 1) * own] = result[
                owner * own : (owner + 1) * own
            ]

    for part, out_ref in zip(parts, out_refs):
        for place, layer in enumerate(part):
            body(layer, place, out_ref)


def correct(sh, c, a, slot, part, fold, parts):
    count = slot.shape[0]
    own = count // sh.owners
    return pl.pallas_call(
        functools.partial(correct_kernel, sh, fold, own, parts),
        out_shape=tuple(
            jax.ShapeDtypeStruct((sh.owners, len(layers) * own, sh.width), jnp.float32)
            for layers in parts
        )
        + (
            jax.ShapeDtypeStruct((count, count), jnp.float32),
            jax.ShapeDtypeStruct((count, LANES), jnp.float32),
        ),
        compiler_params=params(16),
        cost_estimate=cost(10**9, 10**7),
        name="correct",
    )(c, a, slot, part)


def relax_kernel(sh, own, parts, boxes, *refs):
    r_refs = refs[: len(parts)]
    lo_ref, hi_ref, inv_ref, res_hbm, dir_hbm, *refs = refs[len(parts) :]
    res_ref, one_ref, two_ref, res_out, dir_out, sems = refs
    places = {layer: (ref, i) for part, ref in zip(parts, r_refs) for i, layer in enumerate(part)}
    rows = sh.depth * own
    edge = SWEEPS * own
    first = pl.multiple_of(lax.axis_index("orb") * own, own)
    inverse = inv_ref[pl.ds(first, own), :]
    inverse = jnp.concatenate([inverse] * (8 // own), 0)
    keep_lo = inverse * (lax.axis_index("box") > 0).astype(jnp.float32)
    keep_hi = inverse * (lax.axis_index("box") < boxes - 1).astype(jnp.float32)
    tiles = (rows + 2 * edge) // 8
    edge_tiles = edge // 8

    def scale(tile):
        if tile < edge_tiles:
            return keep_lo
        return keep_hi if tile >= tiles - edge_tiles else inverse

    group = min(16, sh.chunks)
    blank = jnp.zeros((rows + 2 * edge, LANES), jnp.float32)
    for ref in (one_ref, two_ref):
        ref[0] = blank
        ref[sh.chunks + 1] = blank

    def leave(source, target, kind, step, width):
        lanes = pl.ds(pl.multiple_of(step * width, LANES), width)
        return pltpu.make_async_copy(
            source.at[:, :, lanes], target.at[:, :, lanes], sems.at[kind, step]
        )

    def gather(block, carry):
        for inner in range(sh.inner):
            chunk = block * sh.inner + inner
            lanes = slice(inner * LANES, (inner + 1) * LANES)
            pieces = [lo_ref[block, :, lanes]]
            for g in range(sh.layered):
                for layer in range(sh.layers):
                    ref, i = places[layer]
                    pieces.append(ref[g * sh.across + block, i * own : (i + 1) * own, lanes])
            pieces += [hi_ref[block, :, lanes]]
            column = jnp.concatenate(pieces, 0)
            for tile in range(tiles):
                value = column[tile * 8 : (tile + 1) * 8]
                res_ref[chunk, tile * 8 : (tile + 1) * 8] = value
                one_ref[chunk + 1, tile * 8 : (tile + 1) * 8] = value * scale(tile)
            out_lanes = pl.ds(pl.multiple_of(chunk * LANES, LANES), LANES)
            for orbital in range(own):
                here = pl.ds(edge + orbital, sh.depth, stride=own)
                res_out[orbital, :, out_lanes] = res_ref[chunk, here, :]
        leave(res_out, res_hbm, 0, block, sh.width).start()
        return carry

    lax.fori_loop(0, sh.across, gather, 0)

    sub = lax.broadcasted_iota(jnp.int32, (8, LANES), 0)
    lane = lax.broadcasted_iota(jnp.int32, (8, LANES), 1)
    upper = sub >= own
    right_half = lane >= LANES // 2
    not_last = (lane % sh.box) != sh.box - 1
    not_first = (lane % sh.box) != 0
    assert 8 // own == 2

    def sweep(source, target, tile_list):
        def body(step, carry):
            seen = {}

            def value_at(column, tile):
                if not 0 <= tile < tiles:
                    return jnp.zeros((8, LANES), jnp.float32)
                if (column, tile) not in seen:
                    seen[column, tile] = source[step * group + column + 1, pl.ds(tile * 8, 8)]
                return seen[column, tile]

            for column in range(group):
                for tile in tile_list:
                    here = pl.ds(tile * 8, 8)
                    value = value_at(column, tile)
                    beside = jnp.where(
                        upper, value_at(column, tile - 1), value_at(column, tile + 1)
                    )
                    along_z = pltpu.roll(value + beside, own, 0)
                    beside = jnp.where(
                        right_half, value_at(column - 1, tile), value_at(column + 1, tile)
                    )
                    along_y = pltpu.roll(value + beside, LANES // 2, 1)
                    along_x = pltpu.roll(jnp.where(not_last, value, 0.0), 1, 1) + pltpu.roll(
                        jnp.where(not_first, value, 0.0), LANES - 1, 1
                    )
                    total = (
                        res_ref[step * group + column, here]
                        + coupling_xy * (along_y + along_x)
                        + coupling_z * along_z
                    )
                    target[step * group + column + 1, here] = total * scale(tile)
            return carry

        lax.fori_loop(0, sh.chunks // group, body, 0)

    source, target = one_ref, two_ref
    for done in range(1, SWEEPS + 1):
        first_tile = done * own // 8
        sweep(source, target, range(first_tile, tiles - first_tile))
        source, target = target, source

    def spread(step, carry):
        for column in range(group):
            chunk = step * group + column
            out_lanes = pl.ds(pl.multiple_of(chunk * LANES, LANES), LANES)
            for orbital in range(own):
                here = pl.ds(edge + orbital, sh.depth, stride=own)
                dir_out[orbital, :, out_lanes] = source[chunk + 1, here, :]
        leave(dir_out, dir_hbm, 1, step, group * LANES).start()
        return carry

    lax.fori_loop(0, sh.chunks // group, spread, 0)
    for block in range(sh.across):
        leave(res_out, res_hbm, 0, block, sh.width).wait()
    for step in range(sh.chunks // group):
        leave(dir_out, dir_hbm, 1, step, group * LANES).wait()


def relax(sh, own, parts, boxes, pieces, lo, hi, inverse):
    rows = (sh.depth + 2 * SWEEPS) * own
    scratch = pltpu.VMEM((sh.chunks, rows, LANES), jnp.float32)
    padded = pltpu.VMEM((sh.chunks + 2, rows, LANES), jnp.float32)
    out = (own, sh.depth, sh.plane)
    hbm = pl.BlockSpec(memory_space=pltpu.HBM)
    vmem = pl.BlockSpec(memory_space=pltpu.VMEM)
    return pl.pallas_call(
        functools.partial(relax_kernel, sh, own, parts, boxes),
        out_shape=(pltpu.HBM(out, jnp.float32),) * 2,
        out_specs=(hbm, hbm),
        in_specs=[vmem] * (3 + len(parts)),
        scratch_shapes=[scratch, padded, padded]
        + [pltpu.VMEM(out, jnp.float32)] * 2
        + [pltpu.SemaphoreType.DMA((2, max(sh.across, sh.chunks)))],
        compiler_params=params(14),
        cost_estimate=cost(10**9, 10**7),
        name="relax",
    )(*pieces, lo, hi, inverse)


def pairs(first, count):
    lower = range(first, count - 1, 2)
    return [(i, i + 1) for i in lower] + [(i + 1, i) for i in lower]


def to_all(value, axes):
    return lax.all_to_all(value, axes, split_axis=0, concat_axis=0, tiled=True)


def step(psi, potential, orbital_slot):
    slots, depth, plane = psi.shape
    owners = lax.axis_size("orb")
    boxes = lax.axis_size("box")
    sh = Shape(slots, depth, plane, owners)
    count = orbital_slot.shape[0]
    own = count // owners
    magic = banded(sh.box, sh.box, 0, 0, magic_weights(MTAPS), 1 - MTAPS // 2)
    kinetic = banded(sh.box, sh.box, 0, 0, second_weights(KREACH), -KREACH)
    fwd, bwd, kin = (jnp.asarray(two_part(m)) for m in (magic, magic.T, kinetic))

    swap_far = pairs(1, boxes)
    swap_near = pairs(0, boxes)
    slot = orbital_slot.reshape(count, 1)
    far = lax.ppermute(psi, "box", swap_far)
    packed = pack(sh, psi)
    received = to_all(packed, "orb")
    near = lax.ppermute(psi, "box", swap_near)
    own_grid, own_kin = own_part(sh, psi, fwd, kin)[1:]
    pieces = choose(sh, slot, received)
    v_far = lax.ppermute(potential, "box", swap_far)
    v_near = lax.ppermute(potential, "box", swap_near)
    near_side = side_part(sh, near, fwd)
    far_side = side_part(sh, far, fwd)
    sides = tuple(far_side) + tuple(near_side)
    applied = halo_part(sh, (own_grid, own_kin), sides, v_far, potential, v_near, bwd)
    applied_pieces = to_all(applied, "orb")

    fold = max(1, LANES // count)
    devices = owners * boxes
    copies = devices if devices * count * count <= 1 << 20 else 0
    part, pieces = gram(sh, pieces, applied_pieces, slot, fold, copies)
    part = to_all(part, ("orb", "box")) if copies else lax.psum(part, ("orb", "box"))
    if sh.layered == 1 and depth > 2 * SWEEPS:
        parts = (
            tuple(range(SWEEPS)) + tuple(range(depth - SWEEPS, depth)),
            tuple(range(SWEEPS, depth - SWEEPS)),
        )
    else:
        parts = (tuple(range(sh.layers)),)
    *corrected, multipliers, inverse = correct(
        sh, pieces, applied_pieces, slot, part, fold, parts
    )
    returned = [to_all(value, "orb") for value in corrected]
    edge = SWEEPS * own
    from_low = lax.ppermute(
        returned[0][-sh.across :, -edge:], "box", [(i, i + 1) for i in range(boxes - 1)]
    )
    from_high = lax.ppermute(
        returned[0][: sh.across, :edge], "box", [(i + 1, i) for i in range(boxes - 1)]
    )
    residual, direction = relax(
        sh, own, parts, boxes, returned, from_low, from_high, inverse
    )
    return (residual, direction, multipliers)


def solution(mesh):
    in_specs = (P("orb", "box", None), P("box", None), P())
    out_specs = (P("orb", "box", None), P("orb", "box", None), P())
    return jax.shard_map(step, mesh=mesh, in_specs=in_specs, out_specs=out_specs, check_vma=False)
```

```python
import functools
import math

import jax
import jax.numpy as jnp
import numpy as np
from jax import lax
from jax.experimental import pallas as pl
from jax.experimental.pallas import tpu as pltpu
from jax.sharding import PartitionSpec as P


MTAPS = 16
KREACH = 14
SWEEPS = 4
LANES = 128

highest = lax.Precision.HIGHEST
coupling_z = 4.0
coupling_xy = 1.0


def magic_weights(tap_count):
    half_len = tap_count // 2
    offsets = np.arange(1 - half_len, half_len + 1) * 1.0
    weights = np.ones(tap_count)
    for index_a in range(tap_count):
        for index_b in range(tap_count):
            if index_b != index_a:
                weights[index_a] *= (0.25 - offsets[index_b]) / (
                    offsets[index_a] - offsets[index_b]
                )
    return weights


def second_weights(reach_cells):
    factor = math.factorial(reach_cells) ** 2
    weights = np.zeros(2 * reach_cells + 1)
    for distance in range(1, reach_cells + 1):
        entry_value = (
            2.0
            * (-1) ** (distance + 1)
            * factor
            / (
                distance
                * distance
                * math.factorial(reach_cells - distance)
                * math.factorial(reach_cells + distance)
            )
        )
        weights[reach_cells + distance] = entry_value
        weights[reach_cells - distance] = entry_value
    weights[reach_cells] = -weights.sum()
    return -0.5 * weights


def banded(row_count, col_count, row_start, col_start, weights, offset_low):
    row_index = np.arange(row_count)[:, None] + row_start
    col_index = np.arange(col_count)[None, :] + col_start
    position = row_index - col_index - offset_low
    inside = (position >= 0) & (position < len(weights))
    return np.where(inside, weights[np.clip(position, 0, len(weights) - 1)], 0.0)


def f32(value):
    return float(np.float32(value))


MAGIC = {k: f32(w) for k, w in zip(range(1 - MTAPS // 2, MTAPS // 2 + 1), magic_weights(MTAPS))}
MAGIC_T = {-k: w for k, w in MAGIC.items()}
KINETIC = {
    d: f32(w) for d, w in zip(range(-KREACH, KREACH + 1), second_weights(KREACH))
}
LOW = MTAPS // 2
HIGH = MTAPS // 2 - 1


def two_part(matrix):
    width = matrix.shape[0]
    block = np.kron(np.eye(LANES // width), matrix).astype(np.float32)
    high = block.astype(jnp.bfloat16)
    low = (block - high.astype(np.float32)).astype(jnp.bfloat16)
    return np.block([[high, low], [high, np.zeros_like(low)]])


def split(value):
    high = value.astype(jnp.bfloat16)
    low = (value - high.astype(jnp.float32)).astype(jnp.bfloat16)
    return high, low


def lane_product(parts, matrix):
    both = jnp.dot(parts, matrix, preferred_element_type=jnp.float32)
    return both[:, :LANES] + both[:, LANES:]


def params(mib):
    return pltpu.CompilerParams(vmem_limit_bytes=mib << 20)


def cost(flops, bytes_accessed):
    return pl.CostEstimate(flops=flops, bytes_accessed=bytes_accessed, transcendentals=0)


class Shape:
    def __init__(self, slots, depth, plane, owners):
        self.slots, self.depth, self.plane, self.owners = slots, depth, plane, owners
        self.box = math.isqrt(plane)
        self.chunks = plane // LANES
        self.across = min(owners, self.chunks)
        self.layered = owners // self.across
        self.layers = depth // self.layered
        self.width = plane // self.across
        self.inner = self.width // LANES

    def at(self, layer, block, inner):
        piece = (layer // self.layers) * self.across + block
        lanes = slice(inner * LANES, (inner + 1) * LANES)
        return piece, layer % self.layers, slice(None), lanes


def pack_kernel(sh, psi_hbm, out_hbm, buffer, sems_in, sems_out):
    def pair(index):
        first = (index // sh.across) * sh.layers
        lane = (index % sh.across) * sh.width
        source = psi_hbm.at[:, pl.ds(first, sh.layers), pl.ds(lane, sh.width)]
        return (
            pltpu.make_async_copy(source, buffer.at[index], sems_in.at[index]),
            pltpu.make_async_copy(buffer.at[index], out_hbm.at[index], sems_out.at[index]),
        )

    copies = [pair(index) for index in range(sh.owners)]
    for arrive, leave in copies:
        arrive.start()
    for arrive, leave in copies:
        arrive.wait()
        leave.start()
    for arrive, leave in copies:
        leave.wait()


def pack(sh, psi):
    shape = (sh.owners, sh.slots, sh.layers, sh.width)
    return pl.pallas_call(
        functools.partial(pack_kernel, sh),
        out_shape=pltpu.HBM(shape, jnp.float32),
        in_specs=[pl.BlockSpec(memory_space=pltpu.HBM)],
        out_specs=pl.BlockSpec(memory_space=pltpu.HBM),
        scratch_shapes=[
            pltpu.VMEM(shape, jnp.float32),
            pltpu.SemaphoreType.DMA((sh.owners,)),
            pltpu.SemaphoreType.DMA((sh.owners,)),
        ],
        compiler_params=params(8),
        cost_estimate=cost(0, 2 * psi.size * 4),
        name="pack",
    )(pltpu.with_memory_space_constraint(psi, pltpu.HBM))


def choose_kernel(sh, slot_ref, in_ref, out_ref):
    count = slot_ref.shape[0]
    total_slots = sh.owners * sh.slots
    chosen = selection(slot_ref, count, total_slots).astype(jnp.bfloat16)
    turned = [
        jnp.transpose(in_ref[index], (1, 0, 2)) for index in range(sh.owners)
    ]
    for layer in range(sh.layers):
        high, low = split(jnp.concatenate([rows[layer] for rows in turned], 0))
        high = jnp.dot(chosen, high, preferred_element_type=jnp.float32)
        low = jnp.dot(chosen, low, preferred_element_type=jnp.float32)
        out_ref[layer, :count] = high.astype(jnp.bfloat16)
        out_ref[layer, count:] = low.astype(jnp.bfloat16)


def choose(sh, slot, pieces):
    count = slot.shape[0]
    return pl.pallas_call(
        functools.partial(choose_kernel, sh),
        out_shape=pltpu.HBM((sh.layers, 2 * count, sh.width), jnp.bfloat16),
        compiler_params=params(12),
        cost_estimate=cost(10**8, 2 * pieces.size * 4),
        name="choose",
    )(slot, pltpu.with_memory_space_constraint(pieces, pltpu.HBM))


def odd_pairs(even, lane):
    turned = [pltpu.roll(v, LANES // 2, 1) for v in even]
    zero = jnp.zeros_like(even[0])
    low = [zero] + turned
    high = turned + [zero]
    return [jnp.where(lane, a, b) for a, b in zip(low, high)]


def row_filter(even, odd, weights):
    count = len(even)
    out = []
    for b in range(count):
        total = None
        for d, w in weights.items():
            e = b + d // 2
            if d % 2 == 0:
                if not 0 <= e < count:
                    continue
                term = even[e]
            else:
                if not 0 <= e + 1 <= count:
                    continue
                term = odd[e + 1]
            total = term * w if total is None else total + term * w
        out.append(total)
    return out


def row_filter_even(even, odd, weights, reach):
    count = len(even)
    out = []
    for b in range(count):
        total = even[b] * weights[0]
        for d in range(1, reach + 1):
            if d % 2 == 0:
                places = [e for e in (b + d // 2, b - d // 2) if 0 <= e < count]
                terms = [even[e] for e in places]
            else:
                places = [e for e in (b + d // 2 + 1, b - d // 2) if 0 <= e <= count]
                terms = [odd[e] for e in places]
            if not terms:
                continue
            term = terms[0] if len(terms) == 1 else terms[0] + terms[1]
            total = total + term * weights[d]
        out.append(total)
    return out


def layer_sum(p, weights, layer, total=None):
    for k, w in weights.items():
        value = layer(p + k)
        if value is not None:
            total = value * w if total is None else total + value * w
    return total


def layer_sum_even(q, total, layer):
    for d in range(1, KREACH + 1):
        terms = [t for t in (layer(q - d), layer(q + d)) if t is not None]
        if terms:
            term = terms[0] if len(terms) == 1 else terms[0] + terms[1]
            total = total + term * KINETIC[d]
    return total


def half_mask(slots):
    return lax.broadcasted_iota(jnp.int32, (slots, LANES), 1) < LANES // 2


def lane_pass(sh, slab, kept, matrices, targets):
    depth = sh.depth

    def body(block, carry):
        parts = []
        for inner in range(sh.inner):
            chunk = block * sh.inner + inner
            lanes = pl.ds(pl.multiple_of(chunk * LANES, LANES), LANES)
            rows = jnp.transpose(slab[:, :, lanes], (1, 0, 2))
            for layer in range(depth):
                kept[layer, chunk] = rows[layer]
            high, low = split(rows.reshape(depth * sh.slots, LANES))
            parts.append(jnp.concatenate([high, low], 1))
        parts = jnp.concatenate(parts, 0)
        for matrix, target in zip(matrices, targets):
            result = lane_product(parts, matrix[...])
            result = result.reshape(sh.inner, depth, sh.slots, LANES)
            for inner in range(sh.inner):
                for layer in range(depth):
                    target[layer, block * sh.inner + inner] = result[inner, layer]
        return carry

    lax.fori_loop(0, sh.across, body, 0)


def own_kernel(sh, psi_ref, fwd_ref, kin_ref, c_out, grid_out, kin_out, x_ref, w_ref):
    lane_pass(sh, psi_ref, c_out, [fwd_ref, kin_ref], [x_ref, kin_out])
    lane = half_mask(sh.slots)

    def body(layer, carry):
        even = [x_ref[layer, b] for b in range(sh.chunks)]
        for b, v in enumerate(row_filter(even, odd_pairs(even, lane), MAGIC)):
            w_ref[layer, b] = v
        even = [c_out[layer, b] for b in range(sh.chunks)]
        sums = row_filter_even(even, odd_pairs(even, lane), KINETIC, KREACH)
        for b, v in enumerate(sums):
            kin_out[layer, b] += v
        return carry

    lax.fori_loop(0, sh.depth, body, 0)
    depth = sh.depth

    def along_z(chunk, carry):
        values = [w_ref[z, chunk] for z in range(depth)]
        for p in range(-LOW, depth + HIGH):
            grid_out[p + LOW, chunk] = layer_sum(
                p, MAGIC, lambda z: values[z] if 0 <= z < depth else None
            )
        cs = [c_out[z, chunk] for z in range(depth)]
        for q in range(depth):
            total = kin_out[q, chunk] + cs[q] * KINETIC[0]
            kin_out[q, chunk] = layer_sum_even(
                q, total, lambda z: cs[z] if 0 <= z < depth else None
            )
        return carry

    lax.fori_loop(0, sh.chunks, along_z, 0)


def own_part(sh, psi, fwd, kin):
    full = jax.ShapeDtypeStruct((sh.depth, sh.chunks, sh.slots, LANES), jnp.float32)
    grid = jax.ShapeDtypeStruct((sh.depth + LOW + HIGH,) + full.shape[1:], jnp.float32)
    return pl.pallas_call(
        functools.partial(own_kernel, sh),
        out_shape=(full, grid, full),
        scratch_shapes=[pltpu.VMEM(full.shape, jnp.float32)] * 2,
        compiler_params=params(18),
        cost_estimate=cost(10 * 10**9, 10**7),
        name="own_part",
    )(psi, fwd, kin)


def side_kernel(sh, slab_hbm, fwd_ref, c_out, w_out, slab_ref, x_ref, sem):
    copy = pltpu.make_async_copy(slab_hbm, slab_ref, sem)
    copy.start()
    lane = half_mask(sh.slots)
    copy.wait()
    lane_pass(sh, slab_ref, c_out, [fwd_ref], [x_ref])

    def filter_rows(layer, carry):
        even = [x_ref[layer, b] for b in range(sh.chunks)]
        for b, v in enumerate(row_filter(even, odd_pairs(even, lane), MAGIC)):
            w_out[layer, b] = v
        return carry

    lax.fori_loop(0, sh.depth, filter_rows, 0)


def side_part(sh, slab, fwd):
    full = (sh.depth, sh.chunks, sh.slots, LANES)
    return pl.pallas_call(
        functools.partial(side_kernel, sh),
        out_shape=(jax.ShapeDtypeStruct(full, jnp.float32),) * 2,
        in_specs=[pl.BlockSpec(memory_space=pl.ANY), pl.BlockSpec(memory_space=pltpu.VMEM)],
        scratch_shapes=[
            pltpu.VMEM(slab.shape, jnp.float32),
            pltpu.VMEM(full, jnp.float32),
            pltpu.SemaphoreType.DMA,
        ],
        compiler_params=params(8),
        cost_estimate=cost(5 * 10**9, 10**7),
        name="side_part",
    )(slab, fwd)


def halo_kernel(
    sh, grid_ref, kin_ref, cfar_ref, wfar_ref, cnear_ref, wnear_ref, vfar_ref, v_ref,
    vnear_ref, bwd_ref, out_hbm, x_ref, y_ref, kz_ref, vlo_ref, vhi_ref, out_ref, sems,
):
    lane = half_mask(sh.slots)
    depth = sh.depth
    even = lax.rem(lax.axis_index("box"), 2) == 0
    vlo_ref[...] = jnp.where(even, vfar_ref[...], vnear_ref[...])
    vhi_ref[...] = jnp.where(even, vnear_ref[...], vfar_ref[...])

    def along_z(clo_ref, wlo_ref, chi_ref, whi_ref, chunk, carry):
        lanes = pl.ds(pl.multiple_of(chunk * LANES, LANES), LANES)

        def outside(below, above):
            places = {}

            def layer(z):
                if 0 <= z < depth:
                    return None
                if z not in places:
                    places[z] = (below if z < 0 else above)[z % depth, chunk]
                return places[z]

            return layer

        def level(z):
            ref = vlo_ref if z < 0 else (v_ref if z < depth else vhi_ref)
            return jnp.broadcast_to(ref[z % depth : z % depth + 1, lanes], (sh.slots, LANES))

        mixed = outside(wlo_ref, whi_ref)
        grid = {}
        for p in range(-LOW, depth + HIGH):
            grid[p] = layer_sum(p, MAGIC, mixed, grid_ref[p + LOW, chunk]) * level(p)
        for q in range(depth):
            x_ref[q, chunk] = layer_sum(q, MAGIC_T, grid.get)
        coeffs = outside(clo_ref, chi_ref)
        for q in range(depth):
            kz_ref[q, chunk] = layer_sum_even(q, kin_ref[q, chunk], coeffs)
        return carry

    far_pair, near_pair = (cfar_ref, wfar_ref), (cnear_ref, wnear_ref)

    @pl.when(even)
    def _():
        lax.fori_loop(0, sh.chunks, functools.partial(along_z, *far_pair, *near_pair), 0)

    @pl.when(jnp.logical_not(even))
    def _():
        lax.fori_loop(0, sh.chunks, functools.partial(along_z, *near_pair, *far_pair), 0)

    def filter_back(layer, carry):
        even = [x_ref[layer, b] for b in range(sh.chunks)]
        for b, v in enumerate(row_filter(even, odd_pairs(even, lane), MAGIC_T)):
            y_ref[layer, b] = v
        return carry

    lax.fori_loop(0, depth, filter_back, 0)

    def piece(index):
        return pltpu.make_async_copy(out_ref.at[index], out_hbm.at[index], sems.at[index])

    def finish(block, carry):
        parts = []
        for inner in range(sh.inner):
            chunk = block * sh.inner + inner
            rows = jnp.concatenate([y_ref[layer, chunk] for layer in range(depth)], 0)
            high, low = split(rows)
            parts.append(jnp.concatenate([high, low], 1))
        result = lane_product(jnp.concatenate(parts, 0), bwd_ref[...])
        result = result.reshape(sh.inner, depth, sh.slots, LANES)
        for inner in range(sh.inner):
            chunk = block * sh.inner + inner
            for layer in range(depth):
                out_ref[sh.at(layer, block, inner)] = result[inner, layer] + kz_ref[layer, chunk]
        for group in range(sh.layered):
            piece(group * sh.across + block).start()
        return carry

    lax.fori_loop(0, sh.across, finish, 0)
    for index in range(sh.owners):
        piece(index).wait()


def halo_part(sh, own, sides, v_far, v, v_near, bwd):
    full = pltpu.VMEM((sh.depth, sh.chunks, sh.slots, LANES), jnp.float32)
    out = (sh.owners, sh.layers, sh.slots, sh.width)
    return pl.pallas_call(
        functools.partial(halo_kernel, sh),
        out_shape=pltpu.HBM(out, jnp.float32),
        in_specs=[pl.BlockSpec(memory_space=pltpu.VMEM)] * 10,
        out_specs=pl.BlockSpec(memory_space=pltpu.HBM),
        scratch_shapes=[full] * 3
        + [pltpu.VMEM(v.shape, jnp.float32)] * 2
        + [pltpu.VMEM(out, jnp.float32), pltpu.SemaphoreType.DMA((sh.owners,))],
        compiler_params=params(14),
        cost_estimate=cost(20 * 10**9, 10**7),
        name="halo_part",
    )(*own, *sides, v_far, v, v_near, bwd)


def selection(slot_ref, count, slots_all):
    column = lax.broadcasted_iota(jnp.int32, (count, slots_all), 1)
    return (column == slot_ref[...]).astype(jnp.float32)


def packed_rows(matrix, fold):
    rows = matrix.shape[0] // fold
    return jnp.concatenate([matrix[i * rows : (i + 1) * rows] for i in range(fold)], 1)


def unpacked_rows(matrix, fold):
    cols = matrix.shape[1] // fold
    return jnp.concatenate([matrix[:, i * cols : (i + 1) * cols] for i in range(fold)], 0)


def gram_kernel(sh, fold, c_hbm, a_ref, slot_ref, out_ref, c_ref, sem):
    copy = pltpu.make_async_copy(c_hbm, c_ref, sem)
    copy.start()
    total_slots = sh.owners * sh.slots
    count = slot_ref.shape[0]
    chosen = selection(slot_ref, count, total_slots)
    both = jnp.zeros((2 * count, 2 * total_slots), jnp.float32)
    copy.wait()
    for layer in range(sh.layers):
        rows = a_ref[:, layer].reshape(total_slots, sh.width)
        both = both + lax.dot_general(
            c_ref[layer],
            jnp.concatenate(split(rows), 0),
            (((1,), (1,)), ((), ())),
            preferred_element_type=jnp.float32,
        )
    wide = both[:count] + both[count:]
    rows = wide[:, :total_slots] + wide[:, total_slots:]
    picked = lax.dot_general(
        rows, chosen, (((1,), (1,)), ((), ())), precision=highest,
        preferred_element_type=jnp.float32,
    ) * (1.0 / sh.box**3)
    picked = packed_rows(picked, fold)
    if len(out_ref.shape) == 2:
        out_ref[...] = picked
    else:
        out_ref[...] = jnp.broadcast_to(picked[None], out_ref.shape)


def gram(sh, c, a, slot, fold, copies):
    count = slot.shape[0]
    shape = (count // fold, count * fold)
    if copies:
        shape = (copies,) + shape
    return pl.pallas_call(
        functools.partial(gram_kernel, sh, fold),
        out_shape=(jax.ShapeDtypeStruct(shape, jnp.float32), pltpu.VMEM(c.shape, c.dtype)),
        in_specs=[pl.BlockSpec(memory_space=pltpu.HBM)]
        + [pl.BlockSpec(memory_space=pltpu.VMEM)] * 2,
        scratch_shapes=[pltpu.SemaphoreType.DMA],
        compiler_params=params(16),
        cost_estimate=cost(10**9, 10**7),
        name="gram",
    )(pltpu.with_memory_space_constraint(c, pltpu.HBM), a, slot)


def correct_kernel(sh, fold, own, parts, c_ref, a_ref, slot_ref, part_ref, *outs):
    *out_refs, mult_ref, inv_ref = outs
    total_slots = sh.owners * sh.slots
    count = slot_ref.shape[0]
    packed = part_ref[...]
    if packed.ndim == 3:
        packed = packed.sum(0)
    multipliers = unpacked_rows(packed, fold)
    mult_ref[...] = multipliers
    row = lax.broadcasted_iota(jnp.int32, (count, count), 0)
    col = lax.broadcasted_iota(jnp.int32, (count, count), 1)
    diagonal = jnp.sum(jnp.where(row == col, multipliers, 0.0), axis=1, keepdims=True)
    denominator = 2.0 * coupling_z + 4.0 * coupling_xy + 1.0 + jnp.abs(diagonal)
    inv_ref[...] = jnp.broadcast_to(1.0 / denominator, (count, LANES))
    chosen = selection(slot_ref, count, total_slots)
    high, low = split(-multipliers.T)
    chosen = chosen.astype(jnp.bfloat16)
    weights = jnp.concatenate(
        [
            jnp.concatenate([chosen, chosen, high, high], 1),
            jnp.concatenate(
                [jnp.zeros((count, 2 * total_slots), jnp.bfloat16), low, jnp.zeros_like(low)], 1
            ),
        ],
        0,
    )

    def body(layer, place, out_ref):
        rows = split(a_ref[:, layer].reshape(total_slots, sh.width))
        data = jnp.concatenate([rows[0], rows[1], c_ref[layer]], 0)
        both = jnp.dot(weights, data, preferred_element_type=jnp.float32)
        result = both[:count] + both[count:]
        for owner in range(sh.owners):
            out_ref[owner, place * own : (place + 1) * own] = result[
                owner * own : (owner + 1) * own
            ]

    for part, out_ref in zip(parts, out_refs):
        for place, layer in enumerate(part):
            body(layer, place, out_ref)


def correct(sh, c, a, slot, part, fold, parts):
    count = slot.shape[0]
    own = count // sh.owners
    return pl.pallas_call(
        functools.partial(correct_kernel, sh, fold, own, parts),
        out_shape=tuple(
            jax.ShapeDtypeStruct((sh.owners, len(layers) * own, sh.width), jnp.float32)
            for layers in parts
        )
        + (
            jax.ShapeDtypeStruct((count, count), jnp.float32),
            jax.ShapeDtypeStruct((count, LANES), jnp.float32),
        ),
        compiler_params=params(16),
        cost_estimate=cost(10**9, 10**7),
        name="correct",
    )(c, a, slot, part)


def relax_kernel(sh, own, parts, boxes, *refs):
    r_refs = refs[: len(parts)]
    lo_ref, hi_ref, inv_ref, res_hbm, dir_hbm, *refs = refs[len(parts) :]
    res_ref, one_ref, two_ref, res_out, dir_out, sems = refs
    places = {layer: (ref, i) for part, ref in zip(parts, r_refs) for i, layer in enumerate(part)}
    rows = sh.depth * own
    edge = SWEEPS * own
    first = pl.multiple_of(lax.axis_index("orb") * own, own)
    inverse = inv_ref[pl.ds(first, own), :]
    inverse = jnp.concatenate([inverse] * (8 // own), 0)
    keep_lo = inverse * (lax.axis_index("box") > 0).astype(jnp.float32)
    keep_hi = inverse * (lax.axis_index("box") < boxes - 1).astype(jnp.float32)
    tiles = (rows + 2 * edge) // 8
    edge_tiles = edge // 8

    def scale(tile):
        if tile < edge_tiles:
            return keep_lo
        return keep_hi if tile >= tiles - edge_tiles else inverse

    group = min(32, sh.chunks)
    blank = jnp.zeros((rows + 2 * edge, LANES), jnp.float32)
    for ref in (one_ref, two_ref):
        ref[0] = blank
        ref[sh.chunks + 1] = blank

    def leave(source, target, kind, step, width):
        lanes = pl.ds(pl.multiple_of(step * width, LANES), width)
        return pltpu.make_async_copy(
            source.at[:, :, lanes], target.at[:, :, lanes], sems.at[kind, step]
        )

    half = sh.chunks // 2
    left = lax.broadcasted_iota(jnp.int32, (8, LANES), 1) < LANES // 2
    assert sh.across % 2 == 0

    def turned(value):
        return pltpu.roll(value, LANES // 2, 1)

    def column_of(block, inner):
        lanes = slice(inner * LANES, (inner + 1) * LANES)
        pieces = [lo_ref[block, :, lanes]]
        for g in range(sh.layered):
            for layer in range(sh.layers):
                ref, i = places[layer]
                pieces.append(ref[g * sh.across + block, i * own : (i + 1) * own, lanes])
        pieces += [hi_ref[block, :, lanes]]
        return jnp.concatenate(pieces, 0)

    def gather(block, carry):
        other = block + sh.across // 2
        for inner in range(sh.inner):
            chunk = block * sh.inner + inner
            columns = (column_of(block, inner), column_of(other, inner))
            for tile in range(tiles):
                here = slice(tile * 8, (tile + 1) * 8)
                low, high = columns[0][here], columns[1][here]
                mixed = (jnp.where(left, low, turned(high)), jnp.where(left, turned(low), high))
                for k in range(2):
                    res_ref[2 * chunk + k, here] = mixed[k]
                    one_ref[2 * chunk + k + 1, here] = mixed[k] * scale(tile)
            for column, place in zip(columns, (chunk, chunk + half)):
                two_ref[place + 1] = column
                out_lanes = pl.ds(pl.multiple_of(place * LANES, LANES), LANES)
                for orbital in range(own):
                    rows_of = pl.ds(edge + orbital, sh.depth, stride=own)
                    res_out[orbital, :, out_lanes] = two_ref[place + 1, rows_of, :]
        leave(res_out, res_hbm, 0, block, sh.width).start()
        leave(res_out, res_hbm, 0, other, sh.width).start()
        return carry

    lax.fori_loop(0, sh.across // 2, gather, 0)

    def seal(ref):
        for tile in range(tiles):
            here = slice(tile * 8, (tile + 1) * 8)
            ref[0, here] = jnp.where(left, 0.0, turned(ref[sh.chunks, here]))
            ref[sh.chunks + 1, here] = jnp.where(left, turned(ref[1, here]), 0.0)

    seal(one_ref)
    sub = lax.broadcasted_iota(jnp.int32, (8, LANES), 0)
    lane = lax.broadcasted_iota(jnp.int32, (8, LANES), 1)
    upper = sub >= own
    not_last = (lane % sh.box) != sh.box - 1
    not_first = (lane % sh.box) != 0
    assert 8 // own == 2

    def sweep(source, target, tile_list):
        def body(step, carry):
            seen = {}

            def value_at(column, tile):
                if not 0 <= tile < tiles:
                    return jnp.zeros((8, LANES), jnp.float32)
                if (column, tile) not in seen:
                    seen[column, tile] = source[step * group + column + 1, pl.ds(tile * 8, 8)]
                return seen[column, tile]

            for column in range(group):
                for tile in tile_list:
                    here = pl.ds(tile * 8, 8)
                    value = value_at(column, tile)
                    beside = jnp.where(
                        upper, value_at(column, tile - 1), value_at(column, tile + 1)
                    )
                    along_z = pltpu.roll(value + beside, own, 0)
                    along_y = value_at(column - 1, tile) + value_at(column + 1, tile)
                    along_x = pltpu.roll(jnp.where(not_last, value, 0.0), 1, 1) + pltpu.roll(
                        jnp.where(not_first, value, 0.0), LANES - 1, 1
                    )
                    total = (
                        res_ref[step * group + column, here]
                        + coupling_xy * (along_y + along_x)
                        + coupling_z * along_z
                    )
                    target[step * group + column + 1, here] = total * scale(tile)
            return carry

        lax.fori_loop(0, sh.chunks // group, body, 0)

    source, target = one_ref, two_ref
    for done in range(1, SWEEPS + 1):
        first_tile = done * own // 8
        sweep(source, target, range(first_tile, tiles - first_tile))
        if done < SWEEPS:
            seal(target)
        source, target = target, source

    few = min(8, half)

    def spread(step, carry):
        for column in range(few):
            chunk = step * few + column
            for tile in range(edge_tiles, tiles - edge_tiles):
                here = slice(tile * 8, (tile + 1) * 8)
                even, odd = source[2 * chunk + 1, here], source[2 * chunk + 2, here]
                target[chunk + 1, here] = jnp.where(left, even, turned(odd))
                target[chunk + half + 1, here] = jnp.where(left, turned(even), odd)
            for place in (chunk, chunk + half):
                out_lanes = pl.ds(pl.multiple_of(place * LANES, LANES), LANES)
                for orbital in range(own):
                    rows_of = pl.ds(edge + orbital, sh.depth, stride=own)
                    dir_out[orbital, :, out_lanes] = target[place + 1, rows_of, :]
        leave(dir_out, dir_hbm, 1, step, few * LANES).start()
        leave(dir_out, dir_hbm, 1, step + half // few, few * LANES).start()
        return carry

    lax.fori_loop(0, half // few, spread, 0)
    for block in range(sh.across):
        leave(res_out, res_hbm, 0, block, sh.width).wait()
    for step in range(sh.chunks // few):
        leave(dir_out, dir_hbm, 1, step, few * LANES).wait()


def relax(sh, own, parts, boxes, pieces, lo, hi, inverse):
    rows = (sh.depth + 2 * SWEEPS) * own
    scratch = pltpu.VMEM((sh.chunks, rows, LANES), jnp.float32)
    padded = pltpu.VMEM((sh.chunks + 2, rows, LANES), jnp.float32)
    out = (own, sh.depth, sh.plane)
    hbm = pl.BlockSpec(memory_space=pltpu.HBM)
    vmem = pl.BlockSpec(memory_space=pltpu.VMEM)
    return pl.pallas_call(
        functools.partial(relax_kernel, sh, own, parts, boxes),
        out_shape=(pltpu.HBM(out, jnp.float32),) * 2,
        out_specs=(hbm, hbm),
        in_specs=[vmem] * (3 + len(parts)),
        scratch_shapes=[scratch, padded, padded]
        + [pltpu.VMEM(out, jnp.float32)] * 2
        + [pltpu.SemaphoreType.DMA((2, max(sh.across, sh.chunks)))],
        compiler_params=params(14),
        cost_estimate=cost(10**9, 10**7),
        name="relax",
    )(*pieces, lo, hi, inverse)


def pairs(first, count):
    lower = range(first, count - 1, 2)
    return [(i, i + 1) for i in lower] + [(i + 1, i) for i in lower]


def to_all(value, axes):
    return lax.all_to_all(value, axes, split_axis=0, concat_axis=0, tiled=True)


def step(psi, potential, orbital_slot):
    slots, depth, plane = psi.shape
    owners = lax.axis_size("orb")
    boxes = lax.axis_size("box")
    sh = Shape(slots, depth, plane, owners)
    count = orbital_slot.shape[0]
    own = count // owners
    magic = banded(sh.box, sh.box, 0, 0, magic_weights(MTAPS), 1 - MTAPS // 2)
    kinetic = banded(sh.box, sh.box, 0, 0, second_weights(KREACH), -KREACH)
    fwd, bwd, kin = (jnp.asarray(two_part(m)) for m in (magic, magic.T, kinetic))

    swap_far = pairs(1, boxes)
    swap_near = pairs(0, boxes)
    slot = orbital_slot.reshape(count, 1)
    far = lax.ppermute(psi, "box", swap_far)
    packed = pack(sh, psi)
    received = to_all(packed, "orb")
    near = lax.ppermute(psi, "box", swap_near)
    own_grid, own_kin = own_part(sh, psi, fwd, kin)[1:]
    pieces = choose(sh, slot, received)
    v_far = lax.ppermute(potential, "box", swap_far)
    v_near = lax.ppermute(potential, "box", swap_near)
    near_side = side_part(sh, near, fwd)
    far_side = side_part(sh, far, fwd)
    sides = tuple(far_side) + tuple(near_side)
    applied = halo_part(sh, (own_grid, own_kin), sides, v_far, potential, v_near, bwd)
    applied_pieces = to_all(applied, "orb")

    fold = max(1, LANES // count)
    devices = owners * boxes
    copies = devices if devices * count * count <= 1 << 20 else 0
    part, pieces = gram(sh, pieces, applied_pieces, slot, fold, copies)
    part = to_all(part, ("orb", "box")) if copies else lax.psum(part, ("orb", "box"))
    if sh.layered == 1 and depth > 2 * SWEEPS:
        parts = (
            tuple(range(SWEEPS)) + tuple(range(depth - SWEEPS, depth)),
            tuple(range(SWEEPS, depth - SWEEPS)),
        )
    else:
        parts = (tuple(range(sh.layers)),)
    *corrected, multipliers, inverse = correct(
        sh, pieces, applied_pieces, slot, part, fold, parts
    )
    returned = [to_all(value, "orb") for value in corrected]
    edge = SWEEPS * own
    from_low = lax.ppermute(
        returned[0][-sh.across :, -edge:], "box", [(i, i + 1) for i in range(boxes - 1)]
    )
    from_high = lax.ppermute(
        returned[0][: sh.across, :edge], "box", [(i + 1, i) for i in range(boxes - 1)]
    )
    residual, direction = relax(
        sh, own, parts, boxes, returned, from_low, from_high, inverse
    )
    return (residual, direction, multipliers)


def solution(mesh):
    in_specs = (P("orb", "box", None), P("box", None), P())
    out_specs = (P("orb", "box", None), P("orb", "box", None), P())
    return jax.shard_map(step, mesh=mesh, in_specs=in_specs, out_specs=out_specs, check_vma=False)
```

```python
import functools
import math

import jax
import jax.numpy as jnp
import numpy as np
from jax import lax
from jax.experimental import pallas as pl
from jax.experimental.pallas import tpu as pltpu
from jax.sharding import PartitionSpec as P


MTAPS = 16
KREACH = 14
SWEEPS = 4
LANES = 128

coupling_z = 4.0
coupling_xy = 1.0


def magic_weights(tap_count):
    half_len = tap_count // 2
    offsets = np.arange(1 - half_len, half_len + 1) * 1.0
    weights = np.ones(tap_count)
    for index_a in range(tap_count):
        for index_b in range(tap_count):
            if index_b != index_a:
                weights[index_a] *= (0.25 - offsets[index_b]) / (
                    offsets[index_a] - offsets[index_b]
                )
    return weights


def second_weights(reach_cells):
    factor = math.factorial(reach_cells) ** 2
    weights = np.zeros(2 * reach_cells + 1)
    for distance in range(1, reach_cells + 1):
        entry_value = (
            2.0
            * (-1) ** (distance + 1)
            * factor
            / (
                distance
                * distance
                * math.factorial(reach_cells - distance)
                * math.factorial(reach_cells + distance)
            )
        )
        weights[reach_cells + distance] = entry_value
        weights[reach_cells - distance] = entry_value
    weights[reach_cells] = -weights.sum()
    return -0.5 * weights


def banded(row_count, col_count, row_start, col_start, weights, offset_low):
    row_index = np.arange(row_count)[:, None] + row_start
    col_index = np.arange(col_count)[None, :] + col_start
    position = row_index - col_index - offset_low
    inside = (position >= 0) & (position < len(weights))
    return np.where(inside, weights[np.clip(position, 0, len(weights) - 1)], 0.0)


def f32(value):
    return float(np.float32(value))


MAGIC = {k: f32(w) for k, w in zip(range(1 - MTAPS // 2, MTAPS // 2 + 1), magic_weights(MTAPS))}
MAGIC_T = {-k: w for k, w in MAGIC.items()}
KINETIC = {
    d: f32(w) for d, w in zip(range(-KREACH, KREACH + 1), second_weights(KREACH))
}
LOW = MTAPS // 2
HIGH = MTAPS // 2 - 1


def two_part(matrix):
    width = matrix.shape[0]
    block = np.kron(np.eye(LANES // width), matrix).astype(np.float32)
    high = block.astype(jnp.bfloat16)
    low = (block - high.astype(np.float32)).astype(jnp.bfloat16)
    return np.block([[high, low], [high, np.zeros_like(low)]])


def split(value):
    high = value.astype(jnp.bfloat16)
    low = (value - high.astype(jnp.float32)).astype(jnp.bfloat16)
    return high, low


def lane_product(parts, matrix):
    both = jnp.dot(parts, matrix, preferred_element_type=jnp.float32)
    return both[:, :LANES] + both[:, LANES:]


def params(mib):
    return pltpu.CompilerParams(vmem_limit_bytes=mib << 20)


def cost(flops, bytes_accessed):
    return pl.CostEstimate(flops=flops, bytes_accessed=bytes_accessed, transcendentals=0)


class Shape:
    def __init__(self, slots, depth, plane, owners):
        self.slots, self.depth, self.plane, self.owners = slots, depth, plane, owners
        self.box = math.isqrt(plane)
        self.chunks = plane // LANES
        self.across = min(owners, self.chunks)
        self.layered = owners // self.across
        self.layers = depth // self.layered
        self.width = plane // self.across
        self.inner = self.width // LANES

    def at(self, layer, block, inner):
        piece = (layer // self.layers) * self.across + block
        lanes = slice(inner * LANES, (inner + 1) * LANES)
        return piece, layer % self.layers, slice(None), lanes


def pack_kernel(sh, psi_hbm, out_hbm, buffer, sems_in, sems_out):
    def pair(index):
        first = (index // sh.across) * sh.layers
        lane = (index % sh.across) * sh.width
        source = psi_hbm.at[:, pl.ds(first, sh.layers), pl.ds(lane, sh.width)]
        return (
            pltpu.make_async_copy(source, buffer.at[index], sems_in.at[index]),
            pltpu.make_async_copy(buffer.at[index], out_hbm.at[index], sems_out.at[index]),
        )

    copies = [pair(index) for index in range(sh.owners)]
    for arrive, leave in copies:
        arrive.start()
    for arrive, leave in copies:
        arrive.wait()
        leave.start()
    for arrive, leave in copies:
        leave.wait()


def pack(sh, psi):
    shape = (sh.owners, sh.slots, sh.layers, sh.width)
    return pl.pallas_call(
        functools.partial(pack_kernel, sh),
        out_shape=pltpu.HBM(shape, jnp.float32),
        in_specs=[pl.BlockSpec(memory_space=pltpu.HBM)],
        out_specs=pl.BlockSpec(memory_space=pltpu.HBM),
        scratch_shapes=[
            pltpu.VMEM(shape, jnp.float32),
            pltpu.SemaphoreType.DMA((sh.owners,)),
            pltpu.SemaphoreType.DMA((sh.owners,)),
        ],
        compiler_params=params(8),
        cost_estimate=cost(0, 2 * psi.size * 4),
        name="pack",
    )(pltpu.with_memory_space_constraint(psi, pltpu.HBM))


def choose_kernel(sh, slot_ref, in_ref, out_ref):
    count = slot_ref.shape[0]
    total_slots = sh.owners * sh.slots
    chosen = selection(slot_ref, count, total_slots).astype(jnp.bfloat16)
    turned = [
        jnp.transpose(in_ref[index], (1, 0, 2)) for index in range(sh.owners)
    ]
    for layer in range(sh.layers):
        high, low = split(jnp.concatenate([rows[layer] for rows in turned], 0))
        high = jnp.dot(chosen, high, preferred_element_type=jnp.float32)
        low = jnp.dot(chosen, low, preferred_element_type=jnp.float32)
        out_ref[layer, :count] = high.astype(jnp.bfloat16)
        out_ref[layer, count:] = low.astype(jnp.bfloat16)


def choose(sh, slot, pieces):
    count = slot.shape[0]
    return pl.pallas_call(
        functools.partial(choose_kernel, sh),
        out_shape=pltpu.HBM((sh.layers, 2 * count, sh.width), jnp.bfloat16),
        compiler_params=params(12),
        cost_estimate=cost(10**8, 2 * pieces.size * 4),
        name="choose",
    )(slot, pltpu.with_memory_space_constraint(pieces, pltpu.HBM))


def odd_pairs(even, lane):
    turned = [pltpu.roll(v, LANES // 2, 1) for v in even]
    zero = jnp.zeros_like(even[0])
    low = [zero] + turned
    high = turned + [zero]
    return [jnp.where(lane, a, b) for a, b in zip(low, high)]


def row_filter(even, odd, weights):
    count = len(even)
    out = []
    for b in range(count):
        total = None
        for d, w in weights.items():
            e = b + d // 2
            if d % 2 == 0:
                if not 0 <= e < count:
                    continue
                term = even[e]
            else:
                if not 0 <= e + 1 <= count:
                    continue
                term = odd[e + 1]
            total = term * w if total is None else total + term * w
        out.append(total)
    return out


def row_filter_even(even, odd, weights, reach):
    count = len(even)
    out = []
    for b in range(count):
        total = even[b] * weights[0]
        for d in range(1, reach + 1):
            if d % 2 == 0:
                places = [e for e in (b + d // 2, b - d // 2) if 0 <= e < count]
                terms = [even[e] for e in places]
            else:
                places = [e for e in (b + d // 2 + 1, b - d // 2) if 0 <= e <= count]
                terms = [odd[e] for e in places]
            if not terms:
                continue
            term = terms[0] if len(terms) == 1 else terms[0] + terms[1]
            total = total + term * weights[d]
        out.append(total)
    return out


def layer_sum(p, weights, layer, total=None):
    for k, w in weights.items():
        value = layer(p + k)
        if value is not None:
            total = value * w if total is None else total + value * w
    return total


def layer_sum_even(q, total, layer):
    for d in range(1, KREACH + 1):
        terms = [t for t in (layer(q - d), layer(q + d)) if t is not None]
        if terms:
            term = terms[0] if len(terms) == 1 else terms[0] + terms[1]
            total = total + term * KINETIC[d]
    return total


def half_mask(slots):
    return lax.broadcasted_iota(jnp.int32, (slots, LANES), 1) < LANES // 2


def lane_pass(sh, slab, kept, matrices, targets):
    depth = sh.depth

    def body(block, carry):
        parts = []
        for inner in range(sh.inner):
            chunk = block * sh.inner + inner
            lanes = pl.ds(pl.multiple_of(chunk * LANES, LANES), LANES)
            rows = jnp.transpose(slab[:, :, lanes], (1, 0, 2))
            for layer in range(depth):
                kept[layer, chunk] = rows[layer]
            high, low = split(rows.reshape(depth * sh.slots, LANES))
            parts.append(jnp.concatenate([high, low], 1))
        parts = jnp.concatenate(parts, 0)
        for matrix, target in zip(matrices, targets):
            result = lane_product(parts, matrix[...])
            result = result.reshape(sh.inner, depth, sh.slots, LANES)
            for inner in range(sh.inner):
                for layer in range(depth):
                    target[layer, block * sh.inner + inner] = result[inner, layer]
        return carry

    lax.fori_loop(0, sh.across, body, 0)


def own_kernel(sh, psi_ref, fwd_ref, kin_ref, c_out, grid_out, kin_out, x_ref, w_ref):
    lane_pass(sh, psi_ref, c_out, [fwd_ref, kin_ref], [x_ref, kin_out])
    lane = half_mask(sh.slots)

    def body(layer, carry):
        even = [x_ref[layer, b] for b in range(sh.chunks)]
        for b, v in enumerate(row_filter(even, odd_pairs(even, lane), MAGIC)):
            w_ref[layer, b] = v
        even = [c_out[layer, b] for b in range(sh.chunks)]
        sums = row_filter_even(even, odd_pairs(even, lane), KINETIC, KREACH)
        for b, v in enumerate(sums):
            kin_out[layer, b] += v
        return carry

    lax.fori_loop(0, sh.depth, body, 0)
    depth = sh.depth

    def along_z(chunk, carry):
        values = [w_ref[z, chunk] for z in range(depth)]
        for p in range(-LOW, depth + HIGH):
            grid_out[p + LOW, chunk] = layer_sum(
                p, MAGIC, lambda z: values[z] if 0 <= z < depth else None
            )
        cs = [c_out[z, chunk] for z in range(depth)]
        for q in range(depth):
            total = kin_out[q, chunk] + cs[q] * KINETIC[0]
            kin_out[q, chunk] = layer_sum_even(
                q, total, lambda z: cs[z] if 0 <= z < depth else None
            )
        return carry

    lax.fori_loop(0, sh.chunks, along_z, 0)


def own_part(sh, psi, fwd, kin):
    full = jax.ShapeDtypeStruct((sh.depth, sh.chunks, sh.slots, LANES), jnp.float32)
    grid = jax.ShapeDtypeStruct((sh.depth + LOW + HIGH,) + full.shape[1:], jnp.float32)
    return pl.pallas_call(
        functools.partial(own_kernel, sh),
        out_shape=(full, grid, full),
        scratch_shapes=[pltpu.VMEM(full.shape, jnp.float32)] * 2,
        compiler_params=params(18),
        cost_estimate=cost(10 * 10**9, 10**7),
        name="own_part",
    )(psi, fwd, kin)


def side_kernel(sh, slab_hbm, fwd_ref, c_out, w_out, slab_ref, x_ref, sem):
    copy = pltpu.make_async_copy(slab_hbm, slab_ref, sem)
    copy.start()
    lane = half_mask(sh.slots)
    copy.wait()
    lane_pass(sh, slab_ref, c_out, [fwd_ref], [x_ref])

    def filter_rows(layer, carry):
        even = [x_ref[layer, b] for b in range(sh.chunks)]
        for b, v in enumerate(row_filter(even, odd_pairs(even, lane), MAGIC)):
            w_out[layer, b] = v
        return carry

    lax.fori_loop(0, sh.depth, filter_rows, 0)


def side_part(sh, slab, fwd):
    full = (sh.depth, sh.chunks, sh.slots, LANES)
    return pl.pallas_call(
        functools.partial(side_kernel, sh),
        out_shape=(jax.ShapeDtypeStruct(full, jnp.float32),) * 2,
        in_specs=[pl.BlockSpec(memory_space=pl.ANY), pl.BlockSpec(memory_space=pltpu.VMEM)],
        scratch_shapes=[
            pltpu.VMEM(slab.shape, jnp.float32),
            pltpu.VMEM(full, jnp.float32),
            pltpu.SemaphoreType.DMA,
        ],
        compiler_params=params(8),
        cost_estimate=cost(5 * 10**9, 10**7),
        name="side_part",
    )(slab, fwd)


def halo_kernel(
    sh, grid_ref, kin_ref, cfar_ref, wfar_ref, cnear_ref, wnear_ref, vfar_ref, v_ref,
    vnear_ref, bwd_ref, out_hbm, x_ref, y_ref, kz_ref, vlo_ref, vhi_ref, out_ref, sems,
):
    lane = half_mask(sh.slots)
    depth = sh.depth
    even = lax.rem(lax.axis_index("box"), 2) == 0
    vlo_ref[...] = jnp.where(even, vfar_ref[...], vnear_ref[...])
    vhi_ref[...] = jnp.where(even, vnear_ref[...], vfar_ref[...])

    def along_z(clo_ref, wlo_ref, chi_ref, whi_ref, chunk, carry):
        lanes = pl.ds(pl.multiple_of(chunk * LANES, LANES), LANES)

        def outside(below, above):
            places = {}

            def layer(z):
                if 0 <= z < depth:
                    return None
                if z not in places:
                    places[z] = (below if z < 0 else above)[z % depth, chunk]
                return places[z]

            return layer

        def level(z):
            ref = vlo_ref if z < 0 else (v_ref if z < depth else vhi_ref)
            return jnp.broadcast_to(ref[z % depth : z % depth + 1, lanes], (sh.slots, LANES))

        mixed = outside(wlo_ref, whi_ref)
        grid = {}
        for p in range(-LOW, depth + HIGH):
            grid[p] = layer_sum(p, MAGIC, mixed, grid_ref[p + LOW, chunk]) * level(p)
        for q in range(depth):
            x_ref[q, chunk] = layer_sum(q, MAGIC_T, grid.get)
        coeffs = outside(clo_ref, chi_ref)
        for q in range(depth):
            kz_ref[q, chunk] = layer_sum_even(q, kin_ref[q, chunk], coeffs)
        return carry

    far_pair, near_pair = (cfar_ref, wfar_ref), (cnear_ref, wnear_ref)

    @pl.when(even)
    def _():
        lax.fori_loop(0, sh.chunks, functools.partial(along_z, *far_pair, *near_pair), 0)

    @pl.when(jnp.logical_not(even))
    def _():
        lax.fori_loop(0, sh.chunks, functools.partial(along_z, *near_pair, *far_pair), 0)

    def filter_back(layer, carry):
        even = [x_ref[layer, b] for b in range(sh.chunks)]
        for b, v in enumerate(row_filter(even, odd_pairs(even, lane), MAGIC_T)):
            y_ref[layer, b] = v
        return carry

    lax.fori_loop(0, depth, filter_back, 0)

    def piece(index):
        return pltpu.make_async_copy(out_ref.at[index], out_hbm.at[index], sems.at[index])

    def finish(block, carry):
        parts = []
        for inner in range(sh.inner):
            chunk = block * sh.inner + inner
            rows = jnp.concatenate([y_ref[layer, chunk] for layer in range(depth)], 0)
            high, low = split(rows)
            parts.append(jnp.concatenate([high, low], 1))
        result = lane_product(jnp.concatenate(parts, 0), bwd_ref[...])
        result = result.reshape(sh.inner, depth, sh.slots, LANES)
        for inner in range(sh.inner):
            chunk = block * sh.inner + inner
            for layer in range(depth):
                out_ref[sh.at(layer, block, inner)] = result[inner, layer] + kz_ref[layer, chunk]
        for group in range(sh.layered):
            piece(group * sh.across + block).start()
        return carry

    lax.fori_loop(0, sh.across, finish, 0)
    for index in range(sh.owners):
        piece(index).wait()


def halo_part(sh, own, sides, v_far, v, v_near, bwd):
    full = pltpu.VMEM((sh.depth, sh.chunks, sh.slots, LANES), jnp.float32)
    out = (sh.owners, sh.layers, sh.slots, sh.width)
    return pl.pallas_call(
        functools.partial(halo_kernel, sh),
        out_shape=pltpu.HBM(out, jnp.float32),
        in_specs=[pl.BlockSpec(memory_space=pltpu.VMEM)] * 10,
        out_specs=pl.BlockSpec(memory_space=pltpu.HBM),
        scratch_shapes=[full] * 3
        + [pltpu.VMEM(v.shape, jnp.float32)] * 2
        + [pltpu.VMEM(out, jnp.float32), pltpu.SemaphoreType.DMA((sh.owners,))],
        compiler_params=params(14),
        cost_estimate=cost(20 * 10**9, 10**7),
        name="halo_part",
    )(*own, *sides, v_far, v, v_near, bwd)


def selection(slot_ref, count, slots_all):
    column = lax.broadcasted_iota(jnp.int32, (count, slots_all), 1)
    return (column == slot_ref[...]).astype(jnp.float32)


def packed_rows(matrix, fold):
    rows = matrix.shape[0] // fold
    return jnp.concatenate([matrix[i * rows : (i + 1) * rows] for i in range(fold)], 1)


def unpacked_rows(matrix, fold):
    cols = matrix.shape[1] // fold
    return jnp.concatenate([matrix[:, i * cols : (i + 1) * cols] for i in range(fold)], 0)


def gram_kernel(sh, fold, c_hbm, a_ref, slot_ref, out_ref, c_ref, sem):
    copy = pltpu.make_async_copy(c_hbm, c_ref, sem)
    copy.start()
    total_slots = sh.owners * sh.slots
    count = slot_ref.shape[0]
    chosen = selection(slot_ref, count, total_slots)
    both = jnp.zeros((2 * total_slots, 2 * count), jnp.float32)
    copy.wait()
    for layer in range(sh.layers):
        rows = a_ref[:, layer].reshape(total_slots, sh.width)
        both = both + lax.dot_general(
            jnp.concatenate(split(rows), 0),
            c_ref[layer],
            (((1,), (1,)), ((), ())),
            preferred_element_type=jnp.float32,
        )
    wide = both[:total_slots] + both[total_slots:]
    columns = wide[:, :count] + wide[:, count:]
    parts = jnp.concatenate(split(columns), 0)
    chosen = chosen.astype(jnp.bfloat16)
    picked = lax.dot_general(
        parts,
        jnp.concatenate([chosen, chosen], 1),
        (((0,), (1,)), ((), ())),
        preferred_element_type=jnp.float32,
    ) * (1.0 / sh.box**3)
    picked = packed_rows(picked, fold)
    if len(out_ref.shape) == 2:
        out_ref[...] = picked
    else:
        out_ref[...] = jnp.broadcast_to(picked[None], out_ref.shape)


def gram(sh, c, a, slot, fold, copies):
    count = slot.shape[0]
    shape = (count // fold, count * fold)
    if copies:
        shape = (copies,) + shape
    return pl.pallas_call(
        functools.partial(gram_kernel, sh, fold),
        out_shape=(jax.ShapeDtypeStruct(shape, jnp.float32), pltpu.VMEM(c.shape, c.dtype)),
        in_specs=[pl.BlockSpec(memory_space=pltpu.HBM)]
        + [pl.BlockSpec(memory_space=pltpu.VMEM)] * 2,
        scratch_shapes=[pltpu.SemaphoreType.DMA],
        compiler_params=params(16),
        cost_estimate=cost(10**9, 10**7),
        name="gram",
    )(pltpu.with_memory_space_constraint(c, pltpu.HBM), a, slot)


def correct_kernel(sh, fold, own, parts, c_ref, a_ref, slot_ref, part_ref, *outs):
    *out_refs, mult_ref, inv_ref = outs
    total_slots = sh.owners * sh.slots
    count = slot_ref.shape[0]
    packed = part_ref[...]
    if packed.ndim == 3:
        packed = packed.sum(0)
    multipliers = unpacked_rows(packed, fold)
    mult_ref[...] = multipliers
    row = lax.broadcasted_iota(jnp.int32, (count, count), 0)
    col = lax.broadcasted_iota(jnp.int32, (count, count), 1)
    diagonal = jnp.sum(jnp.where(row == col, multipliers, 0.0), axis=1, keepdims=True)
    denominator = 2.0 * coupling_z + 4.0 * coupling_xy + 1.0 + jnp.abs(diagonal)
    inv_ref[...] = jnp.broadcast_to(1.0 / denominator, (count, LANES))
    chosen = selection(slot_ref, count, total_slots)
    high, low = split(-multipliers.T)
    chosen = chosen.astype(jnp.bfloat16)
    weights = jnp.concatenate(
        [
            jnp.concatenate([chosen, chosen, high, high], 1),
            jnp.concatenate(
                [jnp.zeros((count, 2 * total_slots), jnp.bfloat16), low, jnp.zeros_like(low)], 1
            ),
        ],
        0,
    )

    def body(layer, place, out_ref):
        rows = split(a_ref[:, layer].reshape(total_slots, sh.width))
        data = jnp.concatenate([rows[0], rows[1], c_ref[layer]], 0)
        both = jnp.dot(weights, data, preferred_element_type=jnp.float32)
        result = both[:count] + both[count:]
        for owner in range(sh.owners):
            out_ref[owner, place * own : (place + 1) * own] = result[
                owner * own : (owner + 1) * own
            ]

    for part, out_ref in zip(parts, out_refs):
        for place, layer in enumerate(part):
            body(layer, place, out_ref)


def correct(sh, c, a, slot, part, fold, parts):
    count = slot.shape[0]
    own = count // sh.owners
    return pl.pallas_call(
        functools.partial(correct_kernel, sh, fold, own, parts),
        out_shape=tuple(
            jax.ShapeDtypeStruct((sh.owners, len(layers) * own, sh.width), jnp.float32)
            for layers in parts
        )
        + (
            jax.ShapeDtypeStruct((count, count), jnp.float32),
            jax.ShapeDtypeStruct((count, LANES), jnp.float32),
        ),
        compiler_params=params(16),
        cost_estimate=cost(10**9, 10**7),
        name="correct",
    )(c, a, slot, part)


def relax_kernel(sh, own, parts, boxes, *refs):
    r_refs = refs[: len(parts)]
    lo_ref, hi_ref, inv_ref, res_hbm, dir_hbm, *refs = refs[len(parts) :]
    res_ref, one_ref, two_ref, res_out, dir_out, sems = refs
    places = {layer: (ref, i) for part, ref in zip(parts, r_refs) for i, layer in enumerate(part)}
    rows = sh.depth * own
    edge = SWEEPS * own
    first = pl.multiple_of(lax.axis_index("orb") * own, own)
    inverse = inv_ref[pl.ds(first, own), :]
    inverse = jnp.concatenate([inverse] * (8 // own), 0)
    keep_lo = inverse * (lax.axis_index("box") > 0).astype(jnp.float32)
    keep_hi = inverse * (lax.axis_index("box") < boxes - 1).astype(jnp.float32)
    tiles = (rows + 2 * edge) // 8
    edge_tiles = edge // 8

    def scale(tile):
        if tile < edge_tiles:
            return keep_lo
        return keep_hi if tile >= tiles - edge_tiles else inverse

    group = min(32, sh.chunks)

    def leave(source, target, kind, step, width):
        lanes = pl.ds(pl.multiple_of(step * width, LANES), width)
        return pltpu.make_async_copy(
            source.at[:, :, lanes], target.at[:, :, lanes], sems.at[kind, step]
        )

    half = sh.chunks // 2
    left = lax.broadcasted_iota(jnp.int32, (8, LANES), 1) < LANES // 2
    assert sh.across % 2 == 0

    def turned(value):
        return pltpu.roll(value, LANES // 2, 1)

    def column_of(block, inner):
        lanes = slice(inner * LANES, (inner + 1) * LANES)
        pieces = [lo_ref[block, :, lanes]]
        for g in range(sh.layered):
            for layer in range(sh.layers):
                ref, i = places[layer]
                pieces.append(ref[g * sh.across + block, i * own : (i + 1) * own, lanes])
        pieces += [hi_ref[block, :, lanes]]
        return jnp.concatenate(pieces, 0)

    def gather(block, carry):
        other = block + sh.across // 2
        for inner in range(sh.inner):
            chunk = block * sh.inner + inner
            columns = (column_of(block, inner), column_of(other, inner))
            for tile in range(tiles):
                here = slice(tile * 8, (tile + 1) * 8)
                low, high = columns[0][here], columns[1][here]
                mixed = (jnp.where(left, low, turned(high)), jnp.where(left, turned(low), high))
                for k in range(2):
                    res_ref[2 * chunk + k, here] = mixed[k]
                    one_ref[2 * chunk + k + 1, here] = mixed[k] * scale(tile)
            for column, place in zip(columns, (chunk, chunk + half)):
                two_ref[place + 1] = column
                out_lanes = pl.ds(pl.multiple_of(place * LANES, LANES), LANES)
                for orbital in range(own):
                    rows_of = pl.ds(edge + orbital, sh.depth, stride=own)
                    res_out[orbital, :, out_lanes] = two_ref[place + 1, rows_of, :]
        leave(res_out, res_hbm, 0, block, sh.width).start()
        leave(res_out, res_hbm, 0, other, sh.width).start()
        return carry

    lax.fori_loop(0, sh.across // 2, gather, 0)

    def seal(ref):
        for tile in range(tiles):
            here = slice(tile * 8, (tile + 1) * 8)
            ref[0, here] = jnp.where(left, 0.0, turned(ref[sh.chunks, here]))
            ref[sh.chunks + 1, here] = jnp.where(left, turned(ref[1, here]), 0.0)

    seal(one_ref)
    sub = lax.broadcasted_iota(jnp.int32, (8, LANES), 0)
    lane = lax.broadcasted_iota(jnp.int32, (8, LANES), 1)
    upper = sub >= own
    not_last = (lane % sh.box) != sh.box - 1
    not_first = (lane % sh.box) != 0
    assert 8 // own == 2

    def sweep(source, target, tile_list):
        def body(step, carry):
            seen = {}

            def value_at(column, tile):
                if not 0 <= tile < tiles:
                    return jnp.zeros((8, LANES), jnp.float32)
                if (column, tile) not in seen:
                    seen[column, tile] = source[step * group + column + 1, pl.ds(tile * 8, 8)]
                return seen[column, tile]

            for column in range(group):
                for tile in tile_list:
                    here = pl.ds(tile * 8, 8)
                    value = value_at(column, tile)
                    beside = jnp.where(
                        upper, value_at(column, tile - 1), value_at(column, tile + 1)
                    )
                    along_z = pltpu.roll(value + beside, own, 0)
                    along_y = value_at(column - 1, tile) + value_at(column + 1, tile)
                    along_x = pltpu.roll(jnp.where(not_last, value, 0.0), 1, 1) + pltpu.roll(
                        jnp.where(not_first, value, 0.0), LANES - 1, 1
                    )
                    total = (
                        res_ref[step * group + column, here]
                        + coupling_xy * (along_y + along_x)
                        + coupling_z * along_z
                    )
                    target[step * group + column + 1, here] = total * scale(tile)
            return carry

        lax.fori_loop(0, sh.chunks // group, body, 0)

    source, target = one_ref, two_ref
    for done in range(1, SWEEPS + 1):
        first_tile = done * own // 8
        sweep(source, target, range(first_tile, tiles - first_tile))
        if done < SWEEPS:
            seal(target)
        source, target = target, source

    few = min(8, half)

    def spread(step, carry):
        for column in range(few):
            chunk = step * few + column
            for tile in range(edge_tiles, tiles - edge_tiles):
                here = slice(tile * 8, (tile + 1) * 8)
                even, odd = source[2 * chunk + 1, here], source[2 * chunk + 2, here]
                target[chunk + 1, here] = jnp.where(left, even, turned(odd))
                target[chunk + half + 1, here] = jnp.where(left, turned(even), odd)
            for place in (chunk, chunk + half):
                out_lanes = pl.ds(pl.multiple_of(place * LANES, LANES), LANES)
                for orbital in range(own):
                    rows_of = pl.ds(edge + orbital, sh.depth, stride=own)
                    dir_out[orbital, :, out_lanes] = target[place + 1, rows_of, :]
        leave(dir_out, dir_hbm, 1, step, few * LANES).start()
        leave(dir_out, dir_hbm, 1, step + half // few, few * LANES).start()
        return carry

    lax.fori_loop(0, half // few, spread, 0)
    for block in range(sh.across):
        leave(res_out, res_hbm, 0, block, sh.width).wait()
    for step in range(sh.chunks // few):
        leave(dir_out, dir_hbm, 1, step, few * LANES).wait()


def relax(sh, own, parts, boxes, pieces, lo, hi, inverse):
    rows = (sh.depth + 2 * SWEEPS) * own
    scratch = pltpu.VMEM((sh.chunks, rows, LANES), jnp.float32)
    padded = pltpu.VMEM((sh.chunks + 2, rows, LANES), jnp.float32)
    out = (own, sh.depth, sh.plane)
    hbm = pl.BlockSpec(memory_space=pltpu.HBM)
    vmem = pl.BlockSpec(memory_space=pltpu.VMEM)
    return pl.pallas_call(
        functools.partial(relax_kernel, sh, own, parts, boxes),
        out_shape=(pltpu.HBM(out, jnp.float32),) * 2,
        out_specs=(hbm, hbm),
        in_specs=[vmem] * (3 + len(parts)),
        scratch_shapes=[scratch, padded, padded]
        + [pltpu.VMEM(out, jnp.float32)] * 2
        + [pltpu.SemaphoreType.DMA((2, max(sh.across, sh.chunks)))],
        compiler_params=params(14),
        cost_estimate=cost(10**9, 10**7),
        name="relax",
    )(*pieces, lo, hi, inverse)


def pairs(first, count):
    lower = range(first, count - 1, 2)
    return [(i, i + 1) for i in lower] + [(i + 1, i) for i in lower]


def to_all(value, axes):
    return lax.all_to_all(value, axes, split_axis=0, concat_axis=0, tiled=True)


def step(psi, potential, orbital_slot):
    slots, depth, plane = psi.shape
    owners = lax.axis_size("orb")
    boxes = lax.axis_size("box")
    sh = Shape(slots, depth, plane, owners)
    count = orbital_slot.shape[0]
    own = count // owners
    magic = banded(sh.box, sh.box, 0, 0, magic_weights(MTAPS), 1 - MTAPS // 2)
    kinetic = banded(sh.box, sh.box, 0, 0, second_weights(KREACH), -KREACH)
    fwd, bwd, kin = (jnp.asarray(two_part(m)) for m in (magic, magic.T, kinetic))

    swap_far = pairs(1, boxes)
    swap_near = pairs(0, boxes)
    slot = orbital_slot.reshape(count, 1)
    far = lax.ppermute(psi, "box", swap_far)
    packed = pack(sh, psi)
    received = to_all(packed, "orb")
    near = lax.ppermute(psi, "box", swap_near)
    own_grid, own_kin = own_part(sh, psi, fwd, kin)[1:]
    pieces = choose(sh, slot, received)
    v_far = lax.ppermute(potential, "box", swap_far)
    v_near = lax.ppermute(potential, "box", swap_near)
    near_side = side_part(sh, near, fwd)
    far_side = side_part(sh, far, fwd)
    sides = tuple(far_side) + tuple(near_side)
    applied = halo_part(sh, (own_grid, own_kin), sides, v_far, potential, v_near, bwd)
    applied_pieces = to_all(applied, "orb")

    fold = max(1, LANES // count)
    devices = owners * boxes
    copies = devices if devices * count * count <= 1 << 20 else 0
    part, pieces = gram(sh, pieces, applied_pieces, slot, fold, copies)
    part = to_all(part, ("orb", "box")) if copies else lax.psum(part, ("orb", "box"))
    if sh.layered == 1 and depth > 2 * SWEEPS:
        parts = (
            tuple(range(SWEEPS)) + tuple(range(depth - SWEEPS, depth)),
            tuple(range(SWEEPS, depth - SWEEPS)),
        )
    else:
        parts = (tuple(range(sh.layers)),)
    *corrected, multipliers, inverse = correct(
        sh, pieces, applied_pieces, slot, part, fold, parts
    )
    returned = [to_all(value, "orb") for value in corrected]
    edge = SWEEPS * own
    from_low = lax.ppermute(
        returned[0][-sh.across :, -edge:], "box", [(i, i + 1) for i in range(boxes - 1)]
    )
    from_high = lax.ppermute(
        returned[0][: sh.across, :edge], "box", [(i + 1, i) for i in range(boxes - 1)]
    )
    residual, direction = relax(
        sh, own, parts, boxes, returned, from_low, from_high, inverse
    )
    return (residual, direction, multipliers)


def solution(mesh):
    in_specs = (P("orb", "box", None), P("box", None), P())
    out_specs = (P("orb", "box", None), P("orb", "box", None), P())
    return jax.shard_map(step, mesh=mesh, in_specs=in_specs, out_specs=out_specs, check_vma=False)
```

```python
import functools
import math

import jax
import jax.numpy as jnp
import numpy as np
from jax import lax
from jax.experimental import pallas as pl
from jax.experimental.pallas import tpu as pltpu
from jax.sharding import PartitionSpec as P


MTAPS = 16
KREACH = 14
SWEEPS = 4
LANES = 128

highest = lax.Precision.HIGHEST
coupling_z = 4.0
coupling_xy = 1.0


def magic_weights(tap_count):
    half_len = tap_count // 2
    offsets = np.arange(1 - half_len, half_len + 1) * 1.0
    weights = np.ones(tap_count)
    for index_a in range(tap_count):
        for index_b in range(tap_count):
            if index_b != index_a:
                weights[index_a] *= (0.25 - offsets[index_b]) / (
                    offsets[index_a] - offsets[index_b]
                )
    return weights


def second_weights(reach_cells):
    factor = math.factorial(reach_cells) ** 2
    weights = np.zeros(2 * reach_cells + 1)
    for distance in range(1, reach_cells + 1):
        entry_value = (
            2.0
            * (-1) ** (distance + 1)
            * factor
            / (
                distance
                * distance
                * math.factorial(reach_cells - distance)
                * math.factorial(reach_cells + distance)
            )
        )
        weights[reach_cells + distance] = entry_value
        weights[reach_cells - distance] = entry_value
    weights[reach_cells] = -weights.sum()
    return -0.5 * weights


def banded(row_count, col_count, row_start, col_start, weights, offset_low):
    row_index = np.arange(row_count)[:, None] + row_start
    col_index = np.arange(col_count)[None, :] + col_start
    position = row_index - col_index - offset_low
    inside = (position >= 0) & (position < len(weights))
    return np.where(inside, weights[np.clip(position, 0, len(weights) - 1)], 0.0)


def f32(value):
    return float(np.float32(value))


MAGIC = {k: f32(w) for k, w in zip(range(1 - MTAPS // 2, MTAPS // 2 + 1), magic_weights(MTAPS))}
MAGIC_T = {-k: w for k, w in MAGIC.items()}
KINETIC = {
    d: f32(w) for d, w in zip(range(-KREACH, KREACH + 1), second_weights(KREACH))
}
LOW = MTAPS // 2
HIGH = MTAPS // 2 - 1


def two_part(matrix):
    width = matrix.shape[0]
    block = np.kron(np.eye(LANES // width), matrix).astype(np.float32)
    high = block.astype(jnp.bfloat16)
    low = (block - high.astype(np.float32)).astype(jnp.bfloat16)
    return np.block([[high, low], [high, np.zeros_like(low)]])


def split(value):
    high = value.astype(jnp.bfloat16)
    low = (value - high.astype(jnp.float32)).astype(jnp.bfloat16)
    return high, low


def lane_product(parts, matrix):
    both = jnp.dot(parts, matrix, preferred_element_type=jnp.float32)
    return both[:, :LANES] + both[:, LANES:]


def params(mib):
    return pltpu.CompilerParams(vmem_limit_bytes=mib << 20)


def cost(flops, bytes_accessed):
    return pl.CostEstimate(flops=flops, bytes_accessed=bytes_accessed, transcendentals=0)


class Shape:
    def __init__(self, slots, depth, plane, owners):
        self.slots, self.depth, self.plane, self.owners = slots, depth, plane, owners
        self.box = math.isqrt(plane)
        self.chunks = plane // LANES
        self.across = min(owners, self.chunks)
        self.layered = owners // self.across
        self.layers = depth // self.layered
        self.width = plane // self.across
        self.inner = self.width // LANES

    def at(self, layer, block, inner):
        piece = (layer // self.layers) * self.across + block
        lanes = slice(inner * LANES, (inner + 1) * LANES)
        return piece, layer % self.layers, slice(None), lanes


def pack_kernel(sh, psi_hbm, out_hbm, buffer, sems_in, sems_out):
    def pair(index):
        first = (index // sh.across) * sh.layers
        lane = (index % sh.across) * sh.width
        source = psi_hbm.at[:, pl.ds(first, sh.layers), pl.ds(lane, sh.width)]
        return (
            pltpu.make_async_copy(source, buffer.at[index], sems_in.at[index]),
            pltpu.make_async_copy(buffer.at[index], out_hbm.at[index], sems_out.at[index]),
        )

    copies = [pair(index) for index in range(sh.owners)]
    for arrive, leave in copies:
        arrive.start()
    for arrive, leave in copies:
        arrive.wait()
        leave.start()
    for arrive, leave in copies:
        leave.wait()


def pack(sh, psi):
    shape = (sh.owners, sh.slots, sh.layers, sh.width)
    return pl.pallas_call(
        functools.partial(pack_kernel, sh),
        out_shape=pltpu.HBM(shape, jnp.float32),
        in_specs=[pl.BlockSpec(memory_space=pltpu.HBM)],
        out_specs=pl.BlockSpec(memory_space=pltpu.HBM),
        scratch_shapes=[
            pltpu.VMEM(shape, jnp.float32),
            pltpu.SemaphoreType.DMA((sh.owners,)),
            pltpu.SemaphoreType.DMA((sh.owners,)),
        ],
        compiler_params=params(8),
        cost_estimate=cost(0, 2 * psi.size * 4),
        name="pack",
    )(pltpu.with_memory_space_constraint(psi, pltpu.HBM))


def choose_kernel(sh, slot_ref, in_ref, out_ref):
    count = slot_ref.shape[0]
    total_slots = sh.owners * sh.slots
    chosen = selection(slot_ref, count, total_slots).astype(jnp.bfloat16)
    turned = [
        jnp.transpose(in_ref[index], (1, 0, 2)) for index in range(sh.owners)
    ]
    for layer in range(sh.layers):
        high, low = split(jnp.concatenate([rows[layer] for rows in turned], 0))
        high = jnp.dot(chosen, high, preferred_element_type=jnp.float32)
        low = jnp.dot(chosen, low, preferred_element_type=jnp.float32)
        out_ref[layer, :count] = high.astype(jnp.bfloat16)
        out_ref[layer, count:] = low.astype(jnp.bfloat16)


def choose(sh, slot, pieces):
    count = slot.shape[0]
    return pl.pallas_call(
        functools.partial(choose_kernel, sh),
        out_shape=pltpu.HBM((sh.layers, 2 * count, sh.width), jnp.bfloat16),
        compiler_params=params(12),
        cost_estimate=cost(10**8, 2 * pieces.size * 4),
        name="choose",
    )(slot, pltpu.with_memory_space_constraint(pieces, pltpu.HBM))


def odd_pairs(even, lane):
    turned = [pltpu.roll(v, LANES // 2, 1) for v in even]
    zero = jnp.zeros_like(even[0])
    low = [zero] + turned
    high = turned + [zero]
    return [jnp.where(lane, a, b) for a, b in zip(low, high)]


def row_filter(even, odd, weights):
    count = len(even)
    out = []
    for b in range(count):
        total = None
        for d, w in weights.items():
            e = b + d // 2
            if d % 2 == 0:
                if not 0 <= e < count:
                    continue
                term = even[e]
            else:
                if not 0 <= e + 1 <= count:
                    continue
                term = odd[e + 1]
            total = term * w if total is None else total + term * w
        out.append(total)
    return out


def row_filter_even(even, odd, weights, reach):
    count = len(even)
    out = []
    for b in range(count):
        total = even[b] * weights[0]
        for d in range(1, reach + 1):
            if d % 2 == 0:
                places = [e for e in (b + d // 2, b - d // 2) if 0 <= e < count]
                terms = [even[e] for e in places]
            else:
                places = [e for e in (b + d // 2 + 1, b - d // 2) if 0 <= e <= count]
                terms = [odd[e] for e in places]
            if not terms:
                continue
            term = terms[0] if len(terms) == 1 else terms[0] + terms[1]
            total = total + term * weights[d]
        out.append(total)
    return out


def layer_sum(p, weights, layer, total=None):
    for k, w in weights.items():
        value = layer(p + k)
        if value is not None:
            total = value * w if total is None else total + value * w
    return total


def layer_sum_even(q, total, layer):
    for d in range(1, KREACH + 1):
        terms = [t for t in (layer(q - d), layer(q + d)) if t is not None]
        if terms:
            term = terms[0] if len(terms) == 1 else terms[0] + terms[1]
            total = total + term * KINETIC[d]
    return total


def half_mask(slots):
    return lax.broadcasted_iota(jnp.int32, (slots, LANES), 1) < LANES // 2


def lane_pass(sh, slab, kept, matrices, targets):
    depth = sh.depth

    def body(block, carry):
        parts = []
        for inner in range(sh.inner):
            chunk = block * sh.inner + inner
            lanes = pl.ds(pl.multiple_of(chunk * LANES, LANES), LANES)
            rows = jnp.transpose(slab[:, :, lanes], (1, 0, 2))
            for layer in range(depth):
                kept[layer, chunk] = rows[layer]
            high, low = split(rows.reshape(depth * sh.slots, LANES))
            parts.append(jnp.concatenate([high, low], 1))
        parts = jnp.concatenate(parts, 0)
        for matrix, target in zip(matrices, targets):
            result = lane_product(parts, matrix[...])
            result = result.reshape(sh.inner, depth, sh.slots, LANES)
            for inner in range(sh.inner):
                for layer in range(depth):
                    target[layer, block * sh.inner + inner] = result[inner, layer]
        return carry

    lax.fori_loop(0, sh.across, body, 0)


def own_kernel(sh, psi_ref, fwd_ref, kin_ref, c_out, grid_out, kin_out, x_ref, w_ref):
    lane_pass(sh, psi_ref, c_out, [fwd_ref, kin_ref], [x_ref, kin_out])
    lane = half_mask(sh.slots)

    def body(layer, carry):
        even = [x_ref[layer, b] for b in range(sh.chunks)]
        for b, v in enumerate(row_filter(even, odd_pairs(even, lane), MAGIC)):
            w_ref[layer, b] = v
        even = [c_out[layer, b] for b in range(sh.chunks)]
        sums = row_filter_even(even, odd_pairs(even, lane), KINETIC, KREACH)
        for b, v in enumerate(sums):
            kin_out[layer, b] += v
        return carry

    lax.fori_loop(0, sh.depth, body, 0)
    depth = sh.depth

    def along_z(chunk, carry):
        values = [w_ref[z, chunk] for z in range(depth)]
        for p in range(-LOW, depth + HIGH):
            grid_out[p + LOW, chunk] = layer_sum(
                p, MAGIC, lambda z: values[z] if 0 <= z < depth else None
            )
        cs = [c_out[z, chunk] for z in range(depth)]
        for q in range(depth):
            total = kin_out[q, chunk] + cs[q] * KINETIC[0]
            kin_out[q, chunk] = layer_sum_even(
                q, total, lambda z: cs[z] if 0 <= z < depth else None
            )
        return carry

    lax.fori_loop(0, sh.chunks, along_z, 0)


def own_part(sh, psi, fwd, kin):
    full = jax.ShapeDtypeStruct((sh.depth, sh.chunks, sh.slots, LANES), jnp.float32)
    grid = jax.ShapeDtypeStruct((sh.depth + LOW + HIGH,) + full.shape[1:], jnp.float32)
    return pl.pallas_call(
        functools.partial(own_kernel, sh),
        out_shape=(full, grid, full),
        scratch_shapes=[pltpu.VMEM(full.shape, jnp.float32)] * 2,
        compiler_params=params(18),
        cost_estimate=cost(10 * 10**9, 10**7),
        name="own_part",
    )(psi, fwd, kin)


def side_kernel(sh, slab_hbm, fwd_ref, c_out, w_out, slab_ref, x_ref, sem):
    copy = pltpu.make_async_copy(slab_hbm, slab_ref, sem)
    copy.start()
    lane = half_mask(sh.slots)
    copy.wait()
    lane_pass(sh, slab_ref, c_out, [fwd_ref], [x_ref])

    def filter_rows(layer, carry):
        even = [x_ref[layer, b] for b in range(sh.chunks)]
        for b, v in enumerate(row_filter(even, odd_pairs(even, lane), MAGIC)):
            w_out[layer, b] = v
        return carry

    lax.fori_loop(0, sh.depth, filter_rows, 0)


def side_part(sh, slab, fwd):
    full = (sh.depth, sh.chunks, sh.slots, LANES)
    return pl.pallas_call(
        functools.partial(side_kernel, sh),
        out_shape=(jax.ShapeDtypeStruct(full, jnp.float32),) * 2,
        in_specs=[pl.BlockSpec(memory_space=pl.ANY), pl.BlockSpec(memory_space=pltpu.VMEM)],
        scratch_shapes=[
            pltpu.VMEM(slab.shape, jnp.float32),
            pltpu.VMEM(full, jnp.float32),
            pltpu.SemaphoreType.DMA,
        ],
        compiler_params=params(8),
        cost_estimate=cost(5 * 10**9, 10**7),
        name="side_part",
    )(slab, fwd)


def halo_kernel(
    sh, grid_ref, kin_ref, cfar_ref, wfar_ref, cnear_ref, wnear_ref, vfar_ref, v_ref,
    vnear_ref, bwd_ref, out_hbm, x_ref, y_ref, kz_ref, vlo_ref, vhi_ref, out_ref, sems,
):
    lane = half_mask(sh.slots)
    depth = sh.depth
    even = lax.rem(lax.axis_index("box"), 2) == 0
    vlo_ref[...] = jnp.where(even, vfar_ref[...], vnear_ref[...])
    vhi_ref[...] = jnp.where(even, vnear_ref[...], vfar_ref[...])

    def along_z(clo_ref, wlo_ref, chi_ref, whi_ref, chunk, carry):
        lanes = pl.ds(pl.multiple_of(chunk * LANES, LANES), LANES)

        def outside(below, above):
            places = {}

            def layer(z):
                if 0 <= z < depth:
                    return None
                if z not in places:
                    places[z] = (below if z < 0 else above)[z % depth, chunk]
                return places[z]

            return layer

        def level(z):
            ref = vlo_ref if z < 0 else (v_ref if z < depth else vhi_ref)
            return jnp.broadcast_to(ref[z % depth : z % depth + 1, lanes], (sh.slots, LANES))

        mixed = outside(wlo_ref, whi_ref)
        grid = {}
        for p in range(-LOW, depth + HIGH):
            grid[p] = layer_sum(p, MAGIC, mixed, grid_ref[p + LOW, chunk]) * level(p)
        for q in range(depth):
            x_ref[q, chunk] = layer_sum(q, MAGIC_T, grid.get)
        coeffs = outside(clo_ref, chi_ref)
        for q in range(depth):
            kz_ref[q, chunk] = layer_sum_even(q, kin_ref[q, chunk], coeffs)
        return carry

    far_pair, near_pair = (cfar_ref, wfar_ref), (cnear_ref, wnear_ref)

    @pl.when(even)
    def _():
        lax.fori_loop(0, sh.chunks, functools.partial(along_z, *far_pair, *near_pair), 0)

    @pl.when(jnp.logical_not(even))
    def _():
        lax.fori_loop(0, sh.chunks, functools.partial(along_z, *near_pair, *far_pair), 0)

    def filter_back(layer, carry):
        even = [x_ref[layer, b] for b in range(sh.chunks)]
        for b, v in enumerate(row_filter(even, odd_pairs(even, lane), MAGIC_T)):
            y_ref[layer, b] = v
        return carry

    lax.fori_loop(0, depth, filter_back, 0)

    def piece(index):
        return pltpu.make_async_copy(out_ref.at[index], out_hbm.at[index], sems.at[index])

    def finish(block, carry):
        parts = []
        for inner in range(sh.inner):
            chunk = block * sh.inner + inner
            rows = jnp.concatenate([y_ref[layer, chunk] for layer in range(depth)], 0)
            high, low = split(rows)
            parts.append(jnp.concatenate([high, low], 1))
        result = lane_product(jnp.concatenate(parts, 0), bwd_ref[...])
        result = result.reshape(sh.inner, depth, sh.slots, LANES)
        for inner in range(sh.inner):
            chunk = block * sh.inner + inner
            for layer in range(depth):
                out_ref[sh.at(layer, block, inner)] = result[inner, layer] + kz_ref[layer, chunk]
        for group in range(sh.layered):
            piece(group * sh.across + block).start()
        return carry

    lax.fori_loop(0, sh.across, finish, 0)
    for index in range(sh.owners):
        piece(index).wait()


def halo_part(sh, own, sides, v_far, v, v_near, bwd):
    full = pltpu.VMEM((sh.depth, sh.chunks, sh.slots, LANES), jnp.float32)
    out = (sh.owners, sh.layers, sh.slots, sh.width)
    return pl.pallas_call(
        functools.partial(halo_kernel, sh),
        out_shape=pltpu.HBM(out, jnp.float32),
        in_specs=[pl.BlockSpec(memory_space=pltpu.VMEM)] * 10,
        out_specs=pl.BlockSpec(memory_space=pltpu.HBM),
        scratch_shapes=[full] * 3
        + [pltpu.VMEM(v.shape, jnp.float32)] * 2
        + [pltpu.VMEM(out, jnp.float32), pltpu.SemaphoreType.DMA((sh.owners,))],
        compiler_params=params(14),
        cost_estimate=cost(20 * 10**9, 10**7),
        name="halo_part",
    )(*own, *sides, v_far, v, v_near, bwd)


def selection(slot_ref, count, slots_all):
    column = lax.broadcasted_iota(jnp.int32, (count, slots_all), 1)
    return (column == slot_ref[...]).astype(jnp.float32)


def packed_rows(matrix, fold):
    rows = matrix.shape[0] // fold
    return jnp.concatenate([matrix[i * rows : (i + 1) * rows] for i in range(fold)], 1)


def unpacked_rows(matrix, fold):
    cols = matrix.shape[1] // fold
    return jnp.concatenate([matrix[:, i * cols : (i + 1) * cols] for i in range(fold)], 0)


def gram_kernel(sh, fold, c_hbm, a_ref, slot_ref, out_ref, c_ref, sem):
    copy = pltpu.make_async_copy(c_hbm, c_ref, sem)
    copy.start()
    total_slots = sh.owners * sh.slots
    count = slot_ref.shape[0]
    chosen = selection(slot_ref, count, total_slots)
    both = jnp.zeros((2 * count, 2 * total_slots), jnp.float32)
    copy.wait()
    for layer in range(sh.layers):
        rows = a_ref[:, layer].reshape(total_slots, sh.width)
        both = both + lax.dot_general(
            c_ref[layer],
            jnp.concatenate(split(rows), 0),
            (((1,), (1,)), ((), ())),
            preferred_element_type=jnp.float32,
        )
    wide = both[:count] + both[count:]
    rows = wide[:, :total_slots] + wide[:, total_slots:]
    picked = lax.dot_general(
        rows, chosen, (((1,), (1,)), ((), ())), precision=highest,
        preferred_element_type=jnp.float32,
    ) * (1.0 / sh.box**3)
    picked = packed_rows(picked, fold)
    if len(out_ref.shape) == 2:
        out_ref[...] = picked
    else:
        out_ref[...] = jnp.broadcast_to(picked[None], out_ref.shape)


def gram(sh, c, a, slot, fold, copies):
    count = slot.shape[0]
    shape = (count // fold, count * fold)
    if copies:
        shape = (copies,) + shape
    return pl.pallas_call(
        functools.partial(gram_kernel, sh, fold),
        out_shape=(jax.ShapeDtypeStruct(shape, jnp.float32), pltpu.VMEM(c.shape, c.dtype)),
        in_specs=[pl.BlockSpec(memory_space=pltpu.HBM)]
        + [pl.BlockSpec(memory_space=pltpu.VMEM)] * 2,
        scratch_shapes=[pltpu.SemaphoreType.DMA],
        compiler_params=params(16),
        cost_estimate=cost(10**9, 10**7),
        name="gram",
    )(pltpu.with_memory_space_constraint(c, pltpu.HBM), a, slot)


def correct_kernel(sh, fold, own, parts, c_ref, a_ref, slot_ref, part_ref, *outs):
    *out_refs, mult_ref, inv_ref = outs
    total_slots = sh.owners * sh.slots
    count = slot_ref.shape[0]
    packed = part_ref[...]
    if packed.ndim == 3:
        packed = packed.sum(0)
    multipliers = unpacked_rows(packed, fold)
    mult_ref[...] = multipliers
    row = lax.broadcasted_iota(jnp.int32, (count, count), 0)
    col = lax.broadcasted_iota(jnp.int32, (count, count), 1)
    diagonal = jnp.sum(jnp.where(row == col, multipliers, 0.0), axis=1, keepdims=True)
    denominator = 2.0 * coupling_z + 4.0 * coupling_xy + 1.0 + jnp.abs(diagonal)
    inv_ref[...] = jnp.broadcast_to(1.0 / denominator, (count, LANES))
    chosen = selection(slot_ref, count, total_slots)
    high, low = split(-multipliers.T)
    chosen = chosen.astype(jnp.bfloat16)
    weights = jnp.concatenate(
        [
            jnp.concatenate([chosen, chosen, high, high], 1),
            jnp.concatenate(
                [jnp.zeros((count, 2 * total_slots), jnp.bfloat16), low, jnp.zeros_like(low)], 1
            ),
        ],
        0,
    )

    def body(layer, place, out_ref):
        rows = split(a_ref[:, layer].reshape(total_slots, sh.width))
        data = jnp.concatenate([rows[0], rows[1], c_ref[layer]], 0)
        both = jnp.dot(weights, data, preferred_element_type=jnp.float32)
        result = both[:count] + both[count:]
        for owner in range(sh.owners):
            out_ref[owner, place * own : (place + 1) * own] = result[
                owner * own : (owner + 1) * own
            ]

    for part, out_ref in zip(parts, out_refs):
        for place, layer in enumerate(part):
            body(layer, place, out_ref)


def correct(sh, c, a, slot, part, fold, parts):
    count = slot.shape[0]
    own = count // sh.owners
    return pl.pallas_call(
        functools.partial(correct_kernel, sh, fold, own, parts),
        out_shape=tuple(
            jax.ShapeDtypeStruct((sh.owners, len(layers) * own, sh.width), jnp.float32)
            for layers in parts
        )
        + (
            jax.ShapeDtypeStruct((count, count), jnp.float32),
            jax.ShapeDtypeStruct((count, LANES), jnp.float32),
        ),
        compiler_params=params(16),
        cost_estimate=cost(10**9, 10**7),
        name="correct",
    )(c, a, slot, part)


def relax_kernel(sh, own, parts, boxes, *refs):
    r_refs = refs[: len(parts)]
    lo_ref, hi_ref, inv_ref, res_hbm, dir_hbm, *refs = refs[len(parts) :]
    res_ref, one_ref, two_ref, res_out, dir_out, sems = refs
    places = {layer: (ref, i) for part, ref in zip(parts, r_refs) for i, layer in enumerate(part)}
    rows = sh.depth * own
    edge = SWEEPS * own
    first = pl.multiple_of(lax.axis_index("orb") * own, own)
    inverse = inv_ref[pl.ds(first, own), :]
    inverse = jnp.concatenate([inverse] * (8 // own), 0)
    keep_lo = inverse * (lax.axis_index("box") > 0).astype(jnp.float32)
    keep_hi = inverse * (lax.axis_index("box") < boxes - 1).astype(jnp.float32)
    tiles = (rows + 2 * edge) // 8
    edge_tiles = edge // 8

    def scale(tile):
        if tile < edge_tiles:
            return keep_lo
        return keep_hi if tile >= tiles - edge_tiles else inverse

    group = min(32, sh.chunks)

    def leave(source, target, kind, step, width):
        lanes = pl.ds(pl.multiple_of(step * width, LANES), width)
        return pltpu.make_async_copy(
            source.at[:, :, lanes], target.at[:, :, lanes], sems.at[kind, step]
        )

    half = sh.chunks // 2
    left = lax.broadcasted_iota(jnp.int32, (8, LANES), 1) < LANES // 2
    assert sh.across % 2 == 0

    def turned(value):
        return pltpu.roll(value, LANES // 2, 1)

    def column_of(block, inner):
        lanes = slice(inner * LANES, (inner + 1) * LANES)
        pieces = [lo_ref[block, :, lanes]]
        for g in range(sh.layered):
            for layer in range(sh.layers):
                ref, i = places[layer]
                pieces.append(ref[g * sh.across + block, i * own : (i + 1) * own, lanes])
        pieces += [hi_ref[block, :, lanes]]
        return jnp.concatenate(pieces, 0)

    def gather(block, carry):
        other = block + sh.across // 2
        for inner in range(sh.inner):
            chunk = block * sh.inner + inner
            columns = (column_of(block, inner), column_of(other, inner))
            for tile in range(tiles):
                here = slice(tile * 8, (tile + 1) * 8)
                low, high = columns[0][here], columns[1][here]
                mixed = (jnp.where(left, low, turned(high)), jnp.where(left, turned(low), high))
                for k in range(2):
                    res_ref[2 * chunk + k, here] = mixed[k]
                    one_ref[2 * chunk + k + 1, here] = mixed[k] * scale(tile)
            for column, place in zip(columns, (chunk, chunk + half)):
                two_ref[place + 1] = column
                out_lanes = pl.ds(pl.multiple_of(place * LANES, LANES), LANES)
                for orbital in range(own):
                    rows_of = pl.ds(edge + orbital, sh.depth, stride=own)
                    res_out[orbital, :, out_lanes] = two_ref[place + 1, rows_of, :]
        leave(res_out, res_hbm, 0, block, sh.width).start()
        leave(res_out, res_hbm, 0, other, sh.width).start()
        return carry

    lax.fori_loop(0, sh.across // 2, gather, 0)

    def seal(ref):
        for tile in range(tiles):
            here = slice(tile * 8, (tile + 1) * 8)
            ref[0, here] = jnp.where(left, 0.0, turned(ref[sh.chunks, here]))
            ref[sh.chunks + 1, here] = jnp.where(left, turned(ref[1, here]), 0.0)

    seal(one_ref)
    sub = lax.broadcasted_iota(jnp.int32, (8, LANES), 0)
    lane = lax.broadcasted_iota(jnp.int32, (8, LANES), 1)
    upper = sub >= own
    not_last = (lane % sh.box) != sh.box - 1
    not_first = (lane % sh.box) != 0
    assert 8 // own == 2

    def sweep(source, target, tile_list):
        def body(step, carry):
            seen = {}

            def value_at(column, tile):
                if not 0 <= tile < tiles:
                    return jnp.zeros((8, LANES), jnp.float32)
                if (column, tile) not in seen:
                    seen[column, tile] = source[step * group + column + 1, pl.ds(tile * 8, 8)]
                return seen[column, tile]

            for column in range(group):
                for tile in tile_list:
                    here = pl.ds(tile * 8, 8)
                    value = value_at(column, tile)
                    beside = jnp.where(
                        upper, value_at(column, tile - 1), value_at(column, tile + 1)
                    )
                    along_z = pltpu.roll(value + beside, own, 0)
                    along_y = value_at(column - 1, tile) + value_at(column + 1, tile)
                    along_x = pltpu.roll(jnp.where(not_last, value, 0.0), 1, 1) + pltpu.roll(
                        jnp.where(not_first, value, 0.0), LANES - 1, 1
                    )
                    total = (
                        res_ref[step * group + column, here]
                        + coupling_xy * (along_y + along_x)
                        + coupling_z * along_z
                    )
                    target[step * group + column + 1, here] = total * scale(tile)
            return carry

        lax.fori_loop(0, sh.chunks // group, body, 0)

    source, target = one_ref, two_ref
    for done in range(1, SWEEPS + 1):
        first_tile = done * own // 8
        sweep(source, target, range(first_tile, tiles - first_tile))
        if done < SWEEPS:
            seal(target)
        source, target = target, source

    few = min(4, half)

    def spread(step, carry):
        for column in range(few):
            chunk = step * few + column
            for tile in range(edge_tiles, tiles - edge_tiles):
                here = slice(tile * 8, (tile + 1) * 8)
                even, odd = source[2 * chunk + 1, here], source[2 * chunk + 2, here]
                target[chunk + 1, here] = jnp.where(left, even, turned(odd))
                target[chunk + half + 1, here] = jnp.where(left, turned(even), odd)
            for place in (chunk, chunk + half):
                out_lanes = pl.ds(pl.multiple_of(place * LANES, LANES), LANES)
                for orbital in range(own):
                    rows_of = pl.ds(edge + orbital, sh.depth, stride=own)
                    dir_out[orbital, :, out_lanes] = target[place + 1, rows_of, :]
        leave(dir_out, dir_hbm, 1, step, few * LANES).start()
        leave(dir_out, dir_hbm, 1, step + half // few, few * LANES).start()
        return carry

    lax.fori_loop(0, half // few, spread, 0)
    for block in range(sh.across):
        leave(res_out, res_hbm, 0, block, sh.width).wait()
    for step in range(sh.chunks // few):
        leave(dir_out, dir_hbm, 1, step, few * LANES).wait()


def relax(sh, own, parts, boxes, pieces, lo, hi, inverse):
    rows = (sh.depth + 2 * SWEEPS) * own
    scratch = pltpu.VMEM((sh.chunks, rows, LANES), jnp.float32)
    padded = pltpu.VMEM((sh.chunks + 2, rows, LANES), jnp.float32)
    out = (own, sh.depth, sh.plane)
    hbm = pl.BlockSpec(memory_space=pltpu.HBM)
    vmem = pl.BlockSpec(memory_space=pltpu.VMEM)
    return pl.pallas_call(
        functools.partial(relax_kernel, sh, own, parts, boxes),
        out_shape=(pltpu.HBM(out, jnp.float32),) * 2,
        out_specs=(hbm, hbm),
        in_specs=[vmem] * (3 + len(parts)),
        scratch_shapes=[scratch, padded, padded]
        + [pltpu.VMEM(out, jnp.float32)] * 2
        + [pltpu.SemaphoreType.DMA((2, max(sh.across, sh.chunks)))],
        compiler_params=params(14),
        cost_estimate=cost(10**9, 10**7),
        name="relax",
    )(*pieces, lo, hi, inverse)


def pairs(first, count):
    lower = range(first, count - 1, 2)
    return [(i, i + 1) for i in lower] + [(i + 1, i) for i in lower]


def to_all(value, axes):
    return lax.all_to_all(value, axes, split_axis=0, concat_axis=0, tiled=True)


def step(psi, potential, orbital_slot):
    slots, depth, plane = psi.shape
    owners = lax.axis_size("orb")
    boxes = lax.axis_size("box")
    sh = Shape(slots, depth, plane, owners)
    count = orbital_slot.shape[0]
    own = count // owners
    magic = banded(sh.box, sh.box, 0, 0, magic_weights(MTAPS), 1 - MTAPS // 2)
    kinetic = banded(sh.box, sh.box, 0, 0, second_weights(KREACH), -KREACH)
    fwd, bwd, kin = (jnp.asarray(two_part(m)) for m in (magic, magic.T, kinetic))

    swap_far = pairs(1, boxes)
    swap_near = pairs(0, boxes)
    slot = orbital_slot.reshape(count, 1)
    far = lax.ppermute(psi, "box", swap_far)
    packed = pack(sh, psi)
    received = to_all(packed, "orb")
    near = lax.ppermute(psi, "box", swap_near)
    own_grid, own_kin = own_part(sh, psi, fwd, kin)[1:]
    pieces = choose(sh, slot, received)
    v_far = lax.ppermute(potential, "box", swap_far)
    v_near = lax.ppermute(potential, "box", swap_near)
    near_side = side_part(sh, near, fwd)
    far_side = side_part(sh, far, fwd)
    sides = tuple(far_side) + tuple(near_side)
    applied = halo_part(sh, (own_grid, own_kin), sides, v_far, potential, v_near, bwd)
    applied_pieces = to_all(applied, "orb")

    fold = max(1, LANES // count)
    devices = owners * boxes
    copies = devices if devices * count * count <= 1 << 20 else 0
    part, pieces = gram(sh, pieces, applied_pieces, slot, fold, copies)
    part = to_all(part, ("orb", "box")) if copies else lax.psum(part, ("orb", "box"))
    if sh.layered == 1 and depth > 2 * SWEEPS:
        parts = (
            tuple(range(SWEEPS)) + tuple(range(depth - SWEEPS, depth)),
            tuple(range(SWEEPS, depth - SWEEPS)),
        )
    else:
        parts = (tuple(range(sh.layers)),)
    *corrected, multipliers, inverse = correct(
        sh, pieces, applied_pieces, slot, part, fold, parts
    )
    returned = [to_all(value, "orb") for value in corrected]
    edge = SWEEPS * own
    from_low = lax.ppermute(
        returned[0][-sh.across :, -edge:], "box", [(i, i + 1) for i in range(boxes - 1)]
    )
    from_high = lax.ppermute(
        returned[0][: sh.across, :edge], "box", [(i + 1, i) for i in range(boxes - 1)]
    )
    residual, direction = relax(
        sh, own, parts, boxes, returned, from_low, from_high, inverse
    )
    return (residual, direction, multipliers)


def solution(mesh):
    in_specs = (P("orb", "box", None), P("box", None), P())
    out_specs = (P("orb", "box", None), P("orb", "box", None), P())
    return jax.shard_map(step, mesh=mesh, in_specs=in_specs, out_specs=out_specs, check_vma=False)
```
